128 devices in a mesh: row: 8 (over x_lo, y), col: 16 (over x_hi, z, core).
Axes of the slice: x: 4 (x_hi: 2, x_lo: 2; x = x_hi * 2 + x_lo), y: 4, z: 4, core: 2. Of those that a mesh axis runs over, the one named last changes fastest.
Arguments:
- vectors: float32 [65536, 2048], P('row', 'col'), may hold values from -6 to 6
- panel_one: float32 [65536, 256], P('row', 'col'), may hold values from -100 to 100
- panel_two: float32 [65536, 256], P('row', 'col'), may hold values from -100 to 100
Outputs:
- rotated: float32 [65536, 2048], P('row', 'col')
The draws below stay inside these ranges and needn't reach their ends.
All inputs are finite; a program needn't handle non-finite values.
Results may differ from the reference program's by a relative error of at most 0.000092.
Values sent between devices are 32-bit elements; how exact they have to be, the bound alone decides.
No kernel may reach another device: no remote copies, remote signals or barrier semaphores. Data moves between devices by JAX's collectives and lax.ppermute only.
A program may use at most 192 MiB of HBM per device.

```python
import math
import jax
import jax.numpy as jnp
from jax import lax

EIGS = 2048
PANEL = 256
ROWS = 65536


def reflector_draw(key, salt):
    key = jax.random.fold_in(key, salt)
    key_entries, key_jitter, key_column, key_mixing = jax.random.split(key, 4)
    positions = jnp.arange(ROWS).astype(jnp.float32)
    rising = jnp.sqrt(1.0 + 2.0 * positions / max(ROWS - 1, 1))
    jitter = jnp.exp(jax.random.uniform(key_jitter, (ROWS, 1), jnp.float32, math.log(0.5), math.log(2.0)))
    entries = jnp.clip(jax.random.normal(key_entries, (ROWS, PANEL), jnp.float32), -6.0, 6.0)
    lower_index = jnp.arange(PANEL)[:, None]
    upper_index = jnp.arange(PANEL)[None, :]
    distance = jnp.maximum(upper_index - lower_index, 0).astype(jnp.float32)
    factor = jax.random.uniform(key_mixing, (PANEL, PANEL), jnp.float32, 0.75, 1.25)
    above = upper_index > lower_index
    mixing = jnp.where(above, jnp.exp(distance * math.log(0.8)) * factor, 0.0) + jnp.eye(PANEL, dtype=jnp.float32)
    mixed = jnp.dot(entries, mixing, precision=lax.Precision.HIGHEST)
    column_scale = jnp.exp(jax.random.uniform(key_column, (1, PANEL), jnp.float32, 0.0, math.log(10.0)))
    return jnp.clip(mixed * rising[:, None] * jitter * column_scale, -100.0, 100.0)


def draw_panel_one(key, part):
    return reflector_draw(key, 101)


def draw_panel_two(key, part):
    return reflector_draw(key, 202)


def shard_levels(key, extent, cuts, smallest, top_value):
    factor_of, own = 1.0, jax.random.fold_in(key, 6)
    for dim, parts in cuts:
        heights = jnp.exp(jax.random.uniform(jax.random.fold_in(own, dim), (parts,), jnp.float32, smallest / len(cuts), top_value / len(cuts)))
        factor_of = factor_of * jnp.repeat(heights, extent[dim] // parts).reshape([-1 if axis == dim else 1 for axis in range(len(extent))])
    return factor_of


def noise(key, extent, width, most, shards=(), kind=jnp.bfloat16):
    array = width * jax.random.normal(key, extent, jnp.float32)
    if shards:
        array = array * shard_levels(key, extent, shards, -0.22, 0.18)
    return jnp.clip(array, -most, most).astype(kind)


def setup_inputs(seed: int = 0) -> dict:
    seeds = jax.random.split(jax.random.key(seed), 4)
    return {
        "vectors": noise(seeds[0], (ROWS, EIGS), 1.0, 6.0, ((0, 8), (1, 16)), jnp.float32),
        "panel_one": draw_panel_one(jax.random.fold_in(seeds[3], 71), 0),
        "panel_two": draw_panel_two(jax.random.fold_in(seeds[3], 71), 0),
    }


def triangle(gramian):
    return jnp.triu(gramian, 1) + jnp.diag(jnp.diagonal(gramian) * 0.5)

def apply_panel(current, mirror):
    gramian = jnp.dot(mirror.T, mirror, precision=lax.Precision.HIGHEST)
    projection = jnp.dot(mirror.T, current, precision=lax.Precision.HIGHEST)
    solved = lax.linalg.triangular_solve(triangle(gramian), projection, left_side=True, lower=False)
    return current - jnp.dot(mirror, solved, precision=lax.Precision.HIGHEST)

def reference(vectors, panel_one, panel_two):
    middle = apply_panel(vectors, panel_two)
    return apply_panel(middle, panel_one)
```

```python
import functools

import jax
import jax.numpy as jnp
from jax import lax
from jax.experimental import pallas as pl
from jax.experimental.pallas import tpu as pltpu
from jax.sharding import PartitionSpec as P

F32 = jnp.float32
BF16 = jnp.bfloat16
HIGHEST = lax.Precision.HIGHEST
PLANES, DEPTH, CORES = 2, 4, 2
CHIPS = PLANES * DEPTH
WIDE = 128
TILE = 512
PIECES = ((0, 0), (0, 1), (1, 1), (0, 2), (0, 3)), ((1, 2), (1, 3), (2, 2), (2, 3), (3, 3))


def split3(value):
    high = value.astype(BF16)
    rest = value - high.astype(F32)
    middle = rest.astype(BF16)
    low = (rest - middle.astype(F32)).astype(BF16)
    return high, middle, low


def nn(left, right):
    return lax.dot_general(left, right, (((1,), (0,)), ((), ())), preferred_element_type=F32)


def nt(left, right):
    return lax.dot_general(left, right, (((1,), (1,)), ((), ())), preferred_element_type=F32)


def full(left, right):
    return lax.dot_general(
        left, right, (((1,), (0,)), ((), ())), precision=HIGHEST, preferred_element_type=F32
    )


def gram_kernel(where_ref, *refs):
    steps = pl.num_programs(0)
    step = pl.program_id(0)
    whole = refs[0:4]
    early = refs[4:8]
    late = refs[8:12]
    own_ref, other_ref, out_ref, high, middle, low, even, skew, proj = refs[12:]
    core = where_ref[CHIPS]
    panel = high.shape[0] // 2
    group = whole[0].shape[0] // 4

    def place(slot, ref):
        value = ref[...]
        chip = where_ref[slot]
        for part in range(2):
            for swap in range(2):
                row = (2 * part + swap) * group
                first, second, third = split3(value[row : row + group])
                start = pl.multiple_of(
                    part * panel + chip * 2 * group + group * (core ^ swap), group
                )
                high[pl.ds(start, group), :] = first
                middle[pl.ds(start, group), :] = second
                low[pl.ds(start, group), :] = third

    for slot in range(4):
        place(slot, whole[slot])

    @pl.when(step < steps // 2)
    def _():
        for slot in range(4):
            place(4 + slot, early[slot])

    @pl.when(step >= steps // 2)
    def _():
        for slot in range(4):
            place(4 + slot, late[slot])

    @pl.when(step == 0)
    def _():
        even[...] = jnp.zeros_like(even)
        skew[...] = jnp.zeros_like(skew)
        proj[...] = jnp.zeros_like(proj)

    one, two, three = high[...], middle[...], low[...]
    even[:panel] += nt(one[:panel], one) + nt(two[:panel], two)
    even[panel:, panel:] += nt(one[panel:], one[panel:]) + nt(two[panel:], two[panel:])
    skew[...] += nt(one, two) + nt(one, three)
    current = jnp.concatenate([own_ref[...], other_ref[...]], axis=1)
    first, second, third = split3(current)
    proj[...] += (
        (nn(one, third) + nn(three, first) + nn(two, second))
        + (nn(one, second) + nn(two, first))
        + nn(one, first)
    )

    @pl.when(step == steps - 1)
    def _():
        rows = 2 * panel
        out_ref[core, 0:rows, :] = proj[:, :WIDE]
        out_ref[1 - core, 0:rows, :] = proj[:, WIDE:]
        for part in range(2):
            for place_at, (i, j) in enumerate(PIECES[part]):
                at_i, at_j = slice(i * WIDE, (i + 1) * WIDE), slice(j * WIDE, (j + 1) * WIDE)
                block = even[at_i, at_j] + (skew[at_i, at_j] + skew[at_j, at_i].T)
                start = rows + place_at * WIDE
                out_ref[part, start : start + WIDE, :] = block


def solve_kernel(where_ref, mine_ref, other_ref, own_ref, partner_ref, both):
    core = where_ref[CHIPS]
    both[core] = mine_ref[...]
    both[1 - core] = other_ref[...]
    count = 4
    size = count * WIDE
    panel = size // 2
    base = 16

    def block(i, j):
        for part in range(2):
            if (i, j) in PIECES[part]:
                start = size + PIECES[part].index((i, j)) * WIDE
                return both[part, start : start + WIDE, :]

    row = lax.broadcasted_iota(jnp.int32, (WIDE, WIDE), 0)
    column = lax.broadcasted_iota(jnp.int32, (WIDE, WIDE), 1)
    same = (row // base) == (column // base)
    diagonals = []
    for i in range(count):
        value = block(i, i)
        diagonals.append(
            jnp.where(row < column, value, jnp.where(row == column, value * 0.5, 0.0))
        )
    lane = lax.broadcasted_iota(jnp.int32, (base, WIDE), 1) % base
    ones = jnp.where(same, 1.0, 0.0).astype(F32)
    spread = []
    for i in range(count):
        flipped = jnp.where(same, diagonals[i], 0.0).T
        folded = flipped[0:base]
        for k in range(1, WIDE // base):
            folded = folded + flipped[k * base : (k + 1) * base]
        stacked = jnp.concatenate([jnp.where(lane == k, folded, 0.0) for k in range(base)], axis=0)
        spread.append(full(stacked, ones))
    wide_lane = lax.broadcasted_iota(jnp.int32, (1, size), 1) % base
    wide_row = lax.broadcasted_iota(jnp.int32, (base, size), 0)
    solved = jnp.zeros((base, size), F32)
    for i in range(base - 1, -1, -1):
        factor = jnp.concatenate([s[i * base : (i + 1) * base] for s in spread], axis=1)
        total = jnp.sum(factor * solved, axis=0, keepdims=True)
        line = (jnp.where(wide_lane == i, 1.0, 0.0) - total) / factor[i : i + 1]
        solved = jnp.where(wide_row == i, line, solved)

    big_row = lax.broadcasted_iota(jnp.int32, (panel, panel), 0)
    big_column = lax.broadcasted_iota(jnp.int32, (panel, panel), 1)
    inverses = []
    for half in range(2):
        left, right = 2 * half, 2 * half + 1
        top = jnp.concatenate([diagonals[left], block(left, right)], axis=1)
        bottom = jnp.concatenate([jnp.zeros((WIDE, WIDE), F32), diagonals[right]], axis=1)
        factor = jnp.concatenate([top, bottom], axis=0)
        lines = solved[:, half * panel : (half + 1) * panel]
        tiled = jnp.concatenate([lines] * (panel // base), axis=0)
        inverse = jnp.where((big_row // base) == (big_column // base), tiled, 0.0)
        width = base
        while width < panel:
            picked = (
                ((big_row // width) % 2 == 0) & (big_column // width == big_row // width + 1)
            )
            coupling = jnp.where(picked, factor, 0.0)
            inverse = inverse - full(full(inverse, coupling), inverse)
            width *= 2
        inverses.append(inverse)
    corner = jnp.concatenate(
        [
            jnp.concatenate([block(0, 2), block(0, 3)], axis=1),
            jnp.concatenate([block(1, 2), block(1, 3)], axis=1),
        ],
        axis=0,
    )
    right_side = jnp.concatenate([mine_ref[0:size, :], other_ref[0:size, :]], axis=1)
    second = full(inverses[1], right_side[panel:])
    first = full(inverses[0], right_side[:panel] - full(corner, second))
    own_ref[0:panel, :] = first[:, :WIDE]
    own_ref[panel:, :] = second[:, :WIDE]
    partner_ref[0:panel, :] = first[:, WIDE:]
    partner_ref[panel:, :] = second[:, WIDE:]


def apply_kernel(where_ref, *refs):
    steps = pl.num_programs(0)
    step = pl.program_id(0)
    whole = refs[0:4]
    early = refs[4:8]
    late = refs[8:12]
    current_own, current_other, solved_own, solved_other, out_own, out_other, high, middle, low = refs[12:]
    core = where_ref[CHIPS]
    panel = solved_own.shape[0] // 2
    group = whole[0].shape[0] // 4

    @pl.when(step == 0)
    def _():
        for slot in range(CHIPS):
            chip = where_ref[slot]
            for part in range(2):
                for swap in range(2):
                    start = pl.multiple_of(
                        part * panel + chip * 2 * group + group * (core ^ swap), group
                    )
                    lines = jnp.concatenate(
                        [solved_own[pl.ds(start, group), :], solved_other[pl.ds(start, group), :]],
                        axis=1,
                    )
                    first, second, third = split3(lines)
                    at = slot * 4 * group + (2 * part + swap) * group
                    high[at : at + group, :] = first
                    middle[at : at + group, :] = second
                    low[at : at + group, :] = third

    def run(refs8):
        value = jnp.concatenate([r[...] for r in refs8], axis=0)
        one, two, three = split3(value)
        first, second, third = high[...], middle[...], low[...]

        def tn(left, right):
            return lax.dot_general(
                left, right, (((0,), (0,)), ((), ())), preferred_element_type=F32
            )

        change = (
            (tn(one, third) + tn(three, first) + tn(two, second))
            + (tn(one, second) + tn(two, first))
            + tn(one, first)
        )
        out_own[...] = current_own[...] - change[:, :WIDE]
        out_other[...] = current_other[...] - change[:, WIDE:]

    @pl.when(step < steps // 2)
    def _():
        run(list(whole) + list(early))

    @pl.when(step >= steps // 2)
    def _():
        run(list(whole) + list(late))


def piece_specs(chunk, half_steps):
    whole = [pl.BlockSpec((chunk, TILE), lambda j, w: (0, j))] * 4
    early = [pl.BlockSpec((chunk, TILE), lambda j, w: (0, jnp.minimum(j, half_steps - 1)))] * 4
    late = [pl.BlockSpec((chunk, TILE), lambda j, w: (0, jnp.maximum(j - half_steps, 0)))] * 4
    return whole + early + late


def per_device(vectors, panel_one, panel_two):
    rows, columns = vectors.shape
    group = panel_one.shape[1]
    half = rows // 2
    quarter = half // 2
    chunk = 4 * group
    size = 2 * group * CHIPS * CORES
    steps = half // TILE
    at = lax.axis_index("col")
    core, depth, plane = at % CORES, (at // CORES) % DEPTH, at // (CORES * DEPTH)

    def permute(value, move):
        pairs = []
        for source in range(CHIPS * CORES):
            k, z, x = source % CORES, (source // CORES) % DEPTH, source // (CORES * DEPTH)
            k, z, x = move(k, z, x)
            pairs.append((source, (x * DEPTH + z % DEPTH) * CORES + k))
        return lax.ppermute(value, "col", pairs)

    def core_swap(value):
        return permute(value, lambda k, z, x: (1 - k, z, x))

    def up(value):
        return permute(value, lambda k, z, x: (k, z + 1, x))

    def down(value):
        return permute(value, lambda k, z, x: (k, z - 1, x))

    def across(value):
        return permute(value, lambda k, z, x: (k, z, 1 - x))

    flat = jnp.stack([panel_one.T, panel_two.T])
    keep = lax.dynamic_slice_in_dim(flat, core * half, half, 2)
    give = lax.dynamic_slice_in_dim(flat, (1 - core) * half, half, 2)
    got = core_swap(give)
    chunk_own = jnp.stack([keep, got], axis=1).reshape(chunk, half)

    away = across(chunk_own)
    below = up(chunk_own)
    above = down(chunk_own)
    far_late = down(above[:, quarter:])
    away_below_early = up(away[:, :quarter])
    far_early = up(below[:, :quarter])
    away_above_early = down(away[:, :quarter])
    away_below_late = across(below[:, quarter:])
    away_above_late = across(above[:, quarter:])
    away_far_late = across(far_late)
    away_far_early = up(away_below_early)

    pieces = (
        chunk_own, below, above, away,
        far_early, away_below_early, away_above_early, away_far_early,
        far_late, away_below_late, away_above_late, away_far_late,
    )
    chips = []
    for x_step, z_step in ((0, 0), (0, -1), (0, 1), (1, 0), (0, 2), (1, -1), (1, 1), (1, 2)):
        chips.append(jnp.bitwise_xor(plane, x_step) * DEPTH + (depth + z_step) % DEPTH)
    where = jnp.stack(chips + [core]).astype(jnp.int32)

    given = lax.dynamic_slice_in_dim(vectors, (1 - core) * half, half, 0)
    other = core_swap(given)

    piece_in = piece_specs(chunk, steps // 2)
    own_spec = pl.BlockSpec((TILE, columns), lambda j, w: (w[CHIPS] * steps + j, 0))
    other_spec = pl.BlockSpec((TILE, columns), lambda j, w: (j, 0))
    length = size + 5 * WIDE
    gathered = pl.pallas_call(
        gram_kernel,
        out_shape=jax.ShapeDtypeStruct((2, length, WIDE), F32),
        grid_spec=pltpu.PrefetchScalarGridSpec(
            num_scalar_prefetch=1,
            grid=(steps,),
            in_specs=piece_in + [own_spec, other_spec],
            out_specs=pl.BlockSpec((2, length, WIDE), lambda j, w: (0, 0, 0)),
            scratch_shapes=[pltpu.VMEM((size, TILE), BF16)] * 3
            + [pltpu.VMEM((size, size), F32)] * 2
            + [pltpu.VMEM((size, 2 * WIDE), F32)],
        ),
        compiler_params=pltpu.CompilerParams(
            dimension_semantics=("arbitrary",), vmem_limit_bytes=40 << 20
        ),
        name="gram",
    )(where, *pieces, vectors, other)

    mine = lax.dynamic_index_in_dim(gathered, core, 0, keepdims=False)
    send = lax.dynamic_index_in_dim(gathered, 1 - core, 0, keepdims=False)
    mine = mine + core_swap(send)
    members = lax.axis_size("row")
    parts = lax.all_to_all(mine.reshape(members, length // members, WIDE), "row", 0, 0)
    total = jnp.sum(parts, axis=0)
    spread = jnp.broadcast_to(total[None], (members,) + total.shape)
    mine = lax.all_to_all(spread, "row", 0, 0).reshape(length, WIDE)
    theirs = core_swap(mine)

    solved_own, solved_other = pl.pallas_call(
        solve_kernel,
        out_shape=[jax.ShapeDtypeStruct((size, WIDE), F32)] * 2,
        grid_spec=pltpu.PrefetchScalarGridSpec(
            num_scalar_prefetch=1,
            grid=(1,),
            in_specs=[pl.BlockSpec((length, WIDE), lambda j, w: (0, 0))] * 2,
            out_specs=[pl.BlockSpec((size, WIDE), lambda j, w: (0, 0))] * 2,
            scratch_shapes=[pltpu.VMEM((2, length, WIDE), F32)],
        ),
        compiler_params=pltpu.CompilerParams(vmem_limit_bytes=32 << 20),
        name="solve",
    )(where, mine, theirs)

    result_own, result_other = pl.pallas_call(
        apply_kernel,
        out_shape=[jax.ShapeDtypeStruct((half, columns), F32)] * 2,
        grid_spec=pltpu.PrefetchScalarGridSpec(
            num_scalar_prefetch=1,
            grid=(steps,),
            in_specs=piece_in
            + [own_spec, other_spec]
            + [pl.BlockSpec((size, WIDE), lambda j, w: (0, 0))] * 2,
            out_specs=[pl.BlockSpec((TILE, columns), lambda j, w: (j, 0))] * 2,
            scratch_shapes=[pltpu.VMEM((size, 2 * WIDE), BF16)] * 3,
        ),
        compiler_params=pltpu.CompilerParams(
            dimension_semantics=("arbitrary",), vmem_limit_bytes=40 << 20
        ),
        name="apply",
    )(where, *pieces, vectors, other, solved_own, solved_other)

    returned = core_swap(result_other)
    result = jnp.zeros((rows, columns), F32)
    result = lax.dynamic_update_slice_in_dim(result, result_own, core * half, 0)
    return lax.dynamic_update_slice_in_dim(result, returned, (1 - core) * half, 0)


def solution(mesh):
    specs = (P("row", "col"), P("row", "col"), P("row", "col"))
    return jax.shard_map(
        per_device, mesh=mesh, in_specs=specs, out_specs=P("row", "col"), check_vma=False
    )
```

```python
import functools

import jax
import jax.numpy as jnp
from jax import lax
from jax.experimental import pallas as pl
from jax.experimental.pallas import tpu as pltpu
from jax.sharding import PartitionSpec as P

F32 = jnp.float32
BF16 = jnp.bfloat16
HIGHEST = lax.Precision.HIGHEST
PLANES, DEPTH, CORES = 2, 4, 2
CHIPS = PLANES * DEPTH
WIDE = 128
TILE = 512
PIECES = ((0, 0), (0, 1), (1, 1), (0, 2), (0, 3)), ((1, 2), (1, 3), (2, 2), (2, 3), (3, 3))


def split3(value):
    high = value.astype(BF16)
    rest = value - high.astype(F32)
    middle = rest.astype(BF16)
    low = (rest - middle.astype(F32)).astype(BF16)
    return high, middle, low


def nn(left, right):
    return lax.dot_general(left, right, (((1,), (0,)), ((), ())), preferred_element_type=F32)


def nt(left, right):
    return lax.dot_general(left, right, (((1,), (1,)), ((), ())), preferred_element_type=F32)


def full(left, right):
    return lax.dot_general(
        left, right, (((1,), (0,)), ((), ())), precision=HIGHEST, preferred_element_type=F32
    )


def gram_kernel(where_ref, *refs, pieces, first):
    steps = pl.num_programs(0)
    step = pl.program_id(0)
    panels, rest = refs[:pieces], refs[pieces:]
    if first:
        own_ref, other_ref, out_ref, high, middle, low, even, skew, proj = rest
    else:
        own_ref, other_ref, before_ref, out_ref, high, middle, low, even, skew, proj = rest
    core = where_ref[CHIPS]
    lines = panels[0].shape[0]
    half = even.shape[1]
    start_row = high.shape[0] - half

    for index, ref in enumerate(panels):
        parts = split3(ref[...])
        begin = pl.multiple_of((index // 2) * 2 * lines + lines * (core ^ (index % 2)), lines)
        for target, value in zip((high, middle, low), parts):
            target[pl.ds(begin, lines), :] = value

    @pl.when(step == 0)
    def _():
        even[...] = jnp.zeros_like(even)
        skew[...] = jnp.zeros_like(skew)
        proj[...] = jnp.zeros_like(proj)

    one, two, three = high[start_row:, :], middle[start_row:, :], low[start_row:, :]
    skew[...] += nt(one, two) + nt(one, three)
    if first:
        even[...] += nt(one, one) + nt(two, two)
    else:
        even[half:, :] += nt(one, one) + nt(two, two)
        one_a, two_a, three_a = high[:half, :], middle[:half, :], low[:half, :]
        even[:half, :] += (
            (nt(one_a, three) + nt(three_a, one) + nt(two_a, two))
            + (nt(one_a, two) + nt(two_a, one))
            + nt(one_a, one)
        )
    current = jnp.concatenate([own_ref[...], other_ref[...]], axis=1)
    x_one, x_two, x_three = split3(current)
    proj[...] += (
        (nn(one, x_three) + nn(three, x_one) + nn(two, x_two))
        + (nn(one, x_two) + nn(two, x_one))
        + nn(one, x_one)
    )

    @pl.when(step == steps - 1)
    def _():
        def corner(i, j):
            at_i, at_j = slice(i * WIDE, (i + 1) * WIDE), slice(j * WIDE, (j + 1) * WIDE)
            base = even.shape[0] - half
            return (
                even[base + i * WIDE : base + (i + 1) * WIDE, at_j]
                + skew[at_i, at_j]
                + skew[at_j, at_i].T
            )

        if first:
            out_ref[core, 0:half, :] = proj[:, :WIDE]
            out_ref[1 - core, 0:half, :] = proj[:, WIDE:]
            for place, (i, j) in enumerate(((0, 0), (0, 1), (1, 1))):
                begin = half + place * WIDE
                out_ref[0, begin : begin + WIDE, :] = corner(i, j)
                out_ref[1, begin : begin + WIDE, :] = jnp.zeros((WIDE, WIDE), F32)
        else:
            out_ref[0, 0:half, :] = before_ref[0, 0:half, :]
            out_ref[1, 0:half, :] = before_ref[1, 0:half, :]
            out_ref[core, half : 2 * half, :] = proj[:, :WIDE]
            out_ref[1 - core, half : 2 * half, :] = proj[:, WIDE:]
            for part in range(2):
                for place, (i, j) in enumerate(PIECES[part]):
                    begin = 2 * half + place * WIDE
                    if j < 2:
                        source = half + ((0, 0), (0, 1), (1, 1)).index((i, j)) * WIDE
                        block = before_ref[0, source : source + WIDE, :]
                    elif i < 2:
                        block = even[i * WIDE : (i + 1) * WIDE, (j - 2) * WIDE : (j - 1) * WIDE]
                    else:
                        block = corner(i - 2, j - 2)
                    out_ref[part, begin : begin + WIDE, :] = block


def solve_kernel(where_ref, mine_ref, other_ref, own_ref, partner_ref, both, rows_done, ordered, sides):
    core = where_ref[CHIPS]
    both[core] = mine_ref[...]
    both[1 - core] = other_ref[...]
    count = 4
    size = count * WIDE
    panel = size // 2
    base = 16

    def relative(i, j):
        for part in range(2):
            if (i, j) in PIECES[part]:
                start = size + PIECES[part].index((i, j)) * WIDE
                return both[part, start : start + WIDE, :]

    group = size // (2 * CORES * CHIPS)

    def target(index):
        slot, at_core, part = index // (2 * CORES), (index // 2) % CORES, index % 2
        start = part * panel + where_ref[slot] * CORES * group + at_core * group
        return pl.ds(pl.multiple_of(start, group), group)

    for i in range(count):
        strip = jnp.concatenate(
            [relative(i, j) if i <= j else relative(j, i).T for j in range(count)], axis=1
        )
        for k in range(WIDE // group):
            rows_done[target(i * (WIDE // group) + k), :] = strip[k * group : (k + 1) * group]
    for i in range(count):
        strip = jnp.concatenate(
            [
                rows_done[j * WIDE : (j + 1) * WIDE, i * WIDE : (i + 1) * WIDE].T
                for j in range(count)
            ],
            axis=1,
        )
        for k in range(WIDE // group):
            ordered[target(i * (WIDE // group) + k), :] = strip[k * group : (k + 1) * group]
    for index in range(size // group):
        at = slice(index * group, (index + 1) * group)
        sides[target(index), :] = jnp.concatenate([mine_ref[at, :], other_ref[at, :]], axis=1)

    def block(i, j):
        return ordered[i * WIDE : (i + 1) * WIDE, j * WIDE : (j + 1) * WIDE]

    row = lax.broadcasted_iota(jnp.int32, (WIDE, WIDE), 0)
    column = lax.broadcasted_iota(jnp.int32, (WIDE, WIDE), 1)
    same = (row // base) == (column // base)
    diagonals = []
    for i in range(count):
        value = block(i, i)
        diagonals.append(
            jnp.where(row < column, value, jnp.where(row == column, value * 0.5, 0.0))
        )
    lane = lax.broadcasted_iota(jnp.int32, (base, WIDE), 1) % base
    ones = jnp.where(same, 1.0, 0.0).astype(F32)
    spread = []
    for i in range(count):
        flipped = jnp.where(same, diagonals[i], 0.0).T
        folded = flipped[0:base]
        for k in range(1, WIDE // base):
            folded = folded + flipped[k * base : (k + 1) * base]
        stacked = jnp.concatenate([jnp.where(lane == k, folded, 0.0) for k in range(base)], axis=0)
        spread.append(full(stacked, ones))
    wide_lane = lax.broadcasted_iota(jnp.int32, (1, size), 1) % base
    wide_row = lax.broadcasted_iota(jnp.int32, (base, size), 0)
    solved = jnp.zeros((base, size), F32)
    for i in range(base - 1, -1, -1):
        factor = jnp.concatenate([s[i * base : (i + 1) * base] for s in spread], axis=1)
        total = jnp.sum(factor * solved, axis=0, keepdims=True)
        line = (jnp.where(wide_lane == i, 1.0, 0.0) - total) / factor[i : i + 1]
        solved = jnp.where(wide_row == i, line, solved)

    big_row = lax.broadcasted_iota(jnp.int32, (panel, panel), 0)
    big_column = lax.broadcasted_iota(jnp.int32, (panel, panel), 1)
    inverses = []
    for half in range(2):
        left, right = 2 * half, 2 * half + 1
        top = jnp.concatenate([diagonals[left], block(left, right)], axis=1)
        bottom = jnp.concatenate([jnp.zeros((WIDE, WIDE), F32), diagonals[right]], axis=1)
        factor = jnp.concatenate([top, bottom], axis=0)
        lines = solved[:, half * panel : (half + 1) * panel]
        tiled = jnp.concatenate([lines] * (panel // base), axis=0)
        inverse = jnp.where((big_row // base) == (big_column // base), tiled, 0.0)
        width = base
        while width < panel:
            picked = (
                ((big_row // width) % 2 == 0) & (big_column // width == big_row // width + 1)
            )
            coupling = jnp.where(picked, factor, 0.0)
            inverse = inverse - full(full(inverse, coupling), inverse)
            width *= 2
        inverses.append(inverse)
    corner = jnp.concatenate(
        [
            jnp.concatenate([block(0, 2), block(0, 3)], axis=1),
            jnp.concatenate([block(1, 2), block(1, 3)], axis=1),
        ],
        axis=0,
    )
    right_side = sides[...]
    second = full(inverses[1], right_side[panel:])
    first = full(inverses[0], right_side[:panel] - full(corner, second))
    own_ref[0:panel, :] = first[:, :WIDE]
    own_ref[panel:, :] = second[:, :WIDE]
    partner_ref[0:panel, :] = first[:, WIDE:]
    partner_ref[panel:, :] = second[:, WIDE:]


def apply_kernel(where_ref, *refs):
    step = pl.program_id(0)
    panels = refs[: 2 * CHIPS]
    current_own, current_other, solved_own, solved_other, out_own, out_other, high, middle, low = refs[
        2 * CHIPS :
    ]
    core = where_ref[CHIPS]
    panel = solved_own.shape[0] // 2
    group = panels[0].shape[0] // 2

    @pl.when(step == 0)
    def _():
        for index in range(2 * CHIPS):
            chip = where_ref[index // 2]
            for part in range(2):
                start = pl.multiple_of(
                    part * panel + chip * 2 * group + group * (core ^ (index % 2)), group
                )
                lines = jnp.concatenate(
                    [solved_own[pl.ds(start, group), :], solved_other[pl.ds(start, group), :]],
                    axis=1,
                )
                at = (2 * index + part) * group
                for target, value in zip((high, middle, low), split3(lines)):
                    target[at : at + group, :] = value

    value = jnp.concatenate([r[...] for r in panels], axis=0)
    one, two, three = split3(value)
    first, second, third = high[...], middle[...], low[...]

    def tn(left, right):
        return lax.dot_general(left, right, (((0,), (0,)), ((), ())), preferred_element_type=F32)

    change = (
        (tn(one, third) + tn(three, first) + tn(two, second))
        + (tn(one, second) + tn(two, first))
        + tn(one, first)
    )
    out_own[...] = current_own[...] - change[:, :WIDE]
    out_other[...] = current_other[...] - change[:, WIDE:]


def per_device(vectors, panel_one, panel_two):
    rows, columns = vectors.shape
    group = panel_one.shape[1]
    half = rows // 2
    size = 2 * group * CHIPS * CORES
    steps = half // TILE
    at = lax.axis_index("col")
    core, depth, plane = at % CORES, (at // CORES) % DEPTH, at // (CORES * DEPTH)

    def permute(value, move):
        pairs = []
        for source in range(CHIPS * CORES):
            k, z, x = source % CORES, (source // CORES) % DEPTH, source // (CORES * DEPTH)
            k, z, x = move(k, z, x)
            pairs.append((source, (x * DEPTH + z % DEPTH) * CORES + k))
        return lax.ppermute(value, "col", pairs)

    def core_swap(value):
        return permute(value, lambda k, z, x: (1 - k, z, x))

    def up(value):
        return permute(value, lambda k, z, x: (k, z + 1, x))

    def down(value):
        return permute(value, lambda k, z, x: (k, z - 1, x))

    def across(value):
        return permute(value, lambda k, z, x: (k, z, 1 - x))

    def half_of(which):
        picked = [lax.dynamic_slice_in_dim(v.T, which * half, half, 1) for v in (panel_one, panel_two)]
        return jnp.concatenate(picked, axis=0)

    a_own = half_of(core)
    b_own = core_swap(half_of(1 - core))
    given = lax.dynamic_slice_in_dim(vectors, (1 - core) * half, half, 0)
    other = core_swap(given)

    a_away, a_below, a_above = across(a_own), up(a_own), down(a_own)
    b_away, b_below, b_above = across(b_own), up(b_own), down(b_own)
    a_away_below = up(a_away)
    a_away_above = down(a_away)
    a_far = up(a_below)
    b_away_below = across(b_below)
    b_far = down(b_above)
    b_away_above = across(b_above)
    a_away_far = up(a_away_below)
    b_away_far = across(b_far)

    near = (a_own, b_own, a_below, b_below, a_above, b_above, a_away, b_away)
    distant = (
        a_far, b_far, a_away_below, b_away_below,
        a_away_above, b_away_above, a_away_far, b_away_far,
    )
    chips = []
    for x_step, z_step in ((0, 0), (0, -1), (0, 1), (1, 0), (0, 2), (1, -1), (1, 1), (1, 2)):
        chips.append(jnp.bitwise_xor(plane, x_step) * DEPTH + (depth + z_step) % DEPTH)
    where = jnp.stack(chips + [core]).astype(jnp.int32)

    lines = 2 * group
    piece = pl.BlockSpec((lines, TILE), lambda j, w: (0, j))
    own_spec = pl.BlockSpec((TILE, columns), lambda j, w: (w[CHIPS] * steps + j, 0))
    other_spec = pl.BlockSpec((TILE, columns), lambda j, w: (j, 0))
    length = size + 5 * WIDE
    span = size // 2

    def gram(first, pieces, extra):
        rows_out = span + 3 * WIDE if first else length
        extra_specs = [pl.BlockSpec(v.shape, lambda j, w: (0, 0, 0)) for v in extra]
        height = span if first else size
        units = 10 if first else 16
        return pl.pallas_call(
            functools.partial(gram_kernel, pieces=len(pieces), first=first),
            out_shape=jax.ShapeDtypeStruct((2, rows_out, WIDE), F32),
            grid_spec=pltpu.PrefetchScalarGridSpec(
                num_scalar_prefetch=1,
                grid=(steps,),
                in_specs=[piece] * len(pieces) + [own_spec, other_spec] + extra_specs,
                out_specs=pl.BlockSpec((2, rows_out, WIDE), lambda j, w: (0, 0, 0)),
                scratch_shapes=[pltpu.VMEM((height, TILE), BF16)] * 3
                + [
                    pltpu.VMEM((height, span), F32),
                    pltpu.VMEM((span, span), F32),
                    pltpu.VMEM((span, 2 * WIDE), F32),
                ],
            ),
            compiler_params=pltpu.CompilerParams(
                dimension_semantics=("arbitrary",), vmem_limit_bytes=32 << 20
            ),
            cost_estimate=pl.CostEstimate(
                flops=2 * units * span * span * half,
                bytes_accessed=4 * half * (height + columns * 2),
                transcendentals=0,
            ),
            name="gram_near" if first else "gram_far",
        )(where, *pieces, vectors, other, *extra)

    before = gram(True, near, ())
    gathered = gram(False, near + distant, (before,))

    mine = lax.dynamic_index_in_dim(gathered, core, 0, keepdims=False)
    send = lax.dynamic_index_in_dim(gathered, 1 - core, 0, keepdims=False)
    mine = mine + core_swap(send)
    members = lax.axis_size("row")
    parts = lax.all_to_all(mine.reshape(members, length // members, WIDE), "row", 0, 0)
    total = jnp.sum(parts, axis=0)
    spread = jnp.broadcast_to(total[None], (members,) + total.shape)
    mine = lax.all_to_all(spread, "row", 0, 0).reshape(length, WIDE)
    theirs = core_swap(mine)

    solved_own, solved_other = pl.pallas_call(
        solve_kernel,
        out_shape=[jax.ShapeDtypeStruct((size, WIDE), F32)] * 2,
        grid_spec=pltpu.PrefetchScalarGridSpec(
            num_scalar_prefetch=1,
            grid=(1,),
            in_specs=[pl.BlockSpec((length, WIDE), lambda j, w: (0, 0))] * 2,
            out_specs=[pl.BlockSpec((size, WIDE), lambda j, w: (0, 0))] * 2,
            scratch_shapes=[pltpu.VMEM((2, length, WIDE), F32)]
            + [pltpu.VMEM((size, size), F32)] * 2
            + [pltpu.VMEM((size, 2 * WIDE), F32)],
        ),
        compiler_params=pltpu.CompilerParams(vmem_limit_bytes=32 << 20),
        name="solve",
    )(where, mine, theirs)

    result_own, result_other = pl.pallas_call(
        apply_kernel,
        out_shape=[jax.ShapeDtypeStruct((half, columns), F32)] * 2,
        grid_spec=pltpu.PrefetchScalarGridSpec(
            num_scalar_prefetch=1,
            grid=(steps,),
            in_specs=[piece] * (2 * CHIPS)
            + [own_spec, other_spec]
            + [pl.BlockSpec((size, WIDE), lambda j, w: (0, 0))] * 2,
            out_specs=[pl.BlockSpec((TILE, columns), lambda j, w: (j, 0))] * 2,
            scratch_shapes=[pltpu.VMEM((size, 2 * WIDE), BF16)] * 3,
        ),
        compiler_params=pltpu.CompilerParams(
            dimension_semantics=("arbitrary",), vmem_limit_bytes=40 << 20
        ),
        name="apply",
    )(where, *near, *distant, vectors, other, solved_own, solved_other)

    returned = core_swap(result_other)
    result = jnp.zeros((rows, columns), F32)
    result = lax.dynamic_update_slice_in_dim(result, result_own, core * half, 0)
    return lax.dynamic_update_slice_in_dim(result, returned, (1 - core) * half, 0)


def solution(mesh):
    specs = (P("row", "col"), P("row", "col"), P("row", "col"))
    return jax.shard_map(
        per_device, mesh=mesh, in_specs=specs, out_specs=P("row", "col"), check_vma=False
    )
```

```python
import functools

import jax
import jax.numpy as jnp
from jax import lax
from jax.experimental import pallas as pl
from jax.experimental.pallas import tpu as pltpu
from jax.sharding import PartitionSpec as P

F32 = jnp.float32
BF16 = jnp.bfloat16
HIGHEST = lax.Precision.HIGHEST
PLANES, DEPTH, CORES = 2, 4, 2
CHIPS = PLANES * DEPTH
WIDE = 128
TILE = 512
PIECES = ((0, 0), (0, 1), (1, 1), (0, 2), (0, 3)), ((1, 2), (1, 3), (2, 2), (2, 3), (3, 3))


def split3(value):
    high = value.astype(BF16)
    rest = value - high.astype(F32)
    middle = rest.astype(BF16)
    low = (rest - middle.astype(F32)).astype(BF16)
    return high, middle, low


def nn(left, right):
    return lax.dot_general(left, right, (((1,), (0,)), ((), ())), preferred_element_type=F32)


def nt(left, right):
    return lax.dot_general(left, right, (((1,), (1,)), ((), ())), preferred_element_type=F32)


def full(left, right):
    return lax.dot_general(
        left, right, (((1,), (0,)), ((), ())), precision=HIGHEST, preferred_element_type=F32
    )


def gram_kernel(where_ref, *refs, pieces, first):
    steps = pl.num_programs(0)
    step = pl.program_id(0)
    panels, rest = refs[:pieces], refs[pieces:]
    if first:
        own_ref, other_ref, out_ref, high, middle, low, even, skew, proj = rest
    else:
        own_ref, other_ref, before_ref, out_ref, high, middle, low, even, skew, proj = rest
    core = where_ref[CHIPS]
    lines = panels[0].shape[0]
    half = even.shape[1]
    start_row = high.shape[0] - half

    for index, ref in enumerate(panels):
        parts = split3(ref[...])
        begin = pl.multiple_of((index // 2) * 2 * lines + lines * (core ^ (index % 2)), lines)
        for target, value in zip((high, middle, low), parts):
            target[pl.ds(begin, lines), :] = value

    @pl.when(step == 0)
    def _():
        even[...] = jnp.zeros_like(even)
        skew[...] = jnp.zeros_like(skew)
        proj[...] = jnp.zeros_like(proj)

    one, two, three = high[start_row:, :], middle[start_row:, :], low[start_row:, :]
    skew[...] += nt(one, two) + nt(one, three)
    if first:
        even[...] += nt(one, one) + nt(two, two)
    else:
        even[half:, :] += nt(one, one) + nt(two, two)
        one_a, two_a, three_a = high[:half, :], middle[:half, :], low[:half, :]
        even[:half, :] += (
            (nt(one_a, three) + nt(three_a, one) + nt(two_a, two))
            + (nt(one_a, two) + nt(two_a, one))
            + nt(one_a, one)
        )
    current = jnp.concatenate([own_ref[...], other_ref[...]], axis=1)
    x_one, x_two, x_three = split3(current)
    proj[...] += (
        (nn(one, x_three) + nn(three, x_one) + nn(two, x_two))
        + (nn(one, x_two) + nn(two, x_one))
        + nn(one, x_one)
    )

    @pl.when(step == steps - 1)
    def _():
        def corner(i, j):
            at_i, at_j = slice(i * WIDE, (i + 1) * WIDE), slice(j * WIDE, (j + 1) * WIDE)
            base = even.shape[0] - half
            return (
                even[base + i * WIDE : base + (i + 1) * WIDE, at_j]
                + skew[at_i, at_j]
                + skew[at_j, at_i].T
            )

        if first:
            out_ref[core, 0:half, :] = proj[:, :WIDE]
            out_ref[1 - core, 0:half, :] = proj[:, WIDE:]
            for place, (i, j) in enumerate(((0, 0), (0, 1), (1, 1))):
                begin = half + place * WIDE
                out_ref[0, begin : begin + WIDE, :] = corner(i, j)
                out_ref[1, begin : begin + WIDE, :] = jnp.zeros((WIDE, WIDE), F32)
        else:
            out_ref[0, 0:half, :] = before_ref[0, 0:half, :]
            out_ref[1, 0:half, :] = before_ref[1, 0:half, :]
            out_ref[core, half : 2 * half, :] = proj[:, :WIDE]
            out_ref[1 - core, half : 2 * half, :] = proj[:, WIDE:]
            for part in range(2):
                for place, (i, j) in enumerate(PIECES[part]):
                    begin = 2 * half + place * WIDE
                    if j < 2:
                        source = half + ((0, 0), (0, 1), (1, 1)).index((i, j)) * WIDE
                        block = before_ref[0, source : source + WIDE, :]
                    elif i < 2:
                        block = even[i * WIDE : (i + 1) * WIDE, (j - 2) * WIDE : (j - 1) * WIDE]
                    else:
                        block = corner(i - 2, j - 2)
                    out_ref[part, begin : begin + WIDE, :] = block


def solve_kernel(where_ref, mine_ref, other_ref, own_ref, partner_ref, both, rows_done, ordered, sides):
    core = where_ref[CHIPS]
    both[core] = mine_ref[...]
    both[1 - core] = other_ref[...]
    count = 4
    size = count * WIDE
    panel = size // 2
    base = 16

    def relative(i, j):
        for part in range(2):
            if (i, j) in PIECES[part]:
                start = size + PIECES[part].index((i, j)) * WIDE
                return both[part, start : start + WIDE, :]

    group = size // (2 * CORES * CHIPS)

    def target(index):
        slot, at_core, part = index // (2 * CORES), (index // 2) % CORES, index % 2
        start = part * panel + where_ref[slot] * CORES * group + at_core * group
        return pl.ds(pl.multiple_of(start, group), group)

    for i in range(count):
        strip = jnp.concatenate(
            [relative(i, j) if i <= j else relative(j, i).T for j in range(count)], axis=1
        )
        for k in range(WIDE // group):
            rows_done[target(i * (WIDE // group) + k), :] = strip[k * group : (k + 1) * group]
    for i in range(count):
        strip = jnp.concatenate(
            [
                rows_done[j * WIDE : (j + 1) * WIDE, i * WIDE : (i + 1) * WIDE].T
                for j in range(count)
            ],
            axis=1,
        )
        for k in range(WIDE // group):
            ordered[target(i * (WIDE // group) + k), :] = strip[k * group : (k + 1) * group]
    for index in range(size // group):
        at = slice(index * group, (index + 1) * group)
        sides[target(index), :] = jnp.concatenate([mine_ref[at, :], other_ref[at, :]], axis=1)

    def block(i, j):
        return ordered[i * WIDE : (i + 1) * WIDE, j * WIDE : (j + 1) * WIDE]

    row = lax.broadcasted_iota(jnp.int32, (WIDE, WIDE), 0)
    column = lax.broadcasted_iota(jnp.int32, (WIDE, WIDE), 1)
    same = (row // base) == (column // base)
    diagonals = []
    for i in range(count):
        value = block(i, i)
        diagonals.append(
            jnp.where(row < column, value, jnp.where(row == column, value * 0.5, 0.0))
        )
    lane = lax.broadcasted_iota(jnp.int32, (base, WIDE), 1) % base
    ones = jnp.where(same, 1.0, 0.0).astype(F32)
    spread = []
    for i in range(count):
        flipped = jnp.where(same, diagonals[i], 0.0).T
        folded = flipped[0:base]
        for k in range(1, WIDE // base):
            folded = folded + flipped[k * base : (k + 1) * base]
        stacked = jnp.concatenate([jnp.where(lane == k, folded, 0.0) for k in range(base)], axis=0)
        spread.append(full(stacked, ones))
    wide_lane = lax.broadcasted_iota(jnp.int32, (1, size), 1) % base
    wide_row = lax.broadcasted_iota(jnp.int32, (base, size), 0)
    solved = jnp.zeros((base, size), F32)
    for i in range(base - 1, -1, -1):
        factor = jnp.concatenate([s[i * base : (i + 1) * base] for s in spread], axis=1)
        total = jnp.sum(factor * solved, axis=0, keepdims=True)
        line = (jnp.where(wide_lane == i, 1.0, 0.0) - total) / factor[i : i + 1]
        solved = jnp.where(wide_row == i, line, solved)

    big_row = lax.broadcasted_iota(jnp.int32, (panel, panel), 0)
    big_column = lax.broadcasted_iota(jnp.int32, (panel, panel), 1)
    inverses = []
    for half in range(2):
        left, right = 2 * half, 2 * half + 1
        top = jnp.concatenate([diagonals[left], block(left, right)], axis=1)
        bottom = jnp.concatenate([jnp.zeros((WIDE, WIDE), F32), diagonals[right]], axis=1)
        factor = jnp.concatenate([top, bottom], axis=0)
        lines = solved[:, half * panel : (half + 1) * panel]
        tiled = jnp.concatenate([lines] * (panel // base), axis=0)
        inverse = jnp.where((big_row // base) == (big_column // base), tiled, 0.0)
        width = base
        while width < panel:
            picked = (
                ((big_row // width) % 2 == 0) & (big_column // width == big_row // width + 1)
            )
            coupling = jnp.where(picked, factor, 0.0)
            inverse = inverse - full(full(inverse, coupling), inverse)
            width *= 2
        inverses.append(inverse)
    corner = jnp.concatenate(
        [
            jnp.concatenate([block(0, 2), block(0, 3)], axis=1),
            jnp.concatenate([block(1, 2), block(1, 3)], axis=1),
        ],
        axis=0,
    )
    right_side = sides[...]
    second = full(inverses[1], right_side[panel:])
    first = full(inverses[0], right_side[:panel] - full(corner, second))
    own_ref[0:panel, :] = first[:, :WIDE]
    own_ref[panel:, :] = second[:, :WIDE]
    partner_ref[0:panel, :] = first[:, WIDE:]
    partner_ref[panel:, :] = second[:, WIDE:]


def apply_kernel(where_ref, *refs):
    step = pl.program_id(0)
    panels = refs[: 2 * CHIPS]
    current_own, current_other, solved_own, solved_other, out_own, out_other, high, middle, low = refs[
        2 * CHIPS :
    ]
    core = where_ref[CHIPS]
    panel = solved_own.shape[0] // 2
    group = panels[0].shape[0] // 2

    @pl.when(step == 0)
    def _():
        for index in range(2 * CHIPS):
            chip = where_ref[index // 2]
            for part in range(2):
                start = pl.multiple_of(
                    part * panel + chip * 2 * group + group * (core ^ (index % 2)), group
                )
                lines = jnp.concatenate(
                    [solved_own[pl.ds(start, group), :], solved_other[pl.ds(start, group), :]],
                    axis=1,
                )
                at = (2 * index + part) * group
                for target, value in zip((high, middle, low), split3(lines)):
                    target[at : at + group, :] = value

    value = jnp.concatenate([r[...] for r in panels], axis=0)
    one, two, three = split3(value)
    first, second, third = high[...], middle[...], low[...]

    def tn(left, right):
        return lax.dot_general(left, right, (((0,), (0,)), ((), ())), preferred_element_type=F32)

    change = (
        (tn(one, third) + tn(three, first) + tn(two, second))
        + (tn(one, second) + tn(two, first))
        + tn(one, first)
    )
    out_own[...] = current_own[...] - change[:, :WIDE]
    out_other[...] = current_other[...] - change[:, WIDE:]


def per_device(vectors, panel_one, panel_two):
    rows, columns = vectors.shape
    group = panel_one.shape[1]
    half = rows // 2
    size = 2 * group * CHIPS * CORES
    steps = half // TILE
    at = lax.axis_index("col")
    core, depth, plane = at % CORES, (at // CORES) % DEPTH, at // (CORES * DEPTH)

    def permute(value, move):
        pairs = []
        for source in range(CHIPS * CORES):
            k, z, x = source % CORES, (source // CORES) % DEPTH, source // (CORES * DEPTH)
            k, z, x = move(k, z, x)
            pairs.append((source, (x * DEPTH + z % DEPTH) * CORES + k))
        return lax.ppermute(value, "col", pairs)

    def core_swap(value):
        return permute(value, lambda k, z, x: (1 - k, z, x))

    def up(value):
        return permute(value, lambda k, z, x: (k, z + 1, x))

    def down(value):
        return permute(value, lambda k, z, x: (k, z - 1, x))

    def across(value):
        return permute(value, lambda k, z, x: (k, z, 1 - x))

    def half_of(which):
        picked = [lax.dynamic_slice_in_dim(v.T, which * half, half, 1) for v in (panel_one, panel_two)]
        return jnp.concatenate(picked, axis=0)

    barrier = lax.optimization_barrier
    a_own = half_of(core)
    swapped = half_of(1 - core)
    b_own = core_swap(swapped)
    offset, _ = barrier(((1 - core) * half, swapped))
    given = lax.dynamic_slice_in_dim(vectors, offset, half, 0)
    other = core_swap(given)

    a_own, b_own, given = barrier((a_own, b_own, given))
    a_away, a_below, a_above, b_away = across(a_own), up(a_own), down(a_own), across(b_own)
    b_hold, other = barrier((b_own, other))
    b_below = up(b_hold)

    a_away, a_below, a_above, b_hold = barrier((a_away, a_below, a_above, b_hold))
    b_above = down(b_hold)
    a_away_below = up(a_away)
    a_far = up(a_below)

    b_away, b_below, b_above, a_hold = barrier((b_away, b_below, b_above, a_away))
    b_away_below = across(b_below)
    b_far = down(b_above)
    a_away_above = down(a_hold)

    a_away_below, b_above_hold = barrier((a_away_below, b_above))
    b_away_above = across(b_above_hold)
    a_away_far = up(a_away_below)
    b_away_far = across(b_far)

    near = (a_own, b_own, a_below, b_below, a_above, b_above, a_away, b_away)
    distant = (
        a_far, b_far, a_away_below, b_away_below,
        a_away_above, b_away_above, a_away_far, b_away_far,
    )
    chips = []
    for x_step, z_step in ((0, 0), (0, -1), (0, 1), (1, 0), (0, 2), (1, -1), (1, 1), (1, 2)):
        chips.append(jnp.bitwise_xor(plane, x_step) * DEPTH + (depth + z_step) % DEPTH)
    where = jnp.stack(chips + [core]).astype(jnp.int32)

    lines = 2 * group
    piece = pl.BlockSpec((lines, TILE), lambda j, w: (0, j))
    own_spec = pl.BlockSpec((TILE, columns), lambda j, w: (w[CHIPS] * steps + j, 0))
    other_spec = pl.BlockSpec((TILE, columns), lambda j, w: (j, 0))
    length = size + 5 * WIDE
    span = size // 2

    def gram(first, pieces, extra):
        rows_out = span + 3 * WIDE if first else length
        extra_specs = [pl.BlockSpec(v.shape, lambda j, w: (0, 0, 0)) for v in extra]
        height = span if first else size
        units = 10 if first else 16
        return pl.pallas_call(
            functools.partial(gram_kernel, pieces=len(pieces), first=first),
            out_shape=jax.ShapeDtypeStruct((2, rows_out, WIDE), F32),
            grid_spec=pltpu.PrefetchScalarGridSpec(
                num_scalar_prefetch=1,
                grid=(steps,),
                in_specs=[piece] * len(pieces) + [own_spec, other_spec] + extra_specs,
                out_specs=pl.BlockSpec((2, rows_out, WIDE), lambda j, w: (0, 0, 0)),
                scratch_shapes=[pltpu.VMEM((height, TILE), BF16)] * 3
                + [
                    pltpu.VMEM((height, span), F32),
                    pltpu.VMEM((span, span), F32),
                    pltpu.VMEM((span, 2 * WIDE), F32),
                ],
            ),
            compiler_params=pltpu.CompilerParams(
                dimension_semantics=("arbitrary",), vmem_limit_bytes=56 << 20
            ),
            cost_estimate=pl.CostEstimate(
                flops=2 * units * span * span * half,
                bytes_accessed=4 * half * (height + columns * 2),
                transcendentals=0,
            ),
            name="gram_near" if first else "gram_far",
        )(where, *pieces, vectors, other, *extra)

    before = gram(True, near, ())
    gathered = gram(False, near + distant, (before,))

    mine = lax.dynamic_index_in_dim(gathered, core, 0, keepdims=False)
    send = lax.dynamic_index_in_dim(gathered, 1 - core, 0, keepdims=False)
    mine = mine + core_swap(send)
    members = lax.axis_size("row")
    parts = lax.all_to_all(mine.reshape(members, length // members, WIDE), "row", 0, 0)
    total = jnp.sum(parts, axis=0)
    spread = jnp.broadcast_to(total[None], (members,) + total.shape)
    mine = lax.all_to_all(spread, "row", 0, 0).reshape(length, WIDE)
    theirs = core_swap(mine)

    solved_own, solved_other = pl.pallas_call(
        solve_kernel,
        out_shape=[jax.ShapeDtypeStruct((size, WIDE), F32)] * 2,
        grid_spec=pltpu.PrefetchScalarGridSpec(
            num_scalar_prefetch=1,
            grid=(1,),
            in_specs=[pl.BlockSpec((length, WIDE), lambda j, w: (0, 0))] * 2,
            out_specs=[pl.BlockSpec((size, WIDE), lambda j, w: (0, 0))] * 2,
            scratch_shapes=[pltpu.VMEM((2, length, WIDE), F32)]
            + [pltpu.VMEM((size, size), F32)] * 2
            + [pltpu.VMEM((size, 2 * WIDE), F32)],
        ),
        compiler_params=pltpu.CompilerParams(vmem_limit_bytes=32 << 20),
        name="solve",
    )(where, mine, theirs)

    result_own, result_other = pl.pallas_call(
        apply_kernel,
        out_shape=[jax.ShapeDtypeStruct((half, columns), F32)] * 2,
        grid_spec=pltpu.PrefetchScalarGridSpec(
            num_scalar_prefetch=1,
            grid=(steps,),
            in_specs=[piece] * (2 * CHIPS)
            + [own_spec, other_spec]
            + [pl.BlockSpec((size, WIDE), lambda j, w: (0, 0))] * 2,
            out_specs=[pl.BlockSpec((TILE, columns), lambda j, w: (j, 0))] * 2,
            scratch_shapes=[pltpu.VMEM((size, 2 * WIDE), BF16)] * 3,
        ),
        compiler_params=pltpu.CompilerParams(
            dimension_semantics=("arbitrary",), vmem_limit_bytes=56 << 20
        ),
        name="apply",
    )(where, *near, *distant, vectors, other, solved_own, solved_other)

    returned = core_swap(result_other)
    result = jnp.zeros((rows, columns), F32)
    result = lax.dynamic_update_slice_in_dim(result, result_own, core * half, 0)
    return lax.dynamic_update_slice_in_dim(result, returned, (1 - core) * half, 0)


def solution(mesh):
    specs = (P("row", "col"), P("row", "col"), P("row", "col"))
    return jax.shard_map(
        per_device, mesh=mesh, in_specs=specs, out_specs=P("row", "col"), check_vma=False
    )
```

```python
import functools

import jax
import jax.numpy as jnp
from jax import lax
from jax.experimental import pallas as pl
from jax.experimental.pallas import tpu as pltpu
from jax.sharding import PartitionSpec as P

F32 = jnp.float32
BF16 = jnp.bfloat16
HIGHEST = lax.Precision.HIGHEST
PLANES, DEPTH, CORES = 2, 4, 2
CHIPS = PLANES * DEPTH
WIDE = 128
TILE = 512
LIMIT = 24 << 20
PIECES = ((0, 0), (0, 1), (1, 1), (0, 2), (0, 3)), ((1, 2), (1, 3), (2, 2), (2, 3), (3, 3))


def split3(value):
    high = value.astype(BF16)
    rest = value - high.astype(F32)
    middle = rest.astype(BF16)
    low = (rest - middle.astype(F32)).astype(BF16)
    return high, middle, low


def nn(left, right):
    return lax.dot_general(left, right, (((1,), (0,)), ((), ())), preferred_element_type=F32)


def nt(left, right):
    return lax.dot_general(left, right, (((1,), (1,)), ((), ())), preferred_element_type=F32)


def full(left, right):
    return lax.dot_general(
        left, right, (((1,), (0,)), ((), ())), precision=HIGHEST, preferred_element_type=F32
    )


def each_far(step, steps, refs, place):
    up_ref, down_ref, across_ref, end_up_ref, end_across_ref = refs
    chunk = down_ref.shape[0]
    early = step < steps // 2

    @pl.when(early)
    def _():
        place(4, up_ref[:chunk])
        place(5, up_ref[chunk:])
        place(6, down_ref[...])
        place(7, end_up_ref[...])

    @pl.when(jnp.logical_not(early))
    def _():
        place(4, down_ref[...])
        place(5, across_ref[:chunk])
        place(6, across_ref[chunk:])
        place(7, end_across_ref[...])


def gram_kernel(where_ref, *refs, first):
    steps = pl.num_programs(0)
    step = pl.program_id(0)
    count = 4 if first else 9
    panels, rest = refs[:count], refs[count:]
    if first:
        own_ref, other_ref, out_ref, high, middle, low, even, skew, proj = rest
    else:
        own_ref, other_ref, before_ref, keep_ref, send_ref, high, middle, low, even, skew, proj = rest
    core = where_ref[CHIPS]
    lines = panels[0].shape[0] // 2
    half = even.shape[1]
    start_row = high.shape[0] - half

    def place(slot, value):
        parts = split3(value)
        for swap in range(2):
            begin = pl.multiple_of(slot * 2 * lines + lines * (core ^ swap), lines)
            for target, part in zip((high, middle, low), parts):
                target[pl.ds(begin, lines), :] = part[swap * lines : (swap + 1) * lines]

    for slot in range(4):
        place(slot, panels[slot][...])
    if not first:
        each_far(step, steps, panels[4:], place)

    @pl.when(step == 0)
    def _():
        even[...] = jnp.zeros_like(even)
        skew[...] = jnp.zeros_like(skew)
        proj[...] = jnp.zeros_like(proj)

    one, two, three = high[start_row:, :], middle[start_row:, :], low[start_row:, :]
    skew[...] += nt(one, two) + nt(one, three)
    if first:
        even[...] += nt(one, one) + nt(two, two)
    else:
        even[half:, :] += nt(one, one) + nt(two, two)
        one_a, two_a, three_a = high[:half, :], middle[:half, :], low[:half, :]
        even[:half, :] += (
            (nt(one_a, three) + nt(three_a, one) + nt(two_a, two))
            + (nt(one_a, two) + nt(two_a, one))
            + nt(one_a, one)
        )
    current = jnp.concatenate([own_ref[...], other_ref[...]], axis=1)
    x_one, x_two, x_three = split3(current)
    proj[...] += (
        (nn(one, x_three) + nn(three, x_one) + nn(two, x_two))
        + (nn(one, x_two) + nn(two, x_one))
        + nn(one, x_one)
    )

    @pl.when(step == steps - 1)
    def _():
        def corner(i, j):
            at_i, at_j = slice(i * WIDE, (i + 1) * WIDE), slice(j * WIDE, (j + 1) * WIDE)
            base = even.shape[0] - half
            return (
                even[base + i * WIDE : base + (i + 1) * WIDE, at_j]
                + skew[at_i, at_j]
                + skew[at_j, at_i].T
            )

        if first:
            out_ref[0, 0:half, :] = proj[:, :WIDE]
            out_ref[1, 0:half, :] = proj[:, WIDE:]
            for at, (i, j) in enumerate(((0, 0), (0, 1), (1, 1))):
                begin = half + at * WIDE
                out_ref[0, begin : begin + WIDE, :] = corner(i, j)
                out_ref[1, begin : begin + WIDE, :] = jnp.zeros((WIDE, WIDE), F32)
        else:
            keep_ref[0:half, :] = before_ref[0, 0:half, :]
            send_ref[0:half, :] = before_ref[1, 0:half, :]
            keep_ref[half : 2 * half, :] = proj[:, :WIDE]
            send_ref[half : 2 * half, :] = proj[:, WIDE:]

            def blocks(part, target):
                for at, (i, j) in enumerate(PIECES[part]):
                    begin = 2 * half + at * WIDE
                    if j < 2:
                        index = half + ((0, 0), (0, 1), (1, 1)).index((i, j)) * WIDE
                        block = before_ref[0, index : index + WIDE, :]
                    elif i < 2:
                        block = even[i * WIDE : (i + 1) * WIDE, (j - 2) * WIDE : (j - 1) * WIDE]
                    else:
                        block = corner(i - 2, j - 2)
                    target[begin : begin + WIDE, :] = block

            @pl.when(core == 0)
            def _():
                blocks(0, keep_ref)
                blocks(1, send_ref)

            @pl.when(core != 0)
            def _():
                blocks(1, keep_ref)
                blocks(0, send_ref)


def solve_kernel(where_ref, mine_ref, other_ref, own_ref, partner_ref, both, rows_done, ordered, sides):
    core = where_ref[CHIPS]
    both[core] = mine_ref[...]
    both[1 - core] = other_ref[...]
    count = 4
    size = count * WIDE
    panel = size // 2
    base = 16

    def relative(i, j):
        for part in range(2):
            if (i, j) in PIECES[part]:
                start = size + PIECES[part].index((i, j)) * WIDE
                return both[part, start : start + WIDE, :]

    group = size // (2 * CORES * CHIPS)

    def target(index):
        slot, at_core, part = index // (2 * CORES), (index // 2) % CORES, index % 2
        start = part * panel + where_ref[slot] * CORES * group + at_core * group
        return pl.ds(pl.multiple_of(start, group), group)

    for i in range(count):
        strip = jnp.concatenate(
            [relative(i, j) if i <= j else relative(j, i).T for j in range(count)], axis=1
        )
        for k in range(WIDE // group):
            rows_done[target(i * (WIDE // group) + k), :] = strip[k * group : (k + 1) * group]
    for i in range(count):
        strip = jnp.concatenate(
            [
                rows_done[j * WIDE : (j + 1) * WIDE, i * WIDE : (i + 1) * WIDE].T
                for j in range(count)
            ],
            axis=1,
        )
        for k in range(WIDE // group):
            ordered[target(i * (WIDE // group) + k), :] = strip[k * group : (k + 1) * group]
    for index in range(size // group):
        at = slice(index * group, (index + 1) * group)
        sides[target(index), :] = jnp.concatenate([mine_ref[at, :], other_ref[at, :]], axis=1)

    def block(i, j):
        return ordered[i * WIDE : (i + 1) * WIDE, j * WIDE : (j + 1) * WIDE]

    row = lax.broadcasted_iota(jnp.int32, (WIDE, WIDE), 0)
    column = lax.broadcasted_iota(jnp.int32, (WIDE, WIDE), 1)
    same = (row // base) == (column // base)
    diagonals = []
    for i in range(count):
        value = block(i, i)
        diagonals.append(
            jnp.where(row < column, value, jnp.where(row == column, value * 0.5, 0.0))
        )
    lane = lax.broadcasted_iota(jnp.int32, (base, WIDE), 1) % base
    ones = jnp.where(same, 1.0, 0.0).astype(F32)
    spread = []
    for i in range(count):
        flipped = jnp.where(same, diagonals[i], 0.0).T
        folded = flipped[0:base]
        for k in range(1, WIDE // base):
            folded = folded + flipped[k * base : (k + 1) * base]
        stacked = jnp.concatenate([jnp.where(lane == k, folded, 0.0) for k in range(base)], axis=0)
        spread.append(full(stacked, ones))
    wide_lane = lax.broadcasted_iota(jnp.int32, (1, size), 1) % base
    wide_row = lax.broadcasted_iota(jnp.int32, (base, size), 0)
    solved = jnp.zeros((base, size), F32)
    for i in range(base - 1, -1, -1):
        factor = jnp.concatenate([s[i * base : (i + 1) * base] for s in spread], axis=1)
        total = jnp.sum(factor * solved, axis=0, keepdims=True)
        line = (jnp.where(wide_lane == i, 1.0, 0.0) - total) / factor[i : i + 1]
        solved = jnp.where(wide_row == i, line, solved)

    big_row = lax.broadcasted_iota(jnp.int32, (panel, panel), 0)
    big_column = lax.broadcasted_iota(jnp.int32, (panel, panel), 1)
    inverses = []
    for half in range(2):
        left, right = 2 * half, 2 * half + 1
        top = jnp.concatenate([diagonals[left], block(left, right)], axis=1)
        bottom = jnp.concatenate([jnp.zeros((WIDE, WIDE), F32), diagonals[right]], axis=1)
        factor = jnp.concatenate([top, bottom], axis=0)
        lines = solved[:, half * panel : (half + 1) * panel]
        tiled = jnp.concatenate([lines] * (panel // base), axis=0)
        inverse = jnp.where((big_row // base) == (big_column // base), tiled, 0.0)
        width = base
        while width < panel:
            picked = (
                ((big_row // width) % 2 == 0) & (big_column // width == big_row // width + 1)
            )
            coupling = jnp.where(picked, factor, 0.0)
            inverse = inverse - full(full(inverse, coupling), inverse)
            width *= 2
        inverses.append(inverse)
    corner = jnp.concatenate(
        [
            jnp.concatenate([block(0, 2), block(0, 3)], axis=1),
            jnp.concatenate([block(1, 2), block(1, 3)], axis=1),
        ],
        axis=0,
    )
    right_side = sides[...]
    second = full(inverses[1], right_side[panel:])
    first = full(inverses[0], right_side[:panel] - full(corner, second))
    own_ref[0:panel, :] = first[:, :WIDE]
    own_ref[panel:, :] = second[:, :WIDE]
    partner_ref[0:panel, :] = first[:, WIDE:]
    partner_ref[panel:, :] = second[:, WIDE:]


def apply_kernel(where_ref, *refs):
    step = pl.program_id(0)
    steps = pl.num_programs(0)
    panels = refs[:9]
    current_own, current_other, solved_own, solved_other, out_own, out_other, high, middle, low, merged = refs[9:]
    core = where_ref[CHIPS]
    panel = solved_own.shape[0] // 2
    chunk = panels[0].shape[0]
    group = chunk // 4

    @pl.when(step == 0)
    def _():
        for index in range(2 * CHIPS):
            chip = where_ref[index // 2]
            for part in range(2):
                start = pl.multiple_of(
                    part * panel + chip * 2 * group + group * (core ^ (index % 2)), group
                )
                lines = jnp.concatenate(
                    [solved_own[pl.ds(start, group), :], solved_other[pl.ds(start, group), :]],
                    axis=1,
                )
                at = (2 * index + part) * group
                for target, value in zip((high, middle, low), split3(lines)):
                    target[at : at + group, :] = value

    def place(slot, value):
        merged[slot * chunk : (slot + 1) * chunk, :] = value

    for slot in range(4):
        place(slot, panels[slot][...])
    each_far(step, steps, panels[4:], place)
    one, two, three = split3(merged[...])
    first, second, third = high[...], middle[...], low[...]

    def tn(left, right):
        return lax.dot_general(left, right, (((0,), (0,)), ((), ())), preferred_element_type=F32)

    change = (
        (tn(one, third) + tn(three, first) + tn(two, second))
        + (tn(one, second) + tn(two, first))
        + tn(one, first)
    )
    out_own[...] = current_own[...] - change[:, :WIDE]
    out_other[...] = current_other[...] - change[:, WIDE:]


def per_device(vectors, panel_one, panel_two):
    rows, columns = vectors.shape
    group = panel_one.shape[1]
    half = rows // 2
    size = 2 * group * CHIPS * CORES
    quarter = half // 2
    chunk = 4 * group
    steps = half // TILE
    at = lax.axis_index("col")
    core, depth, plane = at % CORES, (at // CORES) % DEPTH, at // (CORES * DEPTH)

    def permute(value, move):
        pairs = []
        for source in range(CHIPS * CORES):
            k, z, x = source % CORES, (source // CORES) % DEPTH, source // (CORES * DEPTH)
            k, z, x = move(k, z, x)
            pairs.append((source, (x * DEPTH + z % DEPTH) * CORES + k))
        return lax.ppermute(value, "col", pairs)

    def core_swap(value):
        return permute(value, lambda k, z, x: (1 - k, z, x))

    def up(value):
        return permute(value, lambda k, z, x: (k, z + 1, x))

    def down(value):
        return permute(value, lambda k, z, x: (k, z - 1, x))

    def across(value):
        return permute(value, lambda k, z, x: (k, z, 1 - x))

    def half_of(which):
        picked = [lax.dynamic_slice_in_dim(v.T, which * half, half, 1) for v in (panel_one, panel_two)]
        return jnp.concatenate(picked, axis=0)

    a_own = half_of(core)
    b_own = core_swap(half_of(1 - core))
    own = jnp.concatenate([a_own, b_own], axis=0)
    given = lax.dynamic_slice_in_dim(vectors, (1 - core) * half, half, 0)
    other = core_swap(given)

    away, below, above = across(own), up(own), down(own)
    near = (own, below, above, away)
    sent_up = up(jnp.concatenate([below[:, :quarter], away[:, :quarter]], axis=0))
    sent_down = down(jnp.concatenate([above[:, quarter:], away[:, :quarter]], axis=0))
    sent_across = across(jnp.concatenate([below[:, quarter:], above[:, quarter:]], axis=0))
    chips = []
    for x_step, z_step in ((0, 0), (0, -1), (0, 1), (1, 0), (0, 2), (1, -1), (1, 1), (1, 2)):
        chips.append(jnp.bitwise_xor(plane, x_step) * DEPTH + (depth + z_step) % DEPTH)
    where = jnp.stack(chips + [core]).astype(jnp.int32)

    turn = steps // 2
    whole = [pl.BlockSpec((chunk, TILE), lambda j, w: (0, j))] * 4

    def early(lines):
        return pl.BlockSpec((lines, TILE), lambda j, w: (0, jnp.minimum(j, turn - 1)))

    def late(lines):
        return pl.BlockSpec((lines, TILE), lambda j, w: (0, jnp.maximum(j - turn, 0)))

    both = pl.BlockSpec(
        (chunk, TILE), lambda j, w: (jnp.where(j < turn, 1, 0), jnp.where(j < turn, j, j - turn))
    )
    parts_far = [early(2 * chunk), both, late(2 * chunk), early(chunk), late(chunk)]
    own_spec = pl.BlockSpec((TILE, columns), lambda j, w: (w[CHIPS] * steps + j, 0))
    other_spec = pl.BlockSpec((TILE, columns), lambda j, w: (j, 0))
    length = size + 5 * WIDE
    span = size // 2

    def gram(first, pieces, extra):
        if first:
            shapes = [jax.ShapeDtypeStruct((2, span + 3 * WIDE, WIDE), F32)]
        else:
            shapes = [jax.ShapeDtypeStruct((length, WIDE), F32)] * 2
        height = span if first else size
        units = 10 if first else 16
        return pl.pallas_call(
            functools.partial(gram_kernel, first=first),
            out_shape=shapes,
            grid_spec=pltpu.PrefetchScalarGridSpec(
                num_scalar_prefetch=1,
                grid=(steps,),
                in_specs=whole
                + ([] if first else parts_far)
                + [own_spec, other_spec]
                + [pl.BlockSpec(v.shape, lambda j, w: (0, 0, 0)) for v in extra],
                out_specs=[
                    pl.BlockSpec(v.shape, lambda j, w, n=len(v.shape): (0,) * n) for v in shapes
                ],
                scratch_shapes=[pltpu.VMEM((height, TILE), BF16)] * 3
                + [
                    pltpu.VMEM((height, span), F32),
                    pltpu.VMEM((span, span), F32),
                    pltpu.VMEM((span, 2 * WIDE), F32),
                ],
            ),
            compiler_params=pltpu.CompilerParams(
                dimension_semantics=("arbitrary",), vmem_limit_bytes=LIMIT
            ),
            cost_estimate=pl.CostEstimate(
                flops=2 * 6 * units * span * span * half,
                bytes_accessed=4 * half * (height + columns * 2),
                transcendentals=0,
            ),
            name="gram_near" if first else "gram_far",
        )(where, *pieces, vectors, other, *extra)

    (before,) = gram(True, near, ())
    before, sent_up, sent_down = lax.optimization_barrier((before, sent_up, sent_down))
    end_up = up(sent_up[chunk:])
    end_across = across(sent_down[:chunk])
    far = (sent_up, sent_down, sent_across, end_up, end_across)
    kept, sent = gram(False, near + far, (before,))
    mine = kept + core_swap(sent)
    members = lax.axis_size("row")
    parts = lax.all_to_all(mine.reshape(members, length // members, WIDE), "row", 0, 0)
    total = jnp.sum(parts, axis=0)
    spread = jnp.broadcast_to(total[None], (members,) + total.shape)
    mine = lax.all_to_all(spread, "row", 0, 0).reshape(length, WIDE)
    theirs = core_swap(mine)

    solved_own, solved_other = pl.pallas_call(
        solve_kernel,
        out_shape=[jax.ShapeDtypeStruct((size, WIDE), F32)] * 2,
        grid_spec=pltpu.PrefetchScalarGridSpec(
            num_scalar_prefetch=1,
            grid=(1,),
            in_specs=[pl.BlockSpec((length, WIDE), lambda j, w: (0, 0))] * 2,
            out_specs=[pl.BlockSpec((size, WIDE), lambda j, w: (0, 0))] * 2,
            scratch_shapes=[pltpu.VMEM((2, length, WIDE), F32)]
            + [pltpu.VMEM((size, size), F32)] * 2
            + [pltpu.VMEM((size, 2 * WIDE), F32)],
        ),
        compiler_params=pltpu.CompilerParams(vmem_limit_bytes=32 << 20),
        name="solve",
    )(where, mine, theirs)

    result_own, result_other = pl.pallas_call(
        apply_kernel,
        out_shape=[jax.ShapeDtypeStruct((half, columns), F32)] * 2,
        grid_spec=pltpu.PrefetchScalarGridSpec(
            num_scalar_prefetch=1,
            grid=(steps,),
            in_specs=whole
            + parts_far
            + [own_spec, other_spec]
            + [pl.BlockSpec((size, WIDE), lambda j, w: (0, 0))] * 2,
            out_specs=[pl.BlockSpec((TILE, columns), lambda j, w: (j, 0))] * 2,
            scratch_shapes=[pltpu.VMEM((size, 2 * WIDE), BF16)] * 3
            + [pltpu.VMEM((size, TILE), F32)],
        ),
        compiler_params=pltpu.CompilerParams(
            dimension_semantics=("arbitrary",), vmem_limit_bytes=LIMIT
        ),
        name="apply",
    )(where, *near, *far, vectors, other, solved_own, solved_other)

    returned = core_swap(result_other)
    result = jnp.zeros((rows, columns), F32)
    result = lax.dynamic_update_slice_in_dim(result, result_own, core * half, 0)
    return lax.dynamic_update_slice_in_dim(result, returned, (1 - core) * half, 0)


def solution(mesh):
    specs = (P("row", "col"), P("row", "col"), P("row", "col"))
    return jax.shard_map(
        per_device, mesh=mesh, in_specs=specs, out_specs=P("row", "col"), check_vma=False
    )
```

```python
import functools

import jax
import jax.numpy as jnp
from jax import lax
from jax.experimental import pallas as pl
from jax.experimental.pallas import tpu as pltpu
from jax.sharding import PartitionSpec as P

F32 = jnp.float32
BF16 = jnp.bfloat16
HIGHEST = lax.Precision.HIGHEST
PLANES, DEPTH, CORES = 2, 4, 2
CHIPS = PLANES * DEPTH
WIDE = 128
TILE = 512
LIMIT = 24 << 20
PIECES = ((0, 0), (0, 1), (1, 1), (0, 2), (0, 3)), ((1, 2), (1, 3), (2, 2), (2, 3), (3, 3))


def split2(value):
    high = value.astype(BF16)
    return high, (value - high.astype(F32)).astype(BF16)


def nn(left, right):
    return lax.dot_general(left, right, (((1,), (0,)), ((), ())), preferred_element_type=F32)


def nt(left, right):
    return lax.dot_general(left, right, (((1,), (1,)), ((), ())), preferred_element_type=F32)


def full(left, right):
    return lax.dot_general(
        left, right, (((1,), (0,)), ((), ())), precision=HIGHEST, preferred_element_type=F32
    )


def each_far(step, steps, refs, place):
    up_ref, down_ref, across_ref, end_up_ref, end_across_ref = refs
    chunk = down_ref.shape[0]
    early = step < steps // 2

    @pl.when(early)
    def _():
        place(4, up_ref[:chunk])
        place(5, up_ref[chunk:])
        place(6, down_ref[...])
        place(7, end_up_ref[...])

    @pl.when(jnp.logical_not(early))
    def _():
        place(4, down_ref[...])
        place(5, across_ref[:chunk])
        place(6, across_ref[chunk:])
        place(7, end_across_ref[...])


def gram_kernel(where_ref, *refs, first):
    steps = pl.num_programs(0)
    step = pl.program_id(0)
    count = 4 if first else 9
    panels, rest = refs[:count], refs[count:]
    if first:
        own_ref, other_ref, out_ref, high, low, even, skew, proj = rest
    else:
        own_ref, other_ref, before_ref, keep_ref, send_ref, high, low, even, skew, proj = rest
    core = where_ref[CHIPS]
    lines = panels[0].shape[0] // 2
    half = even.shape[1]
    start_row = high.shape[0] - half

    def place(slot, value):
        parts = split2(value)
        for swap in range(2):
            begin = pl.multiple_of(slot * 2 * lines + lines * (core ^ swap), lines)
            for target, part in zip((high, low), parts):
                target[pl.ds(begin, lines), :] = part[swap * lines : (swap + 1) * lines]

    for slot in range(4):
        place(slot, panels[slot][...])
    if not first:
        each_far(step, steps, panels[4:], place)

    @pl.when(step == 0)
    def _():
        even[...] = jnp.zeros_like(even)
        skew[...] = jnp.zeros_like(skew)
        proj[...] = jnp.zeros_like(proj)

    one, two = high[start_row:, :], low[start_row:, :]
    skew[...] += nt(one, two)
    if first:
        even[...] += nt(one, one)
    else:
        even[half:, :] += nt(one, one)
        one_a, two_a = high[:half, :], low[:half, :]
        even[:half, :] += (nt(one_a, two) + nt(two_a, one)) + nt(one_a, one)
    x_one, x_two = split2(jnp.concatenate([own_ref[...], other_ref[...]], axis=1))
    proj[...] += (nn(one, x_two) + nn(two, x_one)) + nn(one, x_one)

    @pl.when(step == steps - 1)
    def _():
        def corner(i, j):
            at_i, at_j = slice(i * WIDE, (i + 1) * WIDE), slice(j * WIDE, (j + 1) * WIDE)
            base = even.shape[0] - half
            return (
                even[base + i * WIDE : base + (i + 1) * WIDE, at_j]
                + skew[at_i, at_j]
                + skew[at_j, at_i].T
            )

        if first:
            out_ref[0, 0:half, :] = proj[:, :WIDE]
            out_ref[1, 0:half, :] = proj[:, WIDE:]
            for at, (i, j) in enumerate(((0, 0), (0, 1), (1, 1))):
                begin = half + at * WIDE
                out_ref[0, begin : begin + WIDE, :] = corner(i, j)
                out_ref[1, begin : begin + WIDE, :] = jnp.zeros((WIDE, WIDE), F32)
        else:
            keep_ref[0:half, :] = before_ref[0, 0:half, :]
            send_ref[0:half, :] = before_ref[1, 0:half, :]
            keep_ref[half : 2 * half, :] = proj[:, :WIDE]
            send_ref[half : 2 * half, :] = proj[:, WIDE:]

            def blocks(part, target):
                for at, (i, j) in enumerate(PIECES[part]):
                    begin = 2 * half + at * WIDE
                    if j < 2:
                        index = half + ((0, 0), (0, 1), (1, 1)).index((i, j)) * WIDE
                        block = before_ref[0, index : index + WIDE, :]
                    elif i < 2:
                        block = even[i * WIDE : (i + 1) * WIDE, (j - 2) * WIDE : (j - 1) * WIDE]
                    else:
                        block = corner(i - 2, j - 2)
                    target[begin : begin + WIDE, :] = block

            @pl.when(core == 0)
            def _():
                blocks(0, keep_ref)
                blocks(1, send_ref)

            @pl.when(core != 0)
            def _():
                blocks(1, keep_ref)
                blocks(0, send_ref)


def solve(where_ref, mine_ref, other_ref, solved_ref, both, rows_done, ordered, sides):
    core = where_ref[CHIPS]
    both[core] = mine_ref[...]
    both[1 - core] = other_ref[...]
    count = 4
    size = count * WIDE
    panel = size // 2
    base = 16

    def relative(i, j):
        for part in range(2):
            if (i, j) in PIECES[part]:
                start = size + PIECES[part].index((i, j)) * WIDE
                return both[part, start : start + WIDE, :]

    group = size // (2 * CORES * CHIPS)

    def target(index):
        slot, at_core, part = index // (2 * CORES), (index // 2) % CORES, index % 2
        start = part * panel + where_ref[slot] * CORES * group + at_core * group
        return pl.ds(pl.multiple_of(start, group), group)

    for i in range(count):
        strip = jnp.concatenate(
            [relative(i, j) if i <= j else relative(j, i).T for j in range(count)], axis=1
        )
        for k in range(WIDE // group):
            rows_done[target(i * (WIDE // group) + k), :] = strip[k * group : (k + 1) * group]
    for i in range(count):
        strip = jnp.concatenate(
            [
                rows_done[j * WIDE : (j + 1) * WIDE, i * WIDE : (i + 1) * WIDE].T
                for j in range(count)
            ],
            axis=1,
        )
        for k in range(WIDE // group):
            ordered[target(i * (WIDE // group) + k), :] = strip[k * group : (k + 1) * group]
    for index in range(size // group):
        at = slice(index * group, (index + 1) * group)
        sides[target(index), :] = jnp.concatenate([mine_ref[at, :], other_ref[at, :]], axis=1)

    def block(i, j):
        return ordered[i * WIDE : (i + 1) * WIDE, j * WIDE : (j + 1) * WIDE]

    row = lax.broadcasted_iota(jnp.int32, (WIDE, WIDE), 0)
    column = lax.broadcasted_iota(jnp.int32, (WIDE, WIDE), 1)
    same = (row // base) == (column // base)
    diagonals = []
    for i in range(count):
        value = block(i, i)
        diagonals.append(
            jnp.where(row < column, value, jnp.where(row == column, value * 0.5, 0.0))
        )
    lane = lax.broadcasted_iota(jnp.int32, (base, WIDE), 1) % base
    ones = jnp.where(same, 1.0, 0.0).astype(F32)
    spread = []
    for i in range(count):
        flipped = jnp.where(same, diagonals[i], 0.0).T
        folded = flipped[0:base]
        for k in range(1, WIDE // base):
            folded = folded + flipped[k * base : (k + 1) * base]
        stacked = jnp.concatenate([jnp.where(lane == k, folded, 0.0) for k in range(base)], axis=0)
        spread.append(full(stacked, ones))
    wide_lane = lax.broadcasted_iota(jnp.int32, (1, size), 1) % base
    wide_row = lax.broadcasted_iota(jnp.int32, (base, size), 0)
    solved = jnp.zeros((base, size), F32)
    for i in range(base - 1, -1, -1):
        factor = jnp.concatenate([s[i * base : (i + 1) * base] for s in spread], axis=1)
        total = jnp.sum(factor * solved, axis=0, keepdims=True)
        line = (jnp.where(wide_lane == i, 1.0, 0.0) - total) / factor[i : i + 1]
        solved = jnp.where(wide_row == i, line, solved)

    big_row = lax.broadcasted_iota(jnp.int32, (panel, panel), 0)
    big_column = lax.broadcasted_iota(jnp.int32, (panel, panel), 1)
    inverses = []
    for half in range(2):
        left, right = 2 * half, 2 * half + 1
        top = jnp.concatenate([diagonals[left], block(left, right)], axis=1)
        bottom = jnp.concatenate([jnp.zeros((WIDE, WIDE), F32), diagonals[right]], axis=1)
        factor = jnp.concatenate([top, bottom], axis=0)
        lines = solved[:, half * panel : (half + 1) * panel]
        tiled = jnp.concatenate([lines] * (panel // base), axis=0)
        inverse = jnp.where((big_row // base) == (big_column // base), tiled, 0.0)
        width = base
        while width < panel:
            picked = (
                ((big_row // width) % 2 == 0) & (big_column // width == big_row // width + 1)
            )
            coupling = jnp.where(picked, factor, 0.0)
            inverse = inverse - full(full(inverse, coupling), inverse)
            width *= 2
        inverses.append(inverse)
    corner = jnp.concatenate(
        [
            jnp.concatenate([block(0, 2), block(0, 3)], axis=1),
            jnp.concatenate([block(1, 2), block(1, 3)], axis=1),
        ],
        axis=0,
    )
    right_side = sides[...]
    second = full(inverses[1], right_side[panel:])
    first = full(inverses[0], right_side[:panel] - full(corner, second))
    solved_ref[0:panel, :] = first
    solved_ref[panel:, :] = second


def apply_kernel(where_ref, *refs):
    step = pl.program_id(0)
    steps = pl.num_programs(0)
    panels = refs[:9]
    current_own, current_other, mine_ref, theirs_ref, out_own, out_other = refs[9:15]
    solved, high, low, merged, both, rows_done, ordered, sides = refs[15:]
    core = where_ref[CHIPS]
    panel = solved.shape[0] // 2
    chunk = panels[0].shape[0]
    group = chunk // 4

    @pl.when(step == 0)
    def _():
        solve(where_ref, mine_ref, theirs_ref, solved, both, rows_done, ordered, sides)
        for index in range(2 * CHIPS):
            chip = where_ref[index // 2]
            for part in range(2):
                start = pl.multiple_of(
                    part * panel + chip * 2 * group + group * (core ^ (index % 2)), group
                )
                at = (2 * index + part) * group
                for target, value in zip((high, low), split2(solved[pl.ds(start, group), :])):
                    target[at : at + group, :] = value

    def place(slot, value):
        merged[slot * chunk : (slot + 1) * chunk, :] = value

    for slot in range(4):
        place(slot, panels[slot][...])
    each_far(step, steps, panels[4:], place)
    one, two = split2(merged[...])
    first, second = high[...], low[...]

    def tn(left, right):
        return lax.dot_general(left, right, (((0,), (0,)), ((), ())), preferred_element_type=F32)

    change = (tn(one, second) + tn(two, first)) + tn(one, first)
    out_own[...] = current_own[...] - change[:, :WIDE]
    out_other[...] = current_other[...] - change[:, WIDE:]


def per_device(vectors, panel_one, panel_two):
    rows, columns = vectors.shape
    group = panel_one.shape[1]
    half = rows // 2
    size = 2 * group * CHIPS * CORES
    quarter = half // 2
    chunk = 4 * group
    steps = half // TILE
    at = lax.axis_index("col")
    core, depth, plane = at % CORES, (at // CORES) % DEPTH, at // (CORES * DEPTH)

    def permute(value, move):
        pairs = []
        for source in range(CHIPS * CORES):
            k, z, x = source % CORES, (source // CORES) % DEPTH, source // (CORES * DEPTH)
            k, z, x = move(k, z, x)
            pairs.append((source, (x * DEPTH + z % DEPTH) * CORES + k))
        return lax.ppermute(value, "col", pairs)

    def core_swap(value):
        return permute(value, lambda k, z, x: (1 - k, z, x))

    def up(value):
        return permute(value, lambda k, z, x: (k, z + 1, x))

    def down(value):
        return permute(value, lambda k, z, x: (k, z - 1, x))

    def across(value):
        return permute(value, lambda k, z, x: (k, z, 1 - x))

    def half_of(which):
        picked = [lax.dynamic_slice_in_dim(v.T, which * half, half, 1) for v in (panel_one, panel_two)]
        return jnp.concatenate(picked, axis=0)

    a_own = half_of(core)
    b_own = core_swap(half_of(1 - core))
    own = jnp.concatenate([a_own, b_own], axis=0)
    away, below, above = across(own), up(own), down(own)
    near = (own, below, above, away)
    to_up = jnp.concatenate([below[:, :quarter], away[:, :quarter]], axis=0)
    to_down = jnp.concatenate([above[:, quarter:], away[:, :quarter]], axis=0)
    to_across = jnp.concatenate([below[:, quarter:], above[:, quarter:]], axis=0)
    sent_up, sent_down, sent_across = up(to_up), down(to_down), across(to_across)
    other = core_swap(vectors)

    chips = []
    for x_step, z_step in ((0, 0), (0, -1), (0, 1), (1, 0), (0, 2), (1, -1), (1, 1), (1, 2)):
        chips.append(jnp.bitwise_xor(plane, x_step) * DEPTH + (depth + z_step) % DEPTH)
    where = jnp.stack(chips + [core]).astype(jnp.int32)

    turn = steps // 2
    whole = [pl.BlockSpec((chunk, TILE), lambda j, w: (0, j))] * 4

    def early(lines):
        return pl.BlockSpec((lines, TILE), lambda j, w: (0, jnp.minimum(j, turn - 1)))

    def late(lines):
        return pl.BlockSpec((lines, TILE), lambda j, w: (0, jnp.maximum(j - turn, 0)))

    both = pl.BlockSpec(
        (chunk, TILE), lambda j, w: (jnp.where(j < turn, 1, 0), jnp.where(j < turn, j, j - turn))
    )
    parts_far = [early(2 * chunk), both, late(2 * chunk), early(chunk), late(chunk)]
    own_spec = pl.BlockSpec((TILE, columns), lambda j, w: (w[CHIPS] * steps + j, 0))
    length = size + 5 * WIDE
    span = size // 2

    def gram(first, pieces, extra):
        if first:
            shapes = [jax.ShapeDtypeStruct((2, span + 3 * WIDE, WIDE), F32)]
        else:
            shapes = [jax.ShapeDtypeStruct((length, WIDE), F32)] * 2
        height = span if first else size
        units = 10 if first else 16
        return pl.pallas_call(
            functools.partial(gram_kernel, first=first),
            out_shape=shapes,
            grid_spec=pltpu.PrefetchScalarGridSpec(
                num_scalar_prefetch=1,
                grid=(steps,),
                in_specs=whole
                + ([] if first else parts_far)
                + [own_spec, own_spec]
                + [pl.BlockSpec(v.shape, lambda j, w: (0, 0, 0)) for v in extra],
                out_specs=[
                    pl.BlockSpec(v.shape, lambda j, w, n=len(v.shape): (0,) * n) for v in shapes
                ],
                scratch_shapes=[pltpu.VMEM((height, TILE), BF16)] * 2
                + [
                    pltpu.VMEM((height, span), F32),
                    pltpu.VMEM((span, span), F32),
                    pltpu.VMEM((span, 2 * WIDE), F32),
                ],
            ),
            compiler_params=pltpu.CompilerParams(
                dimension_semantics=("arbitrary",), vmem_limit_bytes=LIMIT
            ),
            cost_estimate=pl.CostEstimate(
                flops=2 * 3 * units * span * span * half,
                bytes_accessed=4 * half * (height + columns * 2),
                transcendentals=0,
            ),
            name="gram_near" if first else "gram_far",
        )(where, *pieces, vectors, other, *extra)

    (before,) = gram(True, near, ())
    before, sent_up, sent_down = lax.optimization_barrier((before, sent_up, sent_down))
    end_up = up(sent_up[chunk:])
    end_across = across(sent_down[:chunk])
    far = (sent_up, sent_down, sent_across, end_up, end_across)
    kept, sent = gram(False, near + far, (before,))
    mine = kept + core_swap(sent)
    members = lax.axis_size("row")
    parts = lax.all_to_all(mine.reshape(members, length // members, WIDE), "row", 0, 0)
    total = jnp.sum(parts, axis=0)
    spread = jnp.broadcast_to(total[None], (members,) + total.shape)
    mine = lax.all_to_all(spread, "row", 0, 0).reshape(length, WIDE)
    theirs = core_swap(mine)

    result_own, result_other = pl.pallas_call(
        apply_kernel,
        out_shape=[jax.ShapeDtypeStruct((half, columns), F32)] * 2,
        grid_spec=pltpu.PrefetchScalarGridSpec(
            num_scalar_prefetch=1,
            grid=(steps,),
            in_specs=whole
            + parts_far
            + [own_spec, own_spec]
            + [pl.BlockSpec((length, WIDE), lambda j, w: (0, 0))] * 2,
            out_specs=[pl.BlockSpec((TILE, columns), lambda j, w: (j, 0))] * 2,
            scratch_shapes=[pltpu.VMEM((size, 2 * WIDE), F32)]
            + [pltpu.VMEM((size, 2 * WIDE), BF16)] * 2
            + [pltpu.VMEM((size, TILE), F32), pltpu.VMEM((2, length, WIDE), F32)]
            + [pltpu.VMEM((size, size), F32)] * 2
            + [pltpu.VMEM((size, 2 * WIDE), F32)],
        ),
        compiler_params=pltpu.CompilerParams(
            dimension_semantics=("arbitrary",), vmem_limit_bytes=58 << 20
        ),
        name="solve_apply",
    )(where, *near, *far, vectors, other, mine, theirs)

    returned = core_swap(result_other)
    result = jnp.zeros((rows, columns), F32)
    result = lax.dynamic_update_slice_in_dim(result, result_own, core * half, 0)
    return lax.dynamic_update_slice_in_dim(result, returned, (1 - core) * half, 0)


def solution(mesh):
    specs = (P("row", "col"), P("row", "col"), P("row", "col"))
    return jax.shard_map(
        per_device, mesh=mesh, in_specs=specs, out_specs=P("row", "col"), check_vma=False
    )
```

```python
import functools

import jax
import jax.numpy as jnp
from jax import lax
from jax.experimental import pallas as pl
from jax.experimental.pallas import tpu as pltpu
from jax.sharding import PartitionSpec as P

F32 = jnp.float32
BF16 = jnp.bfloat16
HIGHEST = lax.Precision.HIGHEST
PLANES, DEPTH, CORES = 2, 4, 2
CHIPS = PLANES * DEPTH
WIDE = 128
TILE = 1024
LIMIT = 24 << 20
PIECES = ((0, 0), (0, 1), (1, 1), (0, 2), (0, 3)), ((1, 2), (1, 3), (2, 2), (2, 3), (3, 3))


def split2(value):
    high = value.astype(BF16)
    return high, (value - high.astype(F32)).astype(BF16)


def nn(left, right):
    return lax.dot_general(left, right, (((1,), (0,)), ((), ())), preferred_element_type=F32)


def nt(left, right):
    return lax.dot_general(left, right, (((1,), (1,)), ((), ())), preferred_element_type=F32)


def full(left, right):
    return lax.dot_general(
        left, right, (((1,), (0,)), ((), ())), precision=HIGHEST, preferred_element_type=F32
    )


def each_far(step, steps, refs, place):
    up_ref, down_ref, across_ref, end_up_ref, end_across_ref = refs
    chunk = down_ref.shape[0]
    early = step < steps // 2

    @pl.when(early)
    def _():
        place(4, up_ref[:chunk])
        place(5, up_ref[chunk:])
        place(6, down_ref[...])
        place(7, end_up_ref[...])

    @pl.when(jnp.logical_not(early))
    def _():
        place(4, down_ref[...])
        place(5, across_ref[:chunk])
        place(6, across_ref[chunk:])
        place(7, end_across_ref[...])


def gram_kernel(where_ref, *refs, first):
    steps = pl.num_programs(0)
    step = pl.program_id(0)
    count = 4 if first else 9
    panels, rest = refs[:count], refs[count:]
    if first:
        own_ref, other_ref, out_ref, high, low, even, skew, proj = rest
    else:
        own_ref, other_ref, before_ref, keep_ref, send_ref, high, low, even, skew, proj = rest
    core = where_ref[CHIPS]
    lines = panels[0].shape[0] // 2
    half = even.shape[1]
    start_row = high.shape[0] - half

    def place(slot, value):
        parts = split2(value)
        for swap in range(2):
            begin = pl.multiple_of(slot * 2 * lines + lines * (core ^ swap), lines)
            for target, part in zip((high, low), parts):
                target[pl.ds(begin, lines), :] = part[swap * lines : (swap + 1) * lines]

    for slot in range(4):
        place(slot, panels[slot][...])
    if not first:
        each_far(step, steps, panels[4:], place)

    @pl.when(step == 0)
    def _():
        even[...] = jnp.zeros_like(even)
        skew[...] = jnp.zeros_like(skew)
        proj[...] = jnp.zeros_like(proj)

    one, two = high[start_row:, :], low[start_row:, :]
    skew[...] += nt(one, two)
    if first:
        even[...] += nt(one, one)
    else:
        even[half:, :] += nt(one, one)
        one_a, two_a = high[:half, :], low[:half, :]
        even[:half, :] += (nt(one_a, two) + nt(two_a, one)) + nt(one_a, one)
    x_one, x_two = split2(jnp.concatenate([own_ref[...], other_ref[...]], axis=1))
    proj[...] += (nn(one, x_two) + nn(two, x_one)) + nn(one, x_one)

    @pl.when(step == steps - 1)
    def _():
        def corner(i, j):
            at_i, at_j = slice(i * WIDE, (i + 1) * WIDE), slice(j * WIDE, (j + 1) * WIDE)
            base = even.shape[0] - half
            return (
                even[base + i * WIDE : base + (i + 1) * WIDE, at_j]
                + skew[at_i, at_j]
                + skew[at_j, at_i].T
            )

        if first:
            out_ref[0, 0:half, :] = proj[:, :WIDE]
            out_ref[1, 0:half, :] = proj[:, WIDE:]
            for at, (i, j) in enumerate(((0, 0), (0, 1), (1, 1))):
                begin = half + at * WIDE
                out_ref[0, begin : begin + WIDE, :] = corner(i, j)
                out_ref[1, begin : begin + WIDE, :] = jnp.zeros((WIDE, WIDE), F32)
        else:
            keep_ref[0:half, :] = before_ref[0, 0:half, :]
            send_ref[0:half, :] = before_ref[1, 0:half, :]
            keep_ref[half : 2 * half, :] = proj[:, :WIDE]
            send_ref[half : 2 * half, :] = proj[:, WIDE:]

            def blocks(part, target):
                for at, (i, j) in enumerate(PIECES[part]):
                    begin = 2 * half + at * WIDE
                    if j < 2:
                        index = half + ((0, 0), (0, 1), (1, 1)).index((i, j)) * WIDE
                        block = before_ref[0, index : index + WIDE, :]
                    elif i < 2:
                        block = even[i * WIDE : (i + 1) * WIDE, (j - 2) * WIDE : (j - 1) * WIDE]
                    else:
                        block = corner(i - 2, j - 2)
                    target[begin : begin + WIDE, :] = block

            @pl.when(core == 0)
            def _():
                blocks(0, keep_ref)
                blocks(1, send_ref)

            @pl.when(core != 0)
            def _():
                blocks(1, keep_ref)
                blocks(0, send_ref)


def solve(where_ref, mine_ref, other_ref, solved_ref, both, rows_done, ordered, sides):
    core = where_ref[CHIPS]
    both[core] = mine_ref[...]
    both[1 - core] = other_ref[...]
    count = 4
    size = count * WIDE
    panel = size // 2
    base = 16

    def relative(i, j):
        for part in range(2):
            if (i, j) in PIECES[part]:
                start = size + PIECES[part].index((i, j)) * WIDE
                return both[part, start : start + WIDE, :]

    group = size // (2 * CORES * CHIPS)

    def target(index):
        slot, at_core, part = index // (2 * CORES), (index // 2) % CORES, index % 2
        start = part * panel + where_ref[slot] * CORES * group + at_core * group
        return pl.ds(pl.multiple_of(start, group), group)

    for i in range(count):
        strip = jnp.concatenate(
            [relative(i, j) if i <= j else relative(j, i).T for j in range(count)], axis=1
        )
        for k in range(WIDE // group):
            rows_done[target(i * (WIDE // group) + k), :] = strip[k * group : (k + 1) * group]
    for i in range(count):
        strip = jnp.concatenate(
            [
                rows_done[j * WIDE : (j + 1) * WIDE, i * WIDE : (i + 1) * WIDE].T
                for j in range(count)
            ],
            axis=1,
        )
        for k in range(WIDE // group):
            ordered[target(i * (WIDE // group) + k), :] = strip[k * group : (k + 1) * group]
    for index in range(size // group):
        at = slice(index * group, (index + 1) * group)
        sides[target(index), :] = jnp.concatenate([mine_ref[at, :], other_ref[at, :]], axis=1)

    def block(i, j):
        return ordered[i * WIDE : (i + 1) * WIDE, j * WIDE : (j + 1) * WIDE]

    row = lax.broadcasted_iota(jnp.int32, (WIDE, WIDE), 0)
    column = lax.broadcasted_iota(jnp.int32, (WIDE, WIDE), 1)
    same = (row // base) == (column // base)
    diagonals = []
    for i in range(count):
        value = block(i, i)
        diagonals.append(
            jnp.where(row < column, value, jnp.where(row == column, value * 0.5, 0.0))
        )
    lane = lax.broadcasted_iota(jnp.int32, (base, WIDE), 1) % base
    ones = jnp.where(same, 1.0, 0.0).astype(F32)
    spread = []
    for i in range(count):
        flipped = jnp.where(same, diagonals[i], 0.0).T
        folded = flipped[0:base]
        for k in range(1, WIDE // base):
            folded = folded + flipped[k * base : (k + 1) * base]
        stacked = jnp.concatenate([jnp.where(lane == k, folded, 0.0) for k in range(base)], axis=0)
        spread.append(full(stacked, ones))
    wide_lane = lax.broadcasted_iota(jnp.int32, (1, size), 1) % base
    wide_row = lax.broadcasted_iota(jnp.int32, (base, size), 0)
    solved = jnp.zeros((base, size), F32)
    for i in range(base - 1, -1, -1):
        factor = jnp.concatenate([s[i * base : (i + 1) * base] for s in spread], axis=1)
        total = jnp.sum(factor * solved, axis=0, keepdims=True)
        line = (jnp.where(wide_lane == i, 1.0, 0.0) - total) / factor[i : i + 1]
        solved = jnp.where(wide_row == i, line, solved)

    def three(left, right):
        return (nn(left[0], right[1]) + nn(left[1], right[0])) + nn(left[0], right[0])

    small = []
    for i in range(count):
        tiled = jnp.concatenate([solved[:, i * WIDE : (i + 1) * WIDE]] * (WIDE // base), axis=0)
        small.append(jnp.where(same, tiled, 0.0))
    width = base
    while width < WIDE:
        picked = ((row // width) % 2 == 0) & (column // width == row // width + 1)
        for i in range(count):
            inverse = split2(small[i])
            coupling = split2(jnp.where(picked, diagonals[i], 0.0))
            small[i] = small[i] - three(split2(three(inverse, coupling)), inverse)
        width *= 2
    inverses = []
    for half in range(2):
        left, right = small[2 * half], small[2 * half + 1]
        coupling = split2(block(2 * half, 2 * half + 1))
        corner = -three(split2(three(split2(left), coupling)), split2(right))
        top = jnp.concatenate([left, corner], axis=1)
        bottom = jnp.concatenate([jnp.zeros((WIDE, WIDE), F32), right], axis=1)
        inverses.append(split2(jnp.concatenate([top, bottom], axis=0)))
    corner = jnp.concatenate(
        [
            jnp.concatenate([block(0, 2), block(0, 3)], axis=1),
            jnp.concatenate([block(1, 2), block(1, 3)], axis=1),
        ],
        axis=0,
    )
    right_side = sides[...]
    second = three(inverses[1], split2(right_side[panel:]))
    first = three(
        inverses[0], split2(right_side[:panel] - three(split2(corner), split2(second)))
    )
    solved_ref[0:panel, :] = first
    solved_ref[panel:, :] = second


def apply_kernel(where_ref, *refs):
    step = pl.program_id(0)
    steps = pl.num_programs(0)
    panels = refs[:9]
    current_own, current_other, mine_ref, theirs_ref, out_own, out_other = refs[9:15]
    solved, high, low, merged, both, rows_done, ordered, sides = refs[15:]
    core = where_ref[CHIPS]
    panel = solved.shape[0] // 2
    chunk = panels[0].shape[0]
    group = chunk // 4

    @pl.when(step == 0)
    def _():
        solve(where_ref, mine_ref, theirs_ref, solved, both, rows_done, ordered, sides)
        for index in range(2 * CHIPS):
            chip = where_ref[index // 2]
            for part in range(2):
                start = pl.multiple_of(
                    part * panel + chip * 2 * group + group * (core ^ (index % 2)), group
                )
                at = (2 * index + part) * group
                for target, value in zip((high, low), split2(solved[pl.ds(start, group), :])):
                    target[at : at + group, :] = value

    def place(slot, value):
        merged[slot * chunk : (slot + 1) * chunk, :] = value

    for slot in range(4):
        place(slot, panels[slot][...])
    each_far(step, steps, panels[4:], place)
    one, two = split2(merged[...])
    first, second = high[...], low[...]

    def tn(left, right):
        return lax.dot_general(left, right, (((0,), (0,)), ((), ())), preferred_element_type=F32)

    change = (tn(one, second) + tn(two, first)) + tn(one, first)
    out_own[...] = current_own[...] - change[:, :WIDE]
    out_other[...] = current_other[...] - change[:, WIDE:]


def per_device(vectors, panel_one, panel_two):
    rows, columns = vectors.shape
    group = panel_one.shape[1]
    half = rows // 2
    size = 2 * group * CHIPS * CORES
    quarter = half // 2
    chunk = 4 * group
    steps = half // TILE
    at = lax.axis_index("col")
    core, depth, plane = at % CORES, (at // CORES) % DEPTH, at // (CORES * DEPTH)

    def permute(value, move):
        pairs = []
        for source in range(CHIPS * CORES):
            k, z, x = source % CORES, (source // CORES) % DEPTH, source // (CORES * DEPTH)
            k, z, x = move(k, z, x)
            pairs.append((source, (x * DEPTH + z % DEPTH) * CORES + k))
        return lax.ppermute(value, "col", pairs)

    def core_swap(value):
        return permute(value, lambda k, z, x: (1 - k, z, x))

    def up(value):
        return permute(value, lambda k, z, x: (k, z + 1, x))

    def down(value):
        return permute(value, lambda k, z, x: (k, z - 1, x))

    def across(value):
        return permute(value, lambda k, z, x: (k, z, 1 - x))

    def half_of(which):
        picked = [lax.dynamic_slice_in_dim(v.T, which * half, half, 1) for v in (panel_one, panel_two)]
        return jnp.concatenate(picked, axis=0)

    a_own = half_of(core)
    b_own = core_swap(half_of(1 - core))
    own = jnp.concatenate([a_own, b_own], axis=0)
    away, below, above = across(own), up(own), down(own)
    near = (own, below, above, away)
    to_up = jnp.concatenate([below[:, :quarter], away[:, :quarter]], axis=0)
    to_down = jnp.concatenate([above[:, quarter:], away[:, :quarter]], axis=0)
    to_across = jnp.concatenate([below[:, quarter:], above[:, quarter:]], axis=0)
    sent_up, sent_down, sent_across = up(to_up), down(to_down), across(to_across)
    vectors_late, _ = lax.optimization_barrier((vectors, own))
    other = core_swap(vectors_late)

    chips = []
    for x_step, z_step in ((0, 0), (0, -1), (0, 1), (1, 0), (0, 2), (1, -1), (1, 1), (1, 2)):
        chips.append(jnp.bitwise_xor(plane, x_step) * DEPTH + (depth + z_step) % DEPTH)
    where = jnp.stack(chips + [core]).astype(jnp.int32)

    turn = steps // 2
    whole = [pl.BlockSpec((chunk, TILE), lambda j, w: (0, j))] * 4

    def early(lines):
        return pl.BlockSpec((lines, TILE), lambda j, w: (0, jnp.minimum(j, turn - 1)))

    def late(lines):
        return pl.BlockSpec((lines, TILE), lambda j, w: (0, jnp.maximum(j - turn, 0)))

    both = pl.BlockSpec(
        (chunk, TILE), lambda j, w: (jnp.where(j < turn, 1, 0), jnp.where(j < turn, j, j - turn))
    )
    parts_far = [early(2 * chunk), both, late(2 * chunk), early(chunk), late(chunk)]
    own_spec = pl.BlockSpec((TILE, columns), lambda j, w: (w[CHIPS] * steps + j, 0))
    length = size + 5 * WIDE
    span = size // 2

    def gram(first, pieces, extra):
        if first:
            shapes = [jax.ShapeDtypeStruct((2, span + 3 * WIDE, WIDE), F32)]
        else:
            shapes = [jax.ShapeDtypeStruct((length, WIDE), F32)] * 2
        height = span if first else size
        units = 10 if first else 16
        return pl.pallas_call(
            functools.partial(gram_kernel, first=first),
            out_shape=shapes,
            grid_spec=pltpu.PrefetchScalarGridSpec(
                num_scalar_prefetch=1,
                grid=(steps,),
                in_specs=whole
                + ([] if first else parts_far)
                + [own_spec, own_spec]
                + [pl.BlockSpec(v.shape, lambda j, w: (0, 0, 0)) for v in extra],
                out_specs=[
                    pl.BlockSpec(v.shape, lambda j, w, n=len(v.shape): (0,) * n) for v in shapes
                ],
                scratch_shapes=[pltpu.VMEM((height, TILE), BF16)] * 2
                + [
                    pltpu.VMEM((height, span), F32),
                    pltpu.VMEM((span, span), F32),
                    pltpu.VMEM((span, 2 * WIDE), F32),
                ],
            ),
            compiler_params=pltpu.CompilerParams(
                dimension_semantics=("arbitrary",), vmem_limit_bytes=LIMIT
            ),
            cost_estimate=pl.CostEstimate(
                flops=2 * 3 * units * span * span * half,
                bytes_accessed=4 * half * (height + columns * 2),
                transcendentals=0,
            ),
            name="gram_near" if first else "gram_far",
        )(where, *pieces, vectors, other, *extra)

    (before,) = gram(True, near, ())
    before, sent_up, sent_down = lax.optimization_barrier((before, sent_up, sent_down))
    end_up = up(sent_up[chunk:])
    end_across = across(sent_down[:chunk])
    far = (sent_up, sent_down, sent_across, end_up, end_across)
    kept, sent = gram(False, near + far, (before,))
    mine = kept + core_swap(sent)
    members = lax.axis_size("row")
    parts = lax.all_to_all(mine.reshape(members, length // members, WIDE), "row", 0, 0)
    total = jnp.sum(parts, axis=0)
    spread = jnp.broadcast_to(total[None], (members,) + total.shape)
    mine = lax.all_to_all(spread, "row", 0, 0).reshape(length, WIDE)
    theirs = core_swap(mine)

    far_held = [pltpu.with_memory_space_constraint(v, pltpu.HBM) for v in far]
    result_own, result_other = pl.pallas_call(
        apply_kernel,
        out_shape=[jax.ShapeDtypeStruct((half, columns), F32)] * 2,
        grid_spec=pltpu.PrefetchScalarGridSpec(
            num_scalar_prefetch=1,
            grid=(steps,),
            in_specs=whole
            + parts_far
            + [own_spec, own_spec]
            + [pl.BlockSpec((length, WIDE), lambda j, w: (0, 0))] * 2,
            out_specs=[pl.BlockSpec((TILE, columns), lambda j, w: (j, 0))] * 2,
            scratch_shapes=[pltpu.VMEM((size, 2 * WIDE), F32)]
            + [pltpu.VMEM((size, 2 * WIDE), BF16)] * 2
            + [pltpu.VMEM((size, TILE), F32), pltpu.VMEM((2, length, WIDE), F32)]
            + [pltpu.VMEM((size, size), F32)] * 2
            + [pltpu.VMEM((size, 2 * WIDE), F32)],
        ),
        compiler_params=pltpu.CompilerParams(
            dimension_semantics=("arbitrary",), vmem_limit_bytes=LIMIT
        ),
        name="solve_apply",
    )(where, *near, *far_held, vectors, other, mine, theirs)

    returned = core_swap(result_other)
    result = jnp.zeros((rows, columns), F32)
    result = lax.dynamic_update_slice_in_dim(result, result_own, core * half, 0)
    return lax.dynamic_update_slice_in_dim(result, returned, (1 - core) * half, 0)


def solution(mesh):
    specs = (P("row", "col"), P("row", "col"), P("row", "col"))
    return jax.shard_map(
        per_device, mesh=mesh, in_specs=specs, out_specs=P("row", "col"), check_vma=False
    )
```

```python
import functools

import jax
import jax.numpy as jnp
from jax import lax
from jax.experimental import pallas as pl
from jax.experimental.pallas import tpu as pltpu
from jax.sharding import PartitionSpec as P

F32 = jnp.float32
BF16 = jnp.bfloat16
HIGHEST = lax.Precision.HIGHEST
PLANES, DEPTH, CORES = 2, 4, 2
CHIPS = PLANES * DEPTH
WIDE = 128
TILE = 1024
LIMIT = 24 << 20
PIECES = ((0, 0), (0, 1), (1, 1), (0, 2), (0, 3)), ((1, 2), (1, 3), (2, 2), (2, 3), (3, 3))


def split2(value):
    high = value.astype(BF16)
    return high, (value - high.astype(F32)).astype(BF16)


def nn(left, right):
    return lax.dot_general(left, right, (((1,), (0,)), ((), ())), preferred_element_type=F32)


def nt(left, right):
    return lax.dot_general(left, right, (((1,), (1,)), ((), ())), preferred_element_type=F32)


def full(left, right):
    return lax.dot_general(
        left, right, (((1,), (0,)), ((), ())), precision=HIGHEST, preferred_element_type=F32
    )


def each_far(step, steps, refs, place):
    up_ref, down_ref, across_ref, end_up_ref, end_across_ref = refs
    chunk = down_ref.shape[0]
    early = step < steps // 2

    @pl.when(early)
    def _():
        place(4, up_ref[:chunk])
        place(5, up_ref[chunk:])
        place(6, down_ref[...])
        place(7, end_up_ref[...])

    @pl.when(jnp.logical_not(early))
    def _():
        place(4, down_ref[...])
        place(5, across_ref[:chunk])
        place(6, across_ref[chunk:])
        place(7, end_across_ref[...])


def gram_kernel(where_ref, *refs, first):
    steps = pl.num_programs(0)
    step = pl.program_id(0)
    count = 8 if first else 13
    panels, rest = refs[:count], refs[count:]
    if first:
        own_ref, other_ref, out_ref, high, low, even, skew, proj = rest
    else:
        own_ref, other_ref, before_ref, keep_ref, send_ref, high, low, even, skew, proj = rest
    core = where_ref[CHIPS]
    lines = panels[0].shape[0]
    half = even.shape[1]
    start_row = high.shape[0] - half

    def place_half(slot, swap, value):
        begin = pl.multiple_of(slot * 2 * lines + lines * (core ^ swap), lines)
        for target, part in zip((high, low), split2(value)):
            target[pl.ds(begin, lines), :] = part

    def place(slot, value):
        place_half(slot, 0, value[:lines])
        place_half(slot, 1, value[lines:])

    for index in range(8):
        place_half(index // 2, index % 2, panels[index][...])
    if not first:
        each_far(step, steps, panels[8:], place)

    @pl.when(step == 0)
    def _():
        even[...] = jnp.zeros_like(even)
        skew[...] = jnp.zeros_like(skew)
        proj[...] = jnp.zeros_like(proj)

    one, two = high[start_row:, :], low[start_row:, :]
    skew[...] += nt(one, two)
    if first:
        even[...] += nt(one, one)
    else:
        even[half:, :] += nt(one, one)
        one_a, two_a = high[:half, :], low[:half, :]
        even[:half, :] += (nt(one_a, two) + nt(two_a, one)) + nt(one_a, one)
    x_one, x_two = split2(jnp.concatenate([own_ref[...], other_ref[...]], axis=1))
    proj[...] += (nn(one, x_two) + nn(two, x_one)) + nn(one, x_one)

    @pl.when(step == steps - 1)
    def _():
        def corner(i, j):
            at_i, at_j = slice(i * WIDE, (i + 1) * WIDE), slice(j * WIDE, (j + 1) * WIDE)
            base = even.shape[0] - half
            return (
                even[base + i * WIDE : base + (i + 1) * WIDE, at_j]
                + skew[at_i, at_j]
                + skew[at_j, at_i].T
            )

        if first:
            out_ref[0, 0:half, :] = proj[:, :WIDE]
            out_ref[1, 0:half, :] = proj[:, WIDE:]
            for at, (i, j) in enumerate(((0, 0), (0, 1), (1, 1))):
                begin = half + at * WIDE
                out_ref[0, begin : begin + WIDE, :] = corner(i, j)
                out_ref[1, begin : begin + WIDE, :] = jnp.zeros((WIDE, WIDE), F32)
        else:
            keep_ref[0:half, :] = before_ref[0, 0:half, :]
            send_ref[0:half, :] = before_ref[1, 0:half, :]
            keep_ref[half : 2 * half, :] = proj[:, :WIDE]
            send_ref[half : 2 * half, :] = proj[:, WIDE:]

            def blocks(part, target):
                for at, (i, j) in enumerate(PIECES[part]):
                    begin = 2 * half + at * WIDE
                    if j < 2:
                        index = half + ((0, 0), (0, 1), (1, 1)).index((i, j)) * WIDE
                        block = before_ref[0, index : index + WIDE, :]
                    elif i < 2:
                        block = even[i * WIDE : (i + 1) * WIDE, (j - 2) * WIDE : (j - 1) * WIDE]
                    else:
                        block = corner(i - 2, j - 2)
                    target[begin : begin + WIDE, :] = block

            @pl.when(core == 0)
            def _():
                blocks(0, keep_ref)
                blocks(1, send_ref)

            @pl.when(core != 0)
            def _():
                blocks(1, keep_ref)
                blocks(0, send_ref)


def solve(where_ref, mine_ref, other_ref, solved_ref, both, rows_done, ordered, sides):
    core = where_ref[CHIPS]
    both[core] = mine_ref[...]
    both[1 - core] = other_ref[...]
    count = 4
    size = count * WIDE
    panel = size // 2
    base = 16

    def relative(i, j):
        for part in range(2):
            if (i, j) in PIECES[part]:
                start = size + PIECES[part].index((i, j)) * WIDE
                return both[part, start : start + WIDE, :]

    group = size // (2 * CORES * CHIPS)

    def target(index):
        slot, at_core, part = index // (2 * CORES), (index // 2) % CORES, index % 2
        start = part * panel + where_ref[slot] * CORES * group + at_core * group
        return pl.ds(pl.multiple_of(start, group), group)

    for i in range(count):
        strip = jnp.concatenate(
            [relative(i, j) if i <= j else relative(j, i).T for j in range(count)], axis=1
        )
        for k in range(WIDE // group):
            rows_done[target(i * (WIDE // group) + k), :] = strip[k * group : (k + 1) * group]
    for i in range(count):
        strip = jnp.concatenate(
            [
                rows_done[j * WIDE : (j + 1) * WIDE, i * WIDE : (i + 1) * WIDE].T
                for j in range(count)
            ],
            axis=1,
        )
        for k in range(WIDE // group):
            ordered[target(i * (WIDE // group) + k), :] = strip[k * group : (k + 1) * group]
    for index in range(size // group):
        at = slice(index * group, (index + 1) * group)
        sides[target(index), :] = jnp.concatenate([mine_ref[at, :], other_ref[at, :]], axis=1)

    def block(i, j):
        return ordered[i * WIDE : (i + 1) * WIDE, j * WIDE : (j + 1) * WIDE]

    row = lax.broadcasted_iota(jnp.int32, (WIDE, WIDE), 0)
    column = lax.broadcasted_iota(jnp.int32, (WIDE, WIDE), 1)
    same = (row // base) == (column // base)
    diagonals = []
    for i in range(count):
        value = block(i, i)
        diagonals.append(
            jnp.where(row < column, value, jnp.where(row == column, value * 0.5, 0.0))
        )
    lane = lax.broadcasted_iota(jnp.int32, (base, WIDE), 1) % base
    ones = jnp.where(same, 1.0, 0.0).astype(F32)
    spread = []
    for i in range(count):
        flipped = jnp.where(same, diagonals[i], 0.0).T
        folded = flipped[0:base]
        for k in range(1, WIDE // base):
            folded = folded + flipped[k * base : (k + 1) * base]
        stacked = jnp.concatenate([jnp.where(lane == k, folded, 0.0) for k in range(base)], axis=0)
        spread.append(full(stacked, ones))
    wide_lane = lax.broadcasted_iota(jnp.int32, (1, size), 1) % base
    wide_row = lax.broadcasted_iota(jnp.int32, (base, size), 0)
    solved = jnp.zeros((base, size), F32)
    for i in range(base - 1, -1, -1):
        factor = jnp.concatenate([s[i * base : (i + 1) * base] for s in spread], axis=1)
        total = jnp.sum(factor * solved, axis=0, keepdims=True)
        line = (jnp.where(wide_lane == i, 1.0, 0.0) - total) / factor[i : i + 1]
        solved = jnp.where(wide_row == i, line, solved)

    def three(left, right):
        return (nn(left[0], right[1]) + nn(left[1], right[0])) + nn(left[0], right[0])

    small = []
    for i in range(count):
        tiled = jnp.concatenate([solved[:, i * WIDE : (i + 1) * WIDE]] * (WIDE // base), axis=0)
        small.append(jnp.where(same, tiled, 0.0))
    width = base
    while width < WIDE:
        picked = ((row // width) % 2 == 0) & (column // width == row // width + 1)
        for i in range(count):
            inverse = split2(small[i])
            coupling = split2(jnp.where(picked, diagonals[i], 0.0))
            small[i] = small[i] - three(split2(three(inverse, coupling)), inverse)
        width *= 2
    inverses = []
    for half in range(2):
        left, right = small[2 * half], small[2 * half + 1]
        coupling = split2(block(2 * half, 2 * half + 1))
        corner = -three(split2(three(split2(left), coupling)), split2(right))
        top = jnp.concatenate([left, corner], axis=1)
        bottom = jnp.concatenate([jnp.zeros((WIDE, WIDE), F32), right], axis=1)
        inverses.append(split2(jnp.concatenate([top, bottom], axis=0)))
    corner = jnp.concatenate(
        [
            jnp.concatenate([block(0, 2), block(0, 3)], axis=1),
            jnp.concatenate([block(1, 2), block(1, 3)], axis=1),
        ],
        axis=0,
    )
    right_side = sides[...]
    second = three(inverses[1], split2(right_side[panel:]))
    first = three(
        inverses[0], split2(right_side[:panel] - three(split2(corner), split2(second)))
    )
    solved_ref[0:panel, :] = first
    solved_ref[panel:, :] = second


def apply_kernel(where_ref, *refs):
    step = pl.program_id(0)
    steps = pl.num_programs(0)
    panels = refs[:13]
    current_own, current_other, mine_ref, theirs_ref, out_own, out_other = refs[13:19]
    solved, high, low, merged, both, rows_done, ordered, sides = refs[19:]
    core = where_ref[CHIPS]
    panel = solved.shape[0] // 2
    chunk = 2 * panels[0].shape[0]
    group = chunk // 4

    @pl.when(step == 0)
    def _():
        solve(where_ref, mine_ref, theirs_ref, solved, both, rows_done, ordered, sides)
        for index in range(2 * CHIPS):
            chip = where_ref[index // 2]
            for part in range(2):
                start = pl.multiple_of(
                    part * panel + chip * 2 * group + group * (core ^ (index % 2)), group
                )
                at = (2 * index + part) * group
                for target, value in zip((high, low), split2(solved[pl.ds(start, group), :])):
                    target[at : at + group, :] = value

    def place(slot, value):
        merged[slot * chunk : (slot + 1) * chunk, :] = value

    for index in range(8):
        merged[index * chunk // 2 : (index + 1) * chunk // 2, :] = panels[index][...]
    each_far(step, steps, panels[8:], place)
    one, two = split2(merged[...])
    first, second = high[...], low[...]

    def tn(left, right):
        return lax.dot_general(left, right, (((0,), (0,)), ((), ())), preferred_element_type=F32)

    change = (tn(one, second) + tn(two, first)) + tn(one, first)
    out_own[...] = current_own[...] - change[:, :WIDE]
    out_other[...] = current_other[...] - change[:, WIDE:]


def per_device(vectors, panel_one, panel_two):
    rows, columns = vectors.shape
    group = panel_one.shape[1]
    half = rows // 2
    size = 2 * group * CHIPS * CORES
    quarter = half // 2
    chunk = 4 * group
    steps = half // TILE
    at = lax.axis_index("col")
    core, depth, plane = at % CORES, (at // CORES) % DEPTH, at // (CORES * DEPTH)

    def permute(value, move):
        pairs = []
        for source in range(CHIPS * CORES):
            k, z, x = source % CORES, (source // CORES) % DEPTH, source // (CORES * DEPTH)
            k, z, x = move(k, z, x)
            pairs.append((source, (x * DEPTH + z % DEPTH) * CORES + k))
        return lax.ppermute(value, "col", pairs)

    def core_swap(value):
        return permute(value, lambda k, z, x: (1 - k, z, x))

    def up(value):
        return permute(value, lambda k, z, x: (k, z + 1, x))

    def down(value):
        return permute(value, lambda k, z, x: (k, z - 1, x))

    def across(value):
        return permute(value, lambda k, z, x: (k, z, 1 - x))

    def half_of(which):
        picked = [lax.dynamic_slice_in_dim(v.T, which * half, half, 1) for v in (panel_one, panel_two)]
        return jnp.concatenate(picked, axis=0)

    a_own = half_of(core)
    b_own = core_swap(half_of(1 - core))
    own = jnp.concatenate([a_own, b_own], axis=0)
    a_away, a_below, a_above = across(a_own), up(a_own), down(a_own)
    b_away, b_below, b_above = across(b_own), up(b_own), down(b_own)
    near = (a_own, b_own, a_below, b_below, a_above, b_above, a_away, b_away)

    def early_half(*values):
        return [v[:, :quarter] for v in values]

    def late_half(*values):
        return [v[:, quarter:] for v in values]

    to_up = jnp.concatenate(early_half(a_below, b_below, a_away, b_away), axis=0)
    to_down = jnp.concatenate(
        late_half(a_above, b_above) + early_half(a_away, b_away), axis=0
    )
    to_across = jnp.concatenate(late_half(a_below, b_below, a_above, b_above), axis=0)
    sent_up, sent_down, sent_across = up(to_up), down(to_down), across(to_across)
    vectors_late, _ = lax.optimization_barrier((vectors, to_up))
    other = core_swap(vectors_late)

    chips = []
    for x_step, z_step in ((0, 0), (0, -1), (0, 1), (1, 0), (0, 2), (1, -1), (1, 1), (1, 2)):
        chips.append(jnp.bitwise_xor(plane, x_step) * DEPTH + (depth + z_step) % DEPTH)
    where = jnp.stack(chips + [core]).astype(jnp.int32)

    turn = steps // 2
    whole = [pl.BlockSpec((chunk // 2, TILE), lambda j, w: (0, j))] * 8

    def early(lines):
        return pl.BlockSpec((lines, TILE), lambda j, w: (0, jnp.minimum(j, turn - 1)))

    def late(lines):
        return pl.BlockSpec((lines, TILE), lambda j, w: (0, jnp.maximum(j - turn, 0)))

    both = pl.BlockSpec(
        (chunk, TILE), lambda j, w: (jnp.where(j < turn, 1, 0), jnp.where(j < turn, j, j - turn))
    )
    parts_far = [early(2 * chunk), both, late(2 * chunk), early(chunk), late(chunk)]
    own_spec = pl.BlockSpec((TILE, columns), lambda j, w: (w[CHIPS] * steps + j, 0))
    length = size + 5 * WIDE
    span = size // 2

    def gram(first, pieces, extra):
        if first:
            shapes = [jax.ShapeDtypeStruct((2, span + 3 * WIDE, WIDE), F32)]
        else:
            shapes = [jax.ShapeDtypeStruct((length, WIDE), F32)] * 2
        height = span if first else size
        units = 10 if first else 16
        return pl.pallas_call(
            functools.partial(gram_kernel, first=first),
            out_shape=shapes,
            grid_spec=pltpu.PrefetchScalarGridSpec(
                num_scalar_prefetch=1,
                grid=(steps,),
                in_specs=whole
                + ([] if first else parts_far)
                + [own_spec, own_spec]
                + [pl.BlockSpec(v.shape, lambda j, w: (0, 0, 0)) for v in extra],
                out_specs=[
                    pl.BlockSpec(v.shape, lambda j, w, n=len(v.shape): (0,) * n) for v in shapes
                ],
                scratch_shapes=[pltpu.VMEM((height, TILE), BF16)] * 2
                + [
                    pltpu.VMEM((height, span), F32),
                    pltpu.VMEM((span, span), F32),
                    pltpu.VMEM((span, 2 * WIDE), F32),
                ],
            ),
            compiler_params=pltpu.CompilerParams(
                dimension_semantics=("arbitrary",), vmem_limit_bytes=LIMIT
            ),
            cost_estimate=pl.CostEstimate(
                flops=2 * 3 * units * span * span * half,
                bytes_accessed=4 * half * (height + columns * 2),
                transcendentals=0,
            ),
            name="gram_near" if first else "gram_far",
        )(where, *pieces, vectors, other, *extra)

    (before,) = gram(True, near, ())
    before, sent_up, sent_down = lax.optimization_barrier((before, sent_up, sent_down))
    end_up = up(sent_up[chunk:])
    end_across = across(sent_down[:chunk])
    far = (sent_up, sent_down, sent_across, end_up, end_across)
    kept, sent = gram(False, near + far, (before,))
    mine = kept + core_swap(sent)
    members = lax.axis_size("row")
    parts = lax.all_to_all(mine.reshape(members, length // members, WIDE), "row", 0, 0)
    total = jnp.sum(parts, axis=0)
    spread = jnp.broadcast_to(total[None], (members,) + total.shape)
    mine = lax.all_to_all(spread, "row", 0, 0).reshape(length, WIDE)
    theirs = core_swap(mine)

    held = [pltpu.with_memory_space_constraint(v, pltpu.HBM) for v in near + far]
    result_own, result_other = pl.pallas_call(
        apply_kernel,
        out_shape=[jax.ShapeDtypeStruct((half, columns), F32)] * 2,
        grid_spec=pltpu.PrefetchScalarGridSpec(
            num_scalar_prefetch=1,
            grid=(steps,),
            in_specs=whole
            + parts_far
            + [own_spec, own_spec]
            + [pl.BlockSpec((length, WIDE), lambda j, w: (0, 0))] * 2,
            out_specs=[pl.BlockSpec((TILE, columns), lambda j, w: (j, 0))] * 2,
            scratch_shapes=[pltpu.VMEM((size, 2 * WIDE), F32)]
            + [pltpu.VMEM((size, 2 * WIDE), BF16)] * 2
            + [pltpu.VMEM((size, TILE), F32), pltpu.VMEM((2, length, WIDE), F32)]
            + [pltpu.VMEM((size, size), F32)] * 2
            + [pltpu.VMEM((size, 2 * WIDE), F32)],
        ),
        compiler_params=pltpu.CompilerParams(
            dimension_semantics=("arbitrary",), vmem_limit_bytes=LIMIT
        ),
        name="solve_apply",
    )(where, *held, vectors, other, mine, theirs)

    returned = core_swap(result_other)
    result = jnp.zeros((rows, columns), F32)
    result = lax.dynamic_update_slice_in_dim(result, result_own, core * half, 0)
    return lax.dynamic_update_slice_in_dim(result, returned, (1 - core) * half, 0)


def solution(mesh):
    specs = (P("row", "col"), P("row", "col"), P("row", "col"))
    return jax.shard_map(
        per_device, mesh=mesh, in_specs=specs, out_specs=P("row", "col"), check_vma=False
    )
```

```python
import functools

import jax
import jax.numpy as jnp
from jax import lax
from jax.experimental import pallas as pl
from jax.experimental.pallas import tpu as pltpu
from jax.sharding import PartitionSpec as P

F32 = jnp.float32
BF16 = jnp.bfloat16
HIGHEST = lax.Precision.HIGHEST
PLANES, DEPTH, CORES = 2, 4, 2
CHIPS = PLANES * DEPTH
WIDE = 128
TILE = 1024
LIMIT = 24 << 20
PIECES = ((0, 0), (0, 1), (1, 1), (0, 2), (0, 3)), ((1, 2), (1, 3), (2, 2), (2, 3), (3, 3))


def split2(value):
    high = value.astype(BF16)
    return high, (value - high.astype(F32)).astype(BF16)


def nn(left, right):
    return lax.dot_general(left, right, (((1,), (0,)), ((), ())), preferred_element_type=F32)


def nt(left, right):
    return lax.dot_general(left, right, (((1,), (1,)), ((), ())), preferred_element_type=F32)


def full(left, right):
    return lax.dot_general(
        left, right, (((1,), (0,)), ((), ())), precision=HIGHEST, preferred_element_type=F32
    )


def each_middle(early, refs, place):
    up_ref, down_ref, across_ref = refs
    chunk = down_ref.shape[0]

    @pl.when(early)
    def _():
        place(4, up_ref[:chunk])
        place(5, up_ref[chunk:])
        place(6, down_ref[...])

    @pl.when(jnp.logical_not(early))
    def _():
        place(4, down_ref[...])
        place(5, across_ref[:chunk])
        place(6, across_ref[chunk:])


def each_last(early, refs, place):
    @pl.when(early)
    def _():
        place(7, refs[0][...])

    @pl.when(jnp.logical_not(early))
    def _():
        place(7, refs[1][...])


def each_far(step, steps, refs, place):
    each_middle(step < steps // 2, refs[:3], place)
    each_last(step < steps // 2, refs[3:], place)


def placer(core, lines, high, low):
    def place_half(slot, swap, value):
        begin = pl.multiple_of(slot * 2 * lines + lines * (core ^ swap), lines)
        for target, part in zip((high, low), split2(value)):
            target[pl.ds(begin, lines), :] = part

    def place(slot, value):
        place_half(slot, 0, value[:lines])
        place_half(slot, 1, value[lines:])

    return place_half, place


def gram_kernel(where_ref, *refs, first):
    steps = pl.num_programs(0)
    step = pl.program_id(0)
    count = 8 if first else 11
    panels = refs[:count]
    own_ref, other_ref, out_ref, high, low, even, skew, proj = refs[count:]
    core = where_ref[CHIPS]
    half = even.shape[1]
    start_row = high.shape[0] - half
    place_half, place = placer(core, panels[0].shape[0], high, low)

    @pl.when(step == 0)
    def _():
        even[...] = jnp.zeros_like(even)
        skew[...] = jnp.zeros_like(skew)
        proj[...] = jnp.zeros_like(proj)
        if not first:
            empty = half // 4
            high[2 * half - empty :, :] = jnp.zeros((empty, high.shape[1]), BF16)
            low[2 * half - empty :, :] = jnp.zeros((empty, low.shape[1]), BF16)

    for index in range(8):
        place_half(index // 2, index % 2, panels[index][...])
    if not first:
        each_middle(step < steps // 2, panels[8:], place)

    one, two = high[start_row:, :], low[start_row:, :]
    skew[...] += nt(one, two)
    if first:
        even[...] += nt(one, one)
    else:
        even[half:, :] += nt(one, one)
        one_a, two_a = high[:half, :], low[:half, :]
        even[:half, :] += (nt(one_a, two) + nt(two_a, one)) + nt(one_a, one)
    x_one, x_two = split2(jnp.concatenate([own_ref[...], other_ref[...]], axis=1))
    proj[...] += (nn(one, x_two) + nn(two, x_one)) + nn(one, x_one)

    @pl.when(step == steps - 1)
    def _():
        out_ref[0:half, :] = proj[...]
        out_ref[half : 2 * half, :] = even[start_row:, :] + (skew[...] + skew[...].T)
        if not first:
            out_ref[2 * half :, :] = even[:half, :]


def last_kernel(where_ref, *refs):
    steps = pl.num_programs(0)
    step = pl.program_id(0)
    panels = refs[:13]
    own_ref, other_ref, near_ref, middle_ref, keep_ref, send_ref, high, low, gram, proj = refs[13:]
    core = where_ref[CHIPS]
    size = gram.shape[1]
    half = size // 2
    chunk = gram.shape[0]
    place_half, place = placer(core, panels[0].shape[0], high, low)
    for index in range(8):
        place_half(index // 2, index % 2, panels[index][...])
    each_far(step, steps, panels[8:], place)

    @pl.when(step == 0)
    def _():
        gram[...] = jnp.zeros_like(gram)
        proj[...] = jnp.zeros_like(proj)

    one, two = high[...], low[...]
    last, rest = one[size - chunk :], two[size - chunk :]
    pair = jnp.concatenate([last, rest], axis=0)
    partial = nt(pair, one)
    gram[...] += nt(last, two) + (partial[chunk:] + partial[:chunk])
    x_one, x_two = split2(jnp.concatenate([own_ref[...], other_ref[...]], axis=1))
    partial = nn(pair, x_one)
    proj[...] += nn(last, x_two) + (partial[chunk:] + partial[:chunk])

    @pl.when(step == steps - 1)
    def _():
        for target, lanes in ((keep_ref, slice(0, WIDE)), (send_ref, slice(WIDE, 2 * WIDE))):
            target[0:half, :] = near_ref[0:half, lanes]
            target[half : size - chunk, :] = middle_ref[0 : half - chunk, lanes]
            target[size - chunk : size, :] = proj[:, lanes]

        def spot(ref, base, i, j):
            return ref[base + i * WIDE : base + (i + 1) * WIDE, j * WIDE : (j + 1) * WIDE]

        def lower(j):
            return jnp.concatenate(
                [jnp.zeros((WIDE - chunk, WIDE), F32), gram[:, j * WIDE : (j + 1) * WIDE]], axis=0
            )

        lane = lax.broadcasted_iota(jnp.int32, (WIDE, WIDE), 1)

        def blocks(part, target):
            for at, (i, j) in enumerate(PIECES[part]):
                begin = size + at * WIDE
                if j < 2:
                    block = spot(near_ref, half, i, j)
                elif i < 2:
                    block = spot(middle_ref, 2 * half, i, j - 2)
                else:
                    block = spot(middle_ref, half, i - 2, j - 2)
                if j == 3:
                    added = lower(i)
                    if i == 3:
                        block = block + added
                        added = jnp.where(lane < WIDE - chunk, added, 0.0)
                    block = block + added.T
                target[begin : begin + WIDE, :] = block

        @pl.when(core == 0)
        def _():
            blocks(0, keep_ref)
            blocks(1, send_ref)

        @pl.when(core != 0)
        def _():
            blocks(1, keep_ref)
            blocks(0, send_ref)


def solve(where_ref, mine_ref, other_ref, solved_ref, both, rows_done, ordered, sides):
    core = where_ref[CHIPS]
    both[core] = mine_ref[...]
    both[1 - core] = other_ref[...]
    count = 4
    size = count * WIDE
    panel = size // 2
    base = 16

    def relative(i, j):
        for part in range(2):
            if (i, j) in PIECES[part]:
                start = size + PIECES[part].index((i, j)) * WIDE
                return both[part, start : start + WIDE, :]

    group = size // (2 * CORES * CHIPS)

    def target(index):
        slot, at_core, part = index // (2 * CORES), (index // 2) % CORES, index % 2
        start = part * panel + where_ref[slot] * CORES * group + at_core * group
        return pl.ds(pl.multiple_of(start, group), group)

    for i in range(count):
        strip = jnp.concatenate(
            [relative(i, j) if i <= j else relative(j, i).T for j in range(count)], axis=1
        )
        for k in range(WIDE // group):
            rows_done[target(i * (WIDE // group) + k), :] = strip[k * group : (k + 1) * group]
    for i in range(count):
        strip = jnp.concatenate(
            [
                rows_done[j * WIDE : (j + 1) * WIDE, i * WIDE : (i + 1) * WIDE].T
                for j in range(count)
            ],
            axis=1,
        )
        for k in range(WIDE // group):
            ordered[target(i * (WIDE // group) + k), :] = strip[k * group : (k + 1) * group]
    for index in range(size // group):
        at = slice(index * group, (index + 1) * group)
        sides[target(index), :] = jnp.concatenate([mine_ref[at, :], other_ref[at, :]], axis=1)

    def block(i, j):
        return ordered[i * WIDE : (i + 1) * WIDE, j * WIDE : (j + 1) * WIDE]

    row = lax.broadcasted_iota(jnp.int32, (WIDE, WIDE), 0)
    column = lax.broadcasted_iota(jnp.int32, (WIDE, WIDE), 1)
    same = (row // base) == (column // base)
    diagonals = []
    for i in range(count):
        value = block(i, i)
        diagonals.append(
            jnp.where(row < column, value, jnp.where(row == column, value * 0.5, 0.0))
        )
    lane = lax.broadcasted_iota(jnp.int32, (base, WIDE), 1) % base
    ones = jnp.where(same, 1.0, 0.0).astype(F32)
    spread = []
    for i in range(count):
        flipped = jnp.where(same, diagonals[i], 0.0).T
        folded = flipped[0:base]
        for k in range(1, WIDE // base):
            folded = folded + flipped[k * base : (k + 1) * base]
        stacked = jnp.concatenate([jnp.where(lane == k, folded, 0.0) for k in range(base)], axis=0)
        spread.append(full(stacked, ones))
    wide_lane = lax.broadcasted_iota(jnp.int32, (1, size), 1) % base
    wide_row = lax.broadcasted_iota(jnp.int32, (base, size), 0)
    solved = jnp.zeros((base, size), F32)
    for i in range(base - 1, -1, -1):
        factor = jnp.concatenate([s[i * base : (i + 1) * base] for s in spread], axis=1)
        total = jnp.sum(factor * solved, axis=0, keepdims=True)
        line = (jnp.where(wide_lane == i, 1.0, 0.0) - total) / factor[i : i + 1]
        solved = jnp.where(wide_row == i, line, solved)

    def three(left, right):
        return (nn(left[0], right[1]) + nn(left[1], right[0])) + nn(left[0], right[0])

    small = []
    for i in range(count):
        tiled = jnp.concatenate([solved[:, i * WIDE : (i + 1) * WIDE]] * (WIDE // base), axis=0)
        small.append(jnp.where(same, tiled, 0.0))
    width = base
    while width < WIDE:
        picked = ((row // width) % 2 == 0) & (column // width == row // width + 1)
        for i in range(count):
            inverse = split2(small[i])
            coupling = split2(jnp.where(picked, diagonals[i], 0.0))
            small[i] = small[i] - three(split2(three(inverse, coupling)), inverse)
        width *= 2
    inverses = []
    for half in range(2):
        left, right = small[2 * half], small[2 * half + 1]
        coupling = split2(block(2 * half, 2 * half + 1))
        corner = -three(split2(three(split2(left), coupling)), split2(right))
        top = jnp.concatenate([left, corner], axis=1)
        bottom = jnp.concatenate([jnp.zeros((WIDE, WIDE), F32), right], axis=1)
        inverses.append(split2(jnp.concatenate([top, bottom], axis=0)))
    corner = jnp.concatenate(
        [
            jnp.concatenate([block(0, 2), block(0, 3)], axis=1),
            jnp.concatenate([block(1, 2), block(1, 3)], axis=1),
        ],
        axis=0,
    )
    right_side = sides[...]
    second = three(inverses[1], split2(right_side[panel:]))
    first = three(
        inverses[0], split2(right_side[:panel] - three(split2(corner), split2(second)))
    )
    solved_ref[0:panel, :] = first
    solved_ref[panel:, :] = second


def apply_kernel(where_ref, *refs):
    step = pl.program_id(0)
    steps = pl.num_programs(0)
    panels = refs[:13]
    current_own, current_other, mine_ref, theirs_ref, out_own, out_other = refs[13:19]
    solved, high, low, merged, both, rows_done, ordered, sides = refs[19:]
    core = where_ref[CHIPS]
    panel = solved.shape[0] // 2
    chunk = 2 * panels[0].shape[0]
    group = chunk // 4

    @pl.when(step == 0)
    def _():
        solve(where_ref, mine_ref, theirs_ref, solved, both, rows_done, ordered, sides)
        for index in range(2 * CHIPS):
            chip = where_ref[index // 2]
            for part in range(2):
                start = pl.multiple_of(
                    part * panel + chip * 2 * group + group * (core ^ (index % 2)), group
                )
                at = (2 * index + part) * group
                for target, value in zip((high, low), split2(solved[pl.ds(start, group), :])):
                    target[at : at + group, :] = value

    def place(slot, value):
        merged[slot * chunk : (slot + 1) * chunk, :] = value

    for index in range(8):
        merged[index * chunk // 2 : (index + 1) * chunk // 2, :] = panels[index][...]
    each_far(step, steps, panels[8:], place)
    one, two = split2(merged[...])
    first, second = high[...], low[...]

    def tn(left, right):
        return lax.dot_general(left, right, (((0,), (0,)), ((), ())), preferred_element_type=F32)

    change = (tn(one, second) + tn(two, first)) + tn(one, first)
    out_own[...] = current_own[...] - change[:, :WIDE]
    out_other[...] = current_other[...] - change[:, WIDE:]


def per_device(vectors, panel_one, panel_two):
    rows, columns = vectors.shape
    group = panel_one.shape[1]
    half = rows // 2
    size = 2 * group * CHIPS * CORES
    quarter = half // 2
    chunk = 4 * group
    steps = half // TILE
    at = lax.axis_index("col")
    core, depth, plane = at % CORES, (at // CORES) % DEPTH, at // (CORES * DEPTH)

    def permute(value, move):
        pairs = []
        for source in range(CHIPS * CORES):
            k, z, x = source % CORES, (source // CORES) % DEPTH, source // (CORES * DEPTH)
            k, z, x = move(k, z, x)
            pairs.append((source, (x * DEPTH + z % DEPTH) * CORES + k))
        return lax.ppermute(value, "col", pairs)

    def core_swap(value):
        return permute(value, lambda k, z, x: (1 - k, z, x))

    def up(value):
        return permute(value, lambda k, z, x: (k, z + 1, x))

    def down(value):
        return permute(value, lambda k, z, x: (k, z - 1, x))

    def across(value):
        return permute(value, lambda k, z, x: (k, z, 1 - x))

    def half_of(which):
        picked = [lax.dynamic_slice_in_dim(v.T, which * half, half, 1) for v in (panel_one, panel_two)]
        return jnp.concatenate(picked, axis=0)

    a_own = half_of(core)
    b_own = core_swap(half_of(1 - core))
    own = jnp.concatenate([a_own, b_own], axis=0)
    a_away, a_below, a_above = across(a_own), up(a_own), down(a_own)
    b_away, b_below, b_above = across(b_own), up(b_own), down(b_own)
    near = (a_own, b_own, a_below, b_below, a_above, b_above, a_away, b_away)

    def early_half(*values):
        return [v[:, :quarter] for v in values]

    def late_half(*values):
        return [v[:, quarter:] for v in values]

    to_up = jnp.concatenate(early_half(a_below, b_below, a_away, b_away), axis=0)
    to_down = jnp.concatenate(
        late_half(a_above, b_above) + early_half(a_away, b_away), axis=0
    )
    to_across = jnp.concatenate(late_half(a_below, b_below, a_above, b_above), axis=0)
    sent_up, sent_down, sent_across = up(to_up), down(to_down), across(to_across)
    vectors_late, _ = lax.optimization_barrier((vectors, to_up))
    other = core_swap(vectors_late)

    chips = []
    for x_step, z_step in ((0, 0), (0, -1), (0, 1), (1, 0), (0, 2), (1, -1), (1, 1), (1, 2)):
        chips.append(jnp.bitwise_xor(plane, x_step) * DEPTH + (depth + z_step) % DEPTH)
    where = jnp.stack(chips + [core]).astype(jnp.int32)

    turn = steps // 2
    whole = [pl.BlockSpec((chunk // 2, TILE), lambda j, w: (0, j))] * 8

    def early(lines):
        return pl.BlockSpec((lines, TILE), lambda j, w: (0, jnp.minimum(j, turn - 1)))

    def late(lines):
        return pl.BlockSpec((lines, TILE), lambda j, w: (0, jnp.maximum(j - turn, 0)))

    both = pl.BlockSpec(
        (chunk, TILE), lambda j, w: (jnp.where(j < turn, 1, 0), jnp.where(j < turn, j, j - turn))
    )
    parts_far = [early(2 * chunk), both, late(2 * chunk), early(chunk), late(chunk)]
    own_spec = pl.BlockSpec((TILE, columns), lambda j, w: (w[CHIPS] * steps + j, 0))
    length = size + 5 * WIDE
    span = size // 2

    def products(kernel, pieces, specs, extra, shapes, scratch, units, name):
        return pl.pallas_call(
            kernel,
            out_shape=[jax.ShapeDtypeStruct(v, F32) for v in shapes],
            grid_spec=pltpu.PrefetchScalarGridSpec(
                num_scalar_prefetch=1,
                grid=(steps,),
                in_specs=specs
                + [own_spec, own_spec]
                + [pl.BlockSpec(v.shape, lambda j, w: (0, 0)) for v in extra],
                out_specs=[pl.BlockSpec(v, lambda j, w: (0, 0)) for v in shapes],
                scratch_shapes=scratch,
            ),
            compiler_params=pltpu.CompilerParams(
                dimension_semantics=("arbitrary",), vmem_limit_bytes=LIMIT
            ),
            cost_estimate=pl.CostEstimate(
                flops=2 * 3 * units * span * span * half,
                bytes_accessed=4 * half * (size + columns * 2),
                transcendentals=0,
            ),
            name=name,
        )(where, *pieces, vectors, other, *extra)

    def split_scratch(height):
        return [pltpu.VMEM((height, TILE), BF16)] * 2

    square = pltpu.VMEM((span, span), F32)
    (before,) = products(
        functools.partial(gram_kernel, first=True), near, whole, (),
        [(2 * span, span)], split_scratch(span) + [square] * 3, 10, "gram_near",
    )
    before, sent_up, sent_down, sent_across = lax.optimization_barrier(
        (before, sent_up, sent_down, sent_across)
    )
    end_up = up(sent_up[chunk:])
    end_across = across(sent_down[:chunk])
    middle = (sent_up, sent_down, sent_across)
    (between,) = products(
        functools.partial(gram_kernel, first=False), near + middle, whole + parts_far[:3], (),
        [(3 * span, span)],
        split_scratch(size) + [pltpu.VMEM((size, span), F32), square, square], 16, "gram_middle",
    )
    end_up, end_across, between = lax.optimization_barrier((end_up, end_across, between))
    far = middle + (end_up, end_across)
    kept, sent = products(
        last_kernel, near + far, whole + parts_far, (before, between),
        [(length, WIDE)] * 2,
        split_scratch(size) + [pltpu.VMEM((chunk, size), F32), pltpu.VMEM((chunk, span), F32)],
        8, "gram_last",
    )
    mine = kept + core_swap(sent)
    members = lax.axis_size("row")
    parts = lax.all_to_all(mine.reshape(members, length // members, WIDE), "row", 0, 0)
    total = jnp.sum(parts, axis=0)
    spread = jnp.broadcast_to(total[None], (members,) + total.shape)
    mine = lax.all_to_all(spread, "row", 0, 0).reshape(length, WIDE)
    theirs = core_swap(mine)

    held = [pltpu.with_memory_space_constraint(v, pltpu.HBM) for v in near + far]
    result_own, result_other = pl.pallas_call(
        apply_kernel,
        out_shape=[jax.ShapeDtypeStruct((half, columns), F32)] * 2,
        grid_spec=pltpu.PrefetchScalarGridSpec(
            num_scalar_prefetch=1,
            grid=(steps,),
            in_specs=whole
            + parts_far
            + [own_spec, own_spec]
            + [pl.BlockSpec((length, WIDE), lambda j, w: (0, 0))] * 2,
            out_specs=[pl.BlockSpec((TILE, columns), lambda j, w: (j, 0))] * 2,
            scratch_shapes=[pltpu.VMEM((size, 2 * WIDE), F32)]
            + [pltpu.VMEM((size, 2 * WIDE), BF16)] * 2
            + [pltpu.VMEM((size, TILE), F32), pltpu.VMEM((2, length, WIDE), F32)]
            + [pltpu.VMEM((size, size), F32)] * 2
            + [pltpu.VMEM((size, 2 * WIDE), F32)],
        ),
        compiler_params=pltpu.CompilerParams(
            dimension_semantics=("arbitrary",), vmem_limit_bytes=LIMIT
        ),
        name="solve_apply",
    )(where, *held, vectors, other, mine, theirs)

    returned = core_swap(result_other)
    result = jnp.zeros((rows, columns), F32)
    result = lax.dynamic_update_slice_in_dim(result, result_own, core * half, 0)
    return lax.dynamic_update_slice_in_dim(result, returned, (1 - core) * half, 0)


def solution(mesh):
    specs = (P("row", "col"), P("row", "col"), P("row", "col"))
    return jax.shard_map(
        per_device, mesh=mesh, in_specs=specs, out_specs=P("row", "col"), check_vma=False
    )
```

```python
import functools

import jax
import jax.numpy as jnp
from jax import lax
from jax.experimental import pallas as pl
from jax.experimental.pallas import tpu as pltpu
from jax.sharding import PartitionSpec as P

F32 = jnp.float32
BF16 = jnp.bfloat16
HIGHEST = lax.Precision.HIGHEST
PLANES, DEPTH, CORES = 2, 4, 2
CHIPS = PLANES * DEPTH
WIDE = 128
TILE = 1024
LIMIT = 24 << 20
PIECES = ((0, 0), (0, 1), (1, 1), (0, 2), (0, 3)), ((1, 2), (1, 3), (2, 2), (2, 3), (3, 3))


def split2(value):
    high = value.astype(BF16)
    return high, (value - high.astype(F32)).astype(BF16)


def nn(left, right):
    return lax.dot_general(left, right, (((1,), (0,)), ((), ())), preferred_element_type=F32)


def nt(left, right):
    return lax.dot_general(left, right, (((1,), (1,)), ((), ())), preferred_element_type=F32)


def full(left, right):
    return lax.dot_general(
        left, right, (((1,), (0,)), ((), ())), precision=HIGHEST, preferred_element_type=F32
    )


def each_far(step, steps, refs, place):
    up_ref, down_ref, across_ref, end_up_ref, end_across_ref = refs
    chunk = down_ref.shape[0]
    early = step < steps // 2

    @pl.when(early)
    def _():
        place(4, up_ref[:chunk])
        place(5, up_ref[chunk:])
        place(6, down_ref[...])
        place(7, end_up_ref[...])

    @pl.when(jnp.logical_not(early))
    def _():
        place(4, down_ref[...])
        place(5, across_ref[:chunk])
        place(6, across_ref[chunk:])
        place(7, end_across_ref[...])


def gram_kernel(where_ref, *refs, first):
    steps = pl.num_programs(0)
    step = pl.program_id(0)
    count = 8 if first else 13
    panels, rest = refs[:count], refs[count:]
    if first:
        own_ref, other_ref, out_ref, high, low, even, skew, proj = rest
    else:
        own_ref, other_ref, before_ref, keep_ref, send_ref, high, low, even, skew, proj = rest
    core = where_ref[CHIPS]
    lines = panels[0].shape[0]
    half = even.shape[1]
    start_row = high.shape[0] - half

    def place_half(slot, swap, value):
        begin = pl.multiple_of(slot * 2 * lines + lines * (core ^ swap), lines)
        for target, part in zip((high, low), split2(value)):
            target[pl.ds(begin, lines), :] = part

    def place(slot, value):
        place_half(slot, 0, value[:lines])
        place_half(slot, 1, value[lines:])

    for index in range(8):
        place_half(index // 2, index % 2, panels[index][...])
    if not first:
        each_far(step, steps, panels[8:], place)

    @pl.when(step == 0)
    def _():
        even[...] = jnp.zeros_like(even)
        skew[...] = jnp.zeros_like(skew)
        proj[...] = jnp.zeros_like(proj)

    one, two = high[start_row:, :], low[start_row:, :]
    skew[...] += nt(one, two)
    if first:
        even[...] += nt(one, one)
    else:
        even[half:, :] += nt(one, one)
        one_a, two_a = high[:half, :], low[:half, :]
        even[:half, :] += (nt(one_a, two) + nt(two_a, one)) + nt(one_a, one)
    x_one, x_two = split2(jnp.concatenate([own_ref[...], other_ref[...]], axis=1))
    proj[...] += (nn(one, x_two) + nn(two, x_one)) + nn(one, x_one)

    @pl.when(step == steps - 1)
    def _():
        def corner(i, j):
            at_i, at_j = slice(i * WIDE, (i + 1) * WIDE), slice(j * WIDE, (j + 1) * WIDE)
            base = even.shape[0] - half
            return (
                even[base + i * WIDE : base + (i + 1) * WIDE, at_j]
                + skew[at_i, at_j]
                + skew[at_j, at_i].T
            )

        if first:
            out_ref[0, 0:half, :] = proj[:, :WIDE]
            out_ref[1, 0:half, :] = proj[:, WIDE:]
            for at, (i, j) in enumerate(((0, 0), (0, 1), (1, 1))):
                begin = half + at * WIDE
                out_ref[0, begin : begin + WIDE, :] = corner(i, j)
                out_ref[1, begin : begin + WIDE, :] = jnp.zeros((WIDE, WIDE), F32)
        else:
            keep_ref[0:half, :] = before_ref[0, 0:half, :]
            send_ref[0:half, :] = before_ref[1, 0:half, :]
            keep_ref[half : 2 * half, :] = proj[:, :WIDE]
            send_ref[half : 2 * half, :] = proj[:, WIDE:]

            def blocks(part, target):
                for at, (i, j) in enumerate(PIECES[part]):
                    begin = 2 * half + at * WIDE
                    if j < 2:
                        index = half + ((0, 0), (0, 1), (1, 1)).index((i, j)) * WIDE
                        block = before_ref[0, index : index + WIDE, :]
                    elif i < 2:
                        block = even[i * WIDE : (i + 1) * WIDE, (j - 2) * WIDE : (j - 1) * WIDE]
                    else:
                        block = corner(i - 2, j - 2)
                    target[begin : begin + WIDE, :] = block

            @pl.when(core == 0)
            def _():
                blocks(0, keep_ref)
                blocks(1, send_ref)

            @pl.when(core != 0)
            def _():
                blocks(1, keep_ref)
                blocks(0, send_ref)


def solve(where_ref, mine_ref, other_ref, solved_ref, both, rows_done, ordered, sides):
    core = where_ref[CHIPS]
    both[core] = mine_ref[...]
    both[1 - core] = other_ref[...]
    count = 4
    size = count * WIDE
    panel = size // 2
    base = 16

    def relative(i, j):
        for part in range(2):
            if (i, j) in PIECES[part]:
                start = size + PIECES[part].index((i, j)) * WIDE
                return both[part, start : start + WIDE, :]

    group = size // (2 * CORES * CHIPS)

    def target(index):
        slot, at_core, part = index // (2 * CORES), (index // 2) % CORES, index % 2
        start = part * panel + where_ref[slot] * CORES * group + at_core * group
        return pl.ds(pl.multiple_of(start, group), group)

    for i in range(count):
        strip = jnp.concatenate(
            [relative(i, j) if i <= j else relative(j, i).T for j in range(count)], axis=1
        )
        for k in range(WIDE // group):
            rows_done[target(i * (WIDE // group) + k), :] = strip[k * group : (k + 1) * group]
    for i in range(count):
        strip = jnp.concatenate(
            [
                rows_done[j * WIDE : (j + 1) * WIDE, i * WIDE : (i + 1) * WIDE].T
                for j in range(count)
            ],
            axis=1,
        )
        for k in range(WIDE // group):
            ordered[target(i * (WIDE // group) + k), :] = strip[k * group : (k + 1) * group]
    for index in range(size // group):
        at = slice(index * group, (index + 1) * group)
        sides[target(index), :] = jnp.concatenate([mine_ref[at, :], other_ref[at, :]], axis=1)

    def block(i, j):
        return ordered[i * WIDE : (i + 1) * WIDE, j * WIDE : (j + 1) * WIDE]

    row = lax.broadcasted_iota(jnp.int32, (WIDE, WIDE), 0)
    column = lax.broadcasted_iota(jnp.int32, (WIDE, WIDE), 1)
    same = (row // base) == (column // base)
    diagonals = []
    for i in range(count):
        value = block(i, i)
        diagonals.append(
            jnp.where(row < column, value, jnp.where(row == column, value * 0.5, 0.0))
        )
    lane = lax.broadcasted_iota(jnp.int32, (base, WIDE), 1) % base
    ones = jnp.where(same, 1.0, 0.0).astype(F32)
    spread = []
    for i in range(count):
        flipped = jnp.where(same, diagonals[i], 0.0).T
        folded = flipped[0:base]
        for k in range(1, WIDE // base):
            folded = folded + flipped[k * base : (k + 1) * base]
        stacked = jnp.concatenate([jnp.where(lane == k, folded, 0.0) for k in range(base)], axis=0)
        spread.append(full(stacked, ones))
    wide_lane = lax.broadcasted_iota(jnp.int32, (1, size), 1) % base
    wide_row = lax.broadcasted_iota(jnp.int32, (base, size), 0)
    solved = jnp.zeros((base, size), F32)
    for i in range(base - 1, -1, -1):
        factor = jnp.concatenate([s[i * base : (i + 1) * base] for s in spread], axis=1)
        total = jnp.sum(factor * solved, axis=0, keepdims=True)
        line = (jnp.where(wide_lane == i, 1.0, 0.0) - total) / factor[i : i + 1]
        solved = jnp.where(wide_row == i, line, solved)

    def three(left, right):
        return (nn(left[0], right[1]) + nn(left[1], right[0])) + nn(left[0], right[0])

    small = []
    for i in range(count):
        tiled = jnp.concatenate([solved[:, i * WIDE : (i + 1) * WIDE]] * (WIDE // base), axis=0)
        small.append(jnp.where(same, tiled, 0.0))
    width = base
    while width < WIDE:
        picked = ((row // width) % 2 == 0) & (column // width == row // width + 1)
        for i in range(count):
            inverse = split2(small[i])
            coupling = split2(jnp.where(picked, diagonals[i], 0.0))
            small[i] = small[i] - three(split2(three(inverse, coupling)), inverse)
        width *= 2
    inverses = []
    for half in range(2):
        left, right = small[2 * half], small[2 * half + 1]
        coupling = split2(block(2 * half, 2 * half + 1))
        corner = -three(split2(three(split2(left), coupling)), split2(right))
        top = jnp.concatenate([left, corner], axis=1)
        bottom = jnp.concatenate([jnp.zeros((WIDE, WIDE), F32), right], axis=1)
        inverses.append(split2(jnp.concatenate([top, bottom], axis=0)))
    corner = jnp.concatenate(
        [
            jnp.concatenate([block(0, 2), block(0, 3)], axis=1),
            jnp.concatenate([block(1, 2), block(1, 3)], axis=1),
        ],
        axis=0,
    )
    right_side = sides[...]
    second = three(inverses[1], split2(right_side[panel:]))
    first = three(
        inverses[0], split2(right_side[:panel] - three(split2(corner), split2(second)))
    )
    solved_ref[0:panel, :] = first
    solved_ref[panel:, :] = second


def apply_kernel(where_ref, *refs):
    step = pl.program_id(0)
    steps = pl.num_programs(0)
    panels = refs[:13]
    current_own, current_other, mine_ref, theirs_ref, out_own, out_other = refs[13:19]
    solved, high, low, merged, both, rows_done, ordered, sides = refs[19:]
    core = where_ref[CHIPS]
    panel = solved.shape[0] // 2
    chunk = 2 * panels[0].shape[0]
    group = chunk // 4

    @pl.when(step == 0)
    def _():
        solve(where_ref, mine_ref, theirs_ref, solved, both, rows_done, ordered, sides)
        for index in range(2 * CHIPS):
            chip = where_ref[index // 2]
            for part in range(2):
                start = pl.multiple_of(
                    part * panel + chip * 2 * group + group * (core ^ (index % 2)), group
                )
                at = (2 * index + part) * group
                for target, value in zip((high, low), split2(solved[pl.ds(start, group), :])):
                    target[at : at + group, :] = value

    def place(slot, value):
        merged[slot * chunk : (slot + 1) * chunk, :] = value

    for index in range(8):
        merged[index * chunk // 2 : (index + 1) * chunk // 2, :] = panels[index][...]
    each_far(step, steps, panels[8:], place)
    one, two = split2(merged[...])
    first, second = high[...], low[...]

    def tn(left, right):
        return lax.dot_general(left, right, (((0,), (0,)), ((), ())), preferred_element_type=F32)

    change = (tn(one, second) + tn(two, first)) + tn(one, first)
    out_own[...] = current_own[...] - change[:, :WIDE]
    out_other[...] = current_other[...] - change[:, WIDE:]


def per_device(vectors, panel_one, panel_two):
    rows, columns = vectors.shape
    group = panel_one.shape[1]
    half = rows // 2
    size = 2 * group * CHIPS * CORES
    quarter = half // 2
    chunk = 4 * group
    steps = half // TILE
    at = lax.axis_index("col")
    core, depth, plane = at % CORES, (at // CORES) % DEPTH, at // (CORES * DEPTH)

    def permute(value, move):
        pairs = []
        for source in range(CHIPS * CORES):
            k, z, x = source % CORES, (source // CORES) % DEPTH, source // (CORES * DEPTH)
            k, z, x = move(k, z, x)
            pairs.append((source, (x * DEPTH + z % DEPTH) * CORES + k))
        return lax.ppermute(value, "col", pairs)

    def core_swap(value):
        return permute(value, lambda k, z, x: (1 - k, z, x))

    def up(value):
        return permute(value, lambda k, z, x: (k, z + 1, x))

    def down(value):
        return permute(value, lambda k, z, x: (k, z - 1, x))

    def across(value):
        return permute(value, lambda k, z, x: (k, z, 1 - x))

    def half_of(which):
        picked = [lax.dynamic_slice_in_dim(v.T, which * half, half, 1) for v in (panel_one, panel_two)]
        return jnp.concatenate(picked, axis=0)

    a_own = half_of(core)
    b_own = core_swap(half_of(1 - core))
    own = jnp.concatenate([a_own, b_own], axis=0)
    a_away, a_below, a_above = across(a_own), up(a_own), down(a_own)
    b_own, other = lax.optimization_barrier((b_own, core_swap(vectors)))
    b_away, b_below, b_above = across(b_own), up(b_own), down(b_own)
    near = (a_own, b_own, a_below, b_below, a_above, b_above, a_away, b_away)

    def early_half(*values):
        return [v[:, :quarter] for v in values]

    def late_half(*values):
        return [v[:, quarter:] for v in values]

    to_up = jnp.concatenate(early_half(a_below, b_below, a_away, b_away), axis=0)
    to_down = jnp.concatenate(
        late_half(a_above, b_above) + early_half(a_away, b_away), axis=0
    )
    to_across = jnp.concatenate(late_half(a_below, b_below, a_above, b_above), axis=0)
    sent_up, sent_down, sent_across = up(to_up), down(to_down), across(to_across)

    chips = []
    for x_step, z_step in ((0, 0), (0, -1), (0, 1), (1, 0), (0, 2), (1, -1), (1, 1), (1, 2)):
        chips.append(jnp.bitwise_xor(plane, x_step) * DEPTH + (depth + z_step) % DEPTH)
    where = jnp.stack(chips + [core]).astype(jnp.int32)

    turn = steps // 2
    whole = [pl.BlockSpec((chunk // 2, TILE), lambda j, w: (0, j))] * 8

    def early(lines):
        return pl.BlockSpec((lines, TILE), lambda j, w: (0, jnp.minimum(j, turn - 1)))

    def late(lines):
        return pl.BlockSpec((lines, TILE), lambda j, w: (0, jnp.maximum(j - turn, 0)))

    both = pl.BlockSpec(
        (chunk, TILE), lambda j, w: (jnp.where(j < turn, 1, 0), jnp.where(j < turn, j, j - turn))
    )
    parts_far = [early(2 * chunk), both, late(2 * chunk), early(chunk), late(chunk)]
    own_spec = pl.BlockSpec((TILE, columns), lambda j, w: (w[CHIPS] * steps + j, 0))
    length = size + 5 * WIDE
    span = size // 2

    def gram(first, pieces, extra):
        if first:
            shapes = [jax.ShapeDtypeStruct((2, span + 3 * WIDE, WIDE), F32)]
        else:
            shapes = [jax.ShapeDtypeStruct((length, WIDE), F32)] * 2
        height = span if first else size
        units = 10 if first else 16
        return pl.pallas_call(
            functools.partial(gram_kernel, first=first),
            out_shape=shapes,
            grid_spec=pltpu.PrefetchScalarGridSpec(
                num_scalar_prefetch=1,
                grid=(steps,),
                in_specs=whole
                + ([] if first else parts_far)
                + [own_spec, own_spec]
                + [pl.BlockSpec(v.shape, lambda j, w: (0, 0, 0)) for v in extra],
                out_specs=[
                    pl.BlockSpec(v.shape, lambda j, w, n=len(v.shape): (0,) * n) for v in shapes
                ],
                scratch_shapes=[pltpu.VMEM((height, TILE), BF16)] * 2
                + [
                    pltpu.VMEM((height, span), F32),
                    pltpu.VMEM((span, span), F32),
                    pltpu.VMEM((span, 2 * WIDE), F32),
                ],
            ),
            compiler_params=pltpu.CompilerParams(
                dimension_semantics=("arbitrary",), vmem_limit_bytes=LIMIT
            ),
            cost_estimate=pl.CostEstimate(
                flops=2 * 3 * units * span * span * half,
                bytes_accessed=4 * half * (height + columns * 2),
                transcendentals=0,
            ),
            name="gram_near" if first else "gram_far",
        )(where, *pieces, vectors, other, *extra)

    (before,) = gram(True, near, ())
    before, sent_up, sent_down = lax.optimization_barrier((before, sent_up, sent_down))
    end_up = up(sent_up[chunk:])
    end_across = across(sent_down[:chunk])
    far = (sent_up, sent_down, sent_across, end_up, end_across)
    kept, sent = gram(False, near + far, (before,))
    mine = kept + core_swap(sent)
    members = lax.axis_size("row")
    parts = lax.all_to_all(mine.reshape(members, length // members, WIDE), "row", 0, 0)
    total = jnp.sum(parts, axis=0)
    spread = jnp.broadcast_to(total[None], (members,) + total.shape)
    mine = lax.all_to_all(spread, "row", 0, 0).reshape(length, WIDE)
    theirs = core_swap(mine)

    *held, vectors_held, other_held = [
        pltpu.with_memory_space_constraint(v, pltpu.HBM) for v in near + far + (vectors, other)
    ]
    result_own, result_other = pl.pallas_call(
        apply_kernel,
        out_shape=[jax.ShapeDtypeStruct((half, columns), F32)] * 2,
        grid_spec=pltpu.PrefetchScalarGridSpec(
            num_scalar_prefetch=1,
            grid=(steps,),
            in_specs=whole
            + parts_far
            + [own_spec, own_spec]
            + [pl.BlockSpec((length, WIDE), lambda j, w: (0, 0))] * 2,
            out_specs=[pl.BlockSpec((TILE, columns), lambda j, w: (j, 0))] * 2,
            scratch_shapes=[pltpu.VMEM((size, 2 * WIDE), F32)]
            + [pltpu.VMEM((size, 2 * WIDE), BF16)] * 2
            + [pltpu.VMEM((size, TILE), F32), pltpu.VMEM((2, length, WIDE), F32)]
            + [pltpu.VMEM((size, size), F32)] * 2
            + [pltpu.VMEM((size, 2 * WIDE), F32)],
        ),
        compiler_params=pltpu.CompilerParams(
            dimension_semantics=("arbitrary",), vmem_limit_bytes=LIMIT
        ),
        name="solve_apply",
    )(where, *held, vectors_held, other_held, mine, theirs)

    returned = core_swap(result_other)
    result = jnp.zeros((rows, columns), F32)
    result = lax.dynamic_update_slice_in_dim(result, result_own, core * half, 0)
    return lax.dynamic_update_slice_in_dim(result, returned, (1 - core) * half, 0)


def solution(mesh):
    specs = (P("row", "col"), P("row", "col"), P("row", "col"))
    return jax.shard_map(
        per_device, mesh=mesh, in_specs=specs, out_specs=P("row", "col"), check_vma=False
    )
```

```python
import functools

import jax
import jax.numpy as jnp
from jax import lax
from jax.experimental import pallas as pl
from jax.experimental.pallas import tpu as pltpu
from jax.sharding import PartitionSpec as P

F32 = jnp.float32
BF16 = jnp.bfloat16
HIGHEST = lax.Precision.HIGHEST
PLANES, DEPTH, CORES = 2, 4, 2
CHIPS = PLANES * DEPTH
WIDE = 128
TILE = 1024
LIMIT = 24 << 20
PIECES = ((0, 0), (0, 1), (1, 1), (0, 2), (0, 3)), ((1, 2), (1, 3), (2, 2), (2, 3), (3, 3))


def split2(value):
    high = value.astype(BF16)
    return high, (value - high.astype(F32)).astype(BF16)


def nn(left, right):
    return lax.dot_general(left, right, (((1,), (0,)), ((), ())), preferred_element_type=F32)


def nt(left, right):
    return lax.dot_general(left, right, (((1,), (1,)), ((), ())), preferred_element_type=F32)


def full(left, right):
    return lax.dot_general(
        left, right, (((1,), (0,)), ((), ())), precision=HIGHEST, preferred_element_type=F32
    )


def each_far(step, steps, refs, place_half):
    early = step < steps // 2

    @pl.when(early)
    def _():
        for swap in range(2):
            up_ref, down_ref, across_ref, end_up_ref, end_across_ref = refs[5 * swap : 5 * swap + 5]
            lines = down_ref.shape[0]
            place_half(4, swap, up_ref[:lines])
            place_half(5, swap, up_ref[lines:])
            place_half(6, swap, down_ref[...])
            place_half(7, swap, end_up_ref[...])

    @pl.when(jnp.logical_not(early))
    def _():
        for swap in range(2):
            up_ref, down_ref, across_ref, end_up_ref, end_across_ref = refs[5 * swap : 5 * swap + 5]
            lines = down_ref.shape[0]
            place_half(4, swap, down_ref[...])
            place_half(5, swap, across_ref[:lines])
            place_half(6, swap, across_ref[lines:])
            place_half(7, swap, end_across_ref[...])


def gram_kernel(where_ref, *refs, first):
    steps = pl.num_programs(0)
    step = pl.program_id(0)
    count = 8 if first else 18
    panels, rest = refs[:count], refs[count:]
    if first:
        own_ref, other_ref, out_ref, high, low, even, skew, proj = rest
    else:
        own_ref, other_ref, before_ref, keep_ref, send_ref, high, low, even, skew, proj = rest
    core = where_ref[CHIPS]
    lines = panels[0].shape[0]
    half = even.shape[1]
    start_row = high.shape[0] - half

    def place_half(slot, swap, value):
        begin = pl.multiple_of(slot * 2 * lines + lines * (core ^ swap), lines)
        for target, part in zip((high, low), split2(value)):
            target[pl.ds(begin, lines), :] = part

    for index in range(8):
        place_half(index // 2, index % 2, panels[index][...])
    if not first:
        each_far(step, steps, panels[8:], place_half)

    @pl.when(step == 0)
    def _():
        even[...] = jnp.zeros_like(even)
        skew[...] = jnp.zeros_like(skew)
        proj[...] = jnp.zeros_like(proj)

    one, two = high[start_row:, :], low[start_row:, :]
    skew[...] += nt(one, two)
    if first:
        even[...] += nt(one, one)
    else:
        even[half:, :] += nt(one, one)
        one_a, two_a = high[:half, :], low[:half, :]
        even[:half, :] += (nt(one_a, two) + nt(two_a, one)) + nt(one_a, one)
    x_one, x_two = split2(jnp.concatenate([own_ref[...], other_ref[...]], axis=1))
    proj[...] += (nn(one, x_two) + nn(two, x_one)) + nn(one, x_one)

    @pl.when(step == steps - 1)
    def _():
        def corner(i, j):
            at_i, at_j = slice(i * WIDE, (i + 1) * WIDE), slice(j * WIDE, (j + 1) * WIDE)
            base = even.shape[0] - half
            return (
                even[base + i * WIDE : base + (i + 1) * WIDE, at_j]
                + skew[at_i, at_j]
                + skew[at_j, at_i].T
            )

        if first:
            out_ref[0, 0:half, :] = proj[:, :WIDE]
            out_ref[1, 0:half, :] = proj[:, WIDE:]
            for at, (i, j) in enumerate(((0, 0), (0, 1), (1, 1))):
                begin = half + at * WIDE
                out_ref[0, begin : begin + WIDE, :] = corner(i, j)
                out_ref[1, begin : begin + WIDE, :] = jnp.zeros((WIDE, WIDE), F32)
        else:
            keep_ref[0:half, :] = before_ref[0, 0:half, :]
            send_ref[0:half, :] = before_ref[1, 0:half, :]
            keep_ref[half : 2 * half, :] = proj[:, :WIDE]
            send_ref[half : 2 * half, :] = proj[:, WIDE:]

            def blocks(part, target):
                for at, (i, j) in enumerate(PIECES[part]):
                    begin = 2 * half + at * WIDE
                    if j < 2:
                        index = half + ((0, 0), (0, 1), (1, 1)).index((i, j)) * WIDE
                        block = before_ref[0, index : index + WIDE, :]
                    elif i < 2:
                        block = even[i * WIDE : (i + 1) * WIDE, (j - 2) * WIDE : (j - 1) * WIDE]
                    else:
                        block = corner(i - 2, j - 2)
                    target[begin : begin + WIDE, :] = block

            @pl.when(core == 0)
            def _():
                blocks(0, keep_ref)
                blocks(1, send_ref)

            @pl.when(core != 0)
            def _():
                blocks(1, keep_ref)
                blocks(0, send_ref)


def solve(where_ref, mine_ref, other_ref, solved_ref, both, rows_done, ordered, sides):
    core = where_ref[CHIPS]
    both[core] = mine_ref[...]
    both[1 - core] = other_ref[...]
    count = 4
    size = count * WIDE
    panel = size // 2
    base = 16

    def relative(i, j):
        for part in range(2):
            if (i, j) in PIECES[part]:
                start = size + PIECES[part].index((i, j)) * WIDE
                return both[part, start : start + WIDE, :]

    group = size // (2 * CORES * CHIPS)

    def target(index):
        slot, at_core, part = index // (2 * CORES), (index // 2) % CORES, index % 2
        start = part * panel + where_ref[slot] * CORES * group + at_core * group
        return pl.ds(pl.multiple_of(start, group), group)

    for i in range(count):
        strip = jnp.concatenate(
            [relative(i, j) if i <= j else relative(j, i).T for j in range(count)], axis=1
        )
        for k in range(WIDE // group):
            rows_done[target(i * (WIDE // group) + k), :] = strip[k * group : (k + 1) * group]
    for i in range(count):
        strip = jnp.concatenate(
            [
                rows_done[j * WIDE : (j + 1) * WIDE, i * WIDE : (i + 1) * WIDE].T
                for j in range(count)
            ],
            axis=1,
        )
        for k in range(WIDE // group):
            ordered[target(i * (WIDE // group) + k), :] = strip[k * group : (k + 1) * group]
    for index in range(size // group):
        at = slice(index * group, (index + 1) * group)
        sides[target(index), :] = jnp.concatenate([mine_ref[at, :], other_ref[at, :]], axis=1)

    def block(i, j):
        return ordered[i * WIDE : (i + 1) * WIDE, j * WIDE : (j + 1) * WIDE]

    row = lax.broadcasted_iota(jnp.int32, (WIDE, WIDE), 0)
    column = lax.broadcasted_iota(jnp.int32, (WIDE, WIDE), 1)
    same = (row // base) == (column // base)
    diagonals = []
    for i in range(count):
        value = block(i, i)
        diagonals.append(
            jnp.where(row < column, value, jnp.where(row == column, value * 0.5, 0.0))
        )
    lane = lax.broadcasted_iota(jnp.int32, (base, WIDE), 1) % base
    ones = jnp.where(same, 1.0, 0.0).astype(F32)
    spread = []
    for i in range(count):
        flipped = jnp.where(same, diagonals[i], 0.0).T
        folded = flipped[0:base]
        for k in range(1, WIDE // base):
            folded = folded + flipped[k * base : (k + 1) * base]
        stacked = jnp.concatenate([jnp.where(lane == k, folded, 0.0) for k in range(base)], axis=0)
        spread.append(full(stacked, ones))
    wide_lane = lax.broadcasted_iota(jnp.int32, (1, size), 1) % base
    wide_row = lax.broadcasted_iota(jnp.int32, (base, size), 0)
    solved = jnp.zeros((base, size), F32)
    for i in range(base - 1, -1, -1):
        factor = jnp.concatenate([s[i * base : (i + 1) * base] for s in spread], axis=1)
        total = jnp.sum(factor * solved, axis=0, keepdims=True)
        line = (jnp.where(wide_lane == i, 1.0, 0.0) - total) / factor[i : i + 1]
        solved = jnp.where(wide_row == i, line, solved)

    def three(left, right):
        return (nn(left[0], right[1]) + nn(left[1], right[0])) + nn(left[0], right[0])

    small = []
    for i in range(count):
        tiled = jnp.concatenate([solved[:, i * WIDE : (i + 1) * WIDE]] * (WIDE // base), axis=0)
        small.append(jnp.where(same, tiled, 0.0))
    width = base
    while width < WIDE:
        picked = ((row // width) % 2 == 0) & (column // width == row // width + 1)
        for i in range(count):
            inverse = split2(small[i])
            coupling = split2(jnp.where(picked, diagonals[i], 0.0))
            small[i] = small[i] - three(split2(three(inverse, coupling)), inverse)
        width *= 2
    inverses = []
    for half in range(2):
        left, right = small[2 * half], small[2 * half + 1]
        coupling = split2(block(2 * half, 2 * half + 1))
        corner = -three(split2(three(split2(left), coupling)), split2(right))
        top = jnp.concatenate([left, corner], axis=1)
        bottom = jnp.concatenate([jnp.zeros((WIDE, WIDE), F32), right], axis=1)
        inverses.append(split2(jnp.concatenate([top, bottom], axis=0)))
    corner = jnp.concatenate(
        [
            jnp.concatenate([block(0, 2), block(0, 3)], axis=1),
            jnp.concatenate([block(1, 2), block(1, 3)], axis=1),
        ],
        axis=0,
    )
    right_side = sides[...]
    second = three(inverses[1], split2(right_side[panel:]))
    first = three(
        inverses[0], split2(right_side[:panel] - three(split2(corner), split2(second)))
    )
    solved_ref[0:panel, :] = first
    solved_ref[panel:, :] = second


def apply_kernel(where_ref, *refs):
    step = pl.program_id(0)
    steps = pl.num_programs(0)
    panels = refs[:18]
    current_own, current_other, mine_ref, theirs_ref, out_own, out_other = refs[18:24]
    solved, high, low, merged, both, rows_done, ordered, sides = refs[24:]
    core = where_ref[CHIPS]
    panel = solved.shape[0] // 2
    chunk = 2 * panels[0].shape[0]
    group = chunk // 4

    @pl.when(step == 0)
    def _():
        solve(where_ref, mine_ref, theirs_ref, solved, both, rows_done, ordered, sides)
        for index in range(2 * CHIPS):
            chip = where_ref[index // 2]
            for part in range(2):
                start = pl.multiple_of(
                    part * panel + chip * 2 * group + group * (core ^ (index % 2)), group
                )
                at = (2 * index + part) * group
                for target, value in zip((high, low), split2(solved[pl.ds(start, group), :])):
                    target[at : at + group, :] = value

    def place_half(slot, swap, value):
        at = slot * chunk + swap * (chunk // 2)
        merged[at : at + chunk // 2, :] = value

    for index in range(8):
        place_half(index // 2, index % 2, panels[index][...])
    each_far(step, steps, panels[8:], place_half)
    one, two = split2(merged[...])
    first, second = high[...], low[...]

    def tn(left, right):
        return lax.dot_general(left, right, (((0,), (0,)), ((), ())), preferred_element_type=F32)

    change = (tn(one, second) + tn(two, first)) + tn(one, first)
    out_own[...] = current_own[...] - change[:, :WIDE]
    out_other[...] = current_other[...] - change[:, WIDE:]


def per_device(vectors, panel_one, panel_two):
    rows, columns = vectors.shape
    group = panel_one.shape[1]
    half = rows // 2
    size = 2 * group * CHIPS * CORES
    quarter = half // 2
    chunk = 4 * group
    steps = half // TILE
    at = lax.axis_index("col")
    core, depth, plane = at % CORES, (at // CORES) % DEPTH, at // (CORES * DEPTH)

    def permute(value, move):
        pairs = []
        for source in range(CHIPS * CORES):
            k, z, x = source % CORES, (source // CORES) % DEPTH, source // (CORES * DEPTH)
            k, z, x = move(k, z, x)
            pairs.append((source, (x * DEPTH + z % DEPTH) * CORES + k))
        return lax.ppermute(value, "col", pairs)

    def core_swap(value):
        return permute(value, lambda k, z, x: (1 - k, z, x))

    def up(value):
        return permute(value, lambda k, z, x: (k, z + 1, x))

    def down(value):
        return permute(value, lambda k, z, x: (k, z - 1, x))

    def across(value):
        return permute(value, lambda k, z, x: (k, z, 1 - x))

    def half_of(which):
        picked = [lax.dynamic_slice_in_dim(v.T, which * half, half, 1) for v in (panel_one, panel_two)]
        return jnp.concatenate(picked, axis=0)

    a_own = half_of(core)
    b_own = core_swap(half_of(1 - core))
    own = jnp.concatenate([a_own, b_own], axis=0)
    a_own, b_own, other = lax.optimization_barrier((a_own, b_own, core_swap(vectors)))
    a_away, a_below, a_above = across(a_own), up(a_own), down(a_own)
    b_away, b_below, b_above = across(b_own), up(b_own), down(b_own)
    near = (a_own, b_own, a_below, b_below, a_above, b_above, a_away, b_away)

    def early_half(*values):
        return [v[:, :quarter] for v in values]

    def late_half(*values):
        return [v[:, quarter:] for v in values]

    def second_wave(below, above, away):
        to_up = jnp.concatenate(early_half(below, away), axis=0)
        to_down = jnp.concatenate(late_half(above) + early_half(away), axis=0)
        to_across = jnp.concatenate(late_half(below, above), axis=0)
        return up(to_up), down(to_down), across(to_across)

    a_sent = second_wave(a_below, a_above, a_away)
    b_sent = second_wave(b_below, b_above, b_away)

    chips = []
    for x_step, z_step in ((0, 0), (0, -1), (0, 1), (1, 0), (0, 2), (1, -1), (1, 1), (1, 2)):
        chips.append(jnp.bitwise_xor(plane, x_step) * DEPTH + (depth + z_step) % DEPTH)
    where = jnp.stack(chips + [core]).astype(jnp.int32)

    turn = steps // 2
    whole = [pl.BlockSpec((chunk // 2, TILE), lambda j, w: (0, j))] * 8

    def early(lines):
        return pl.BlockSpec((lines, TILE), lambda j, w: (0, jnp.minimum(j, turn - 1)))

    def late(lines):
        return pl.BlockSpec((lines, TILE), lambda j, w: (0, jnp.maximum(j - turn, 0)))

    both = pl.BlockSpec(
        (chunk // 2, TILE), lambda j, w: (jnp.where(j < turn, 1, 0), jnp.where(j < turn, j, j - turn))
    )
    parts_far = [early(chunk), both, late(chunk), early(chunk // 2), late(chunk // 2)] * 2
    own_spec = pl.BlockSpec((TILE, columns), lambda j, w: (w[CHIPS] * steps + j, 0))
    length = size + 5 * WIDE
    span = size // 2

    def gram(first, pieces, extra):
        if first:
            shapes = [jax.ShapeDtypeStruct((2, span + 3 * WIDE, WIDE), F32)]
        else:
            shapes = [jax.ShapeDtypeStruct((length, WIDE), F32)] * 2
        height = span if first else size
        units = 10 if first else 16
        return pl.pallas_call(
            functools.partial(gram_kernel, first=first),
            out_shape=shapes,
            grid_spec=pltpu.PrefetchScalarGridSpec(
                num_scalar_prefetch=1,
                grid=(steps,),
                in_specs=whole
                + ([] if first else parts_far)
                + [own_spec, own_spec]
                + [pl.BlockSpec(v.shape, lambda j, w: (0, 0, 0)) for v in extra],
                out_specs=[
                    pl.BlockSpec(v.shape, lambda j, w, n=len(v.shape): (0,) * n) for v in shapes
                ],
                scratch_shapes=[pltpu.VMEM((height, TILE), BF16)] * 2
                + [
                    pltpu.VMEM((height, span), F32),
                    pltpu.VMEM((span, span), F32),
                    pltpu.VMEM((span, 2 * WIDE), F32),
                ],
            ),
            compiler_params=pltpu.CompilerParams(
                dimension_semantics=("arbitrary",), vmem_limit_bytes=LIMIT
            ),
            cost_estimate=pl.CostEstimate(
                flops=2 * 3 * units * span * span * half,
                bytes_accessed=4 * half * (height + columns * 2),
                transcendentals=0,
            ),
            name="gram_near" if first else "gram_far",
        )(where, *pieces, vectors, other, *extra)

    (before,) = gram(True, near, ())
    lines = chunk // 2
    far = ()
    for sent_up, sent_down, sent_across in (a_sent, b_sent):
        _, sent_up, sent_down = lax.optimization_barrier((before, sent_up, sent_down))
        far += (sent_up, sent_down, sent_across, up(sent_up[lines:]), across(sent_down[:lines]))
    kept, sent = gram(False, near + far, (before,))
    mine = kept + core_swap(sent)
    members = lax.axis_size("row")
    parts = lax.all_to_all(mine.reshape(members, length // members, WIDE), "row", 0, 0)
    total = jnp.sum(parts, axis=0)
    spread = jnp.broadcast_to(total[None], (members,) + total.shape)
    mine = lax.all_to_all(spread, "row", 0, 0).reshape(length, WIDE)
    theirs = core_swap(mine)

    *held, vectors_held, other_held = [
        pltpu.with_memory_space_constraint(v, pltpu.HBM) for v in near + far + (vectors, other)
    ]
    result_own, result_other = pl.pallas_call(
        apply_kernel,
        out_shape=[jax.ShapeDtypeStruct((half, columns), F32)] * 2,
        grid_spec=pltpu.PrefetchScalarGridSpec(
            num_scalar_prefetch=1,
            grid=(steps,),
            in_specs=whole
            + parts_far
            + [own_spec, own_spec]
            + [pl.BlockSpec((length, WIDE), lambda j, w: (0, 0))] * 2,
            out_specs=[pl.BlockSpec((TILE, columns), lambda j, w: (j, 0))] * 2,
            scratch_shapes=[pltpu.VMEM((size, 2 * WIDE), F32)]
            + [pltpu.VMEM((size, 2 * WIDE), BF16)] * 2
            + [pltpu.VMEM((size, TILE), F32), pltpu.VMEM((2, length, WIDE), F32)]
            + [pltpu.VMEM((size, size), F32)] * 2
            + [pltpu.VMEM((size, 2 * WIDE), F32)],
        ),
        compiler_params=pltpu.CompilerParams(
            dimension_semantics=("arbitrary",), vmem_limit_bytes=LIMIT
        ),
        name="solve_apply",
    )(where, *held, vectors_held, other_held, mine, theirs)

    returned = core_swap(result_other)
    result = jnp.zeros((rows, columns), F32)
    result = lax.dynamic_update_slice_in_dim(result, result_own, core * half, 0)
    return lax.dynamic_update_slice_in_dim(result, returned, (1 - core) * half, 0)


def solution(mesh):
    specs = (P("row", "col"), P("row", "col"), P("row", "col"))
    return jax.shard_map(
        per_device, mesh=mesh, in_specs=specs, out_specs=P("row", "col"), check_vma=False
    )
```

```python
import functools

import jax
import jax.numpy as jnp
from jax import lax
from jax.experimental import pallas as pl
from jax.experimental.pallas import tpu as pltpu
from jax.sharding import PartitionSpec as P

F32 = jnp.float32
BF16 = jnp.bfloat16
HIGHEST = lax.Precision.HIGHEST
PLANES, DEPTH, CORES = 2, 4, 2
CHIPS = PLANES * DEPTH
WIDE = 128
TILE = 2048
LIMIT = 32 << 20
PIECES = ((0, 0), (0, 1), (1, 1), (0, 2), (0, 3)), ((1, 2), (1, 3), (2, 2), (2, 3), (3, 3))


def split2(value):
    high = value.astype(BF16)
    return high, (value - high.astype(F32)).astype(BF16)


def nn(left, right):
    return lax.dot_general(left, right, (((1,), (0,)), ((), ())), preferred_element_type=F32)


def nt(left, right):
    return lax.dot_general(left, right, (((1,), (1,)), ((), ())), preferred_element_type=F32)


def full(left, right):
    return lax.dot_general(
        left, right, (((1,), (0,)), ((), ())), precision=HIGHEST, preferred_element_type=F32
    )


def each_far(step, steps, refs, place):
    up_ref, down_ref, across_ref, end_up_ref, end_across_ref = refs
    chunk = down_ref.shape[0]
    early = step < steps // 2

    @pl.when(early)
    def _():
        place(4, up_ref[:chunk])
        place(5, up_ref[chunk:])
        place(6, down_ref[...])
        place(7, end_up_ref[...])

    @pl.when(jnp.logical_not(early))
    def _():
        place(4, down_ref[...])
        place(5, across_ref[:chunk])
        place(6, across_ref[chunk:])
        place(7, end_across_ref[...])


def gram_kernel(where_ref, *refs, first):
    steps = pl.num_programs(0)
    step = pl.program_id(0)
    count = 8 if first else 13
    panels, rest = refs[:count], refs[count:]
    if first:
        own_ref, other_ref, out_ref, high, low, even, skew, proj = rest
    else:
        own_ref, other_ref, before_ref, keep_ref, send_ref, high, low, even, skew, proj = rest
    core = where_ref[CHIPS]
    lines = panels[0].shape[0]
    half = even.shape[1]
    start_row = high.shape[0] - half

    def place_half(slot, swap, value):
        begin = pl.multiple_of(slot * 2 * lines + lines * (core ^ swap), lines)
        for target, part in zip((high, low), split2(value)):
            target[pl.ds(begin, lines), :] = part

    def place(slot, value):
        place_half(slot, 0, value[:lines])
        place_half(slot, 1, value[lines:])

    for index in range(8):
        place_half(index // 2, index % 2, panels[index][...])
    if not first:
        each_far(step, steps, panels[8:], place)

    @pl.when(step == 0)
    def _():
        even[...] = jnp.zeros_like(even)
        skew[...] = jnp.zeros_like(skew)
        proj[...] = jnp.zeros_like(proj)

    one, two = high[start_row:, :], low[start_row:, :]
    skew[...] += nt(one, two)
    if first:
        even[...] += nt(one, one)
    else:
        even[half:, :] += nt(one, one)
        one_a, two_a = high[:half, :], low[:half, :]
        even[:half, :] += (nt(one_a, two) + nt(two_a, one)) + nt(one_a, one)
    x_one, x_two = split2(jnp.concatenate([own_ref[...], other_ref[...]], axis=1))
    proj[...] += (nn(one, x_two) + nn(two, x_one)) + nn(one, x_one)

    @pl.when(step == steps - 1)
    def _():
        def corner(i, j):
            at_i, at_j = slice(i * WIDE, (i + 1) * WIDE), slice(j * WIDE, (j + 1) * WIDE)
            base = even.shape[0] - half
            return (
                even[base + i * WIDE : base + (i + 1) * WIDE, at_j]
                + skew[at_i, at_j]
                + skew[at_j, at_i].T
            )

        if first:
            out_ref[0, 0:half, :] = proj[:, :WIDE]
            out_ref[1, 0:half, :] = proj[:, WIDE:]
            for at, (i, j) in enumerate(((0, 0), (0, 1), (1, 1))):
                begin = half + at * WIDE
                out_ref[0, begin : begin + WIDE, :] = corner(i, j)
                out_ref[1, begin : begin + WIDE, :] = jnp.zeros((WIDE, WIDE), F32)
        else:
            keep_ref[0:half, :] = before_ref[0, 0:half, :]
            send_ref[0:half, :] = before_ref[1, 0:half, :]
            keep_ref[half : 2 * half, :] = proj[:, :WIDE]
            send_ref[half : 2 * half, :] = proj[:, WIDE:]

            def blocks(part, target):
                for at, (i, j) in enumerate(PIECES[part]):
                    begin = 2 * half + at * WIDE
                    if j < 2:
                        index = half + ((0, 0), (0, 1), (1, 1)).index((i, j)) * WIDE
                        block = before_ref[0, index : index + WIDE, :]
                    elif i < 2:
                        block = even[i * WIDE : (i + 1) * WIDE, (j - 2) * WIDE : (j - 1) * WIDE]
                    else:
                        block = corner(i - 2, j - 2)
                    target[begin : begin + WIDE, :] = block

            @pl.when(core == 0)
            def _():
                blocks(0, keep_ref)
                blocks(1, send_ref)

            @pl.when(core != 0)
            def _():
                blocks(1, keep_ref)
                blocks(0, send_ref)


def solve(where_ref, mine_ref, other_ref, solved_ref, both, rows_done, ordered, sides):
    core = where_ref[CHIPS]
    both[core] = mine_ref[...]
    both[1 - core] = other_ref[...]
    count = 4
    size = count * WIDE
    panel = size // 2
    base = 16

    def relative(i, j):
        for part in range(2):
            if (i, j) in PIECES[part]:
                start = size + PIECES[part].index((i, j)) * WIDE
                return both[part, start : start + WIDE, :]

    group = size // (2 * CORES * CHIPS)

    def target(index):
        slot, at_core, part = index // (2 * CORES), (index // 2) % CORES, index % 2
        start = part * panel + where_ref[slot] * CORES * group + at_core * group
        return pl.ds(pl.multiple_of(start, group), group)

    for i in range(count):
        strip = jnp.concatenate(
            [relative(i, j) if i <= j else relative(j, i).T for j in range(count)], axis=1
        )
        for k in range(WIDE // group):
            rows_done[target(i * (WIDE // group) + k), :] = strip[k * group : (k + 1) * group]
    for i in range(count):
        strip = jnp.concatenate(
            [
                rows_done[j * WIDE : (j + 1) * WIDE, i * WIDE : (i + 1) * WIDE].T
                for j in range(count)
            ],
            axis=1,
        )
        for k in range(WIDE // group):
            ordered[target(i * (WIDE // group) + k), :] = strip[k * group : (k + 1) * group]
    for index in range(size // group):
        at = slice(index * group, (index + 1) * group)
        sides[target(index), :] = jnp.concatenate([mine_ref[at, :], other_ref[at, :]], axis=1)

    def block(i, j):
        return ordered[i * WIDE : (i + 1) * WIDE, j * WIDE : (j + 1) * WIDE]

    row = lax.broadcasted_iota(jnp.int32, (WIDE, WIDE), 0)
    column = lax.broadcasted_iota(jnp.int32, (WIDE, WIDE), 1)
    same = (row // base) == (column // base)
    diagonals = []
    for i in range(count):
        value = block(i, i)
        diagonals.append(
            jnp.where(row < column, value, jnp.where(row == column, value * 0.5, 0.0))
        )
    lane = lax.broadcasted_iota(jnp.int32, (base, WIDE), 1) % base
    ones = jnp.where(same, 1.0, 0.0).astype(F32)
    spread = []
    for i in range(count):
        flipped = jnp.where(same, diagonals[i], 0.0).T
        folded = flipped[0:base]
        for k in range(1, WIDE // base):
            folded = folded + flipped[k * base : (k + 1) * base]
        stacked = jnp.concatenate([jnp.where(lane == k, folded, 0.0) for k in range(base)], axis=0)
        spread.append(full(stacked, ones))
    wide_lane = lax.broadcasted_iota(jnp.int32, (1, size), 1) % base
    wide_row = lax.broadcasted_iota(jnp.int32, (base, size), 0)
    solved = jnp.zeros((base, size), F32)
    for i in range(base - 1, -1, -1):
        factor = jnp.concatenate([s[i * base : (i + 1) * base] for s in spread], axis=1)
        total = jnp.sum(factor * solved, axis=0, keepdims=True)
        line = (jnp.where(wide_lane == i, 1.0, 0.0) - total) / factor[i : i + 1]
        solved = jnp.where(wide_row == i, line, solved)

    def three(left, right):
        return (nn(left[0], right[1]) + nn(left[1], right[0])) + nn(left[0], right[0])

    small = []
    for i in range(count):
        tiled = jnp.concatenate([solved[:, i * WIDE : (i + 1) * WIDE]] * (WIDE // base), axis=0)
        small.append(jnp.where(same, tiled, 0.0))
    width = base
    while width < WIDE:
        picked = ((row // width) % 2 == 0) & (column // width == row // width + 1)
        for i in range(count):
            inverse = split2(small[i])
            coupling = split2(jnp.where(picked, diagonals[i], 0.0))
            small[i] = small[i] - three(split2(three(inverse, coupling)), inverse)
        width *= 2
    inverses = []
    for half in range(2):
        left, right = small[2 * half], small[2 * half + 1]
        coupling = split2(block(2 * half, 2 * half + 1))
        corner = -three(split2(three(split2(left), coupling)), split2(right))
        top = jnp.concatenate([left, corner], axis=1)
        bottom = jnp.concatenate([jnp.zeros((WIDE, WIDE), F32), right], axis=1)
        inverses.append(split2(jnp.concatenate([top, bottom], axis=0)))
    corner = jnp.concatenate(
        [
            jnp.concatenate([block(0, 2), block(0, 3)], axis=1),
            jnp.concatenate([block(1, 2), block(1, 3)], axis=1),
        ],
        axis=0,
    )
    right_side = sides[...]
    second = three(inverses[1], split2(right_side[panel:]))
    first = three(
        inverses[0], split2(right_side[:panel] - three(split2(corner), split2(second)))
    )
    solved_ref[0:panel, :] = first
    solved_ref[panel:, :] = second


def apply_kernel(where_ref, *refs):
    step = pl.program_id(0)
    steps = pl.num_programs(0)
    panels = refs[:13]
    current_own, current_other, mine_ref, theirs_ref, out_own, out_other = refs[13:19]
    solved, high, low, merged, both, rows_done, ordered, sides = refs[19:]
    core = where_ref[CHIPS]
    panel = solved.shape[0] // 2
    chunk = 2 * panels[0].shape[0]
    group = chunk // 4

    @pl.when(step == 0)
    def _():
        solve(where_ref, mine_ref, theirs_ref, solved, both, rows_done, ordered, sides)
        for index in range(2 * CHIPS):
            chip = where_ref[index // 2]
            for part in range(2):
                start = pl.multiple_of(
                    part * panel + chip * 2 * group + group * (core ^ (index % 2)), group
                )
                at = (2 * index + part) * group
                for target, value in zip((high, low), split2(solved[pl.ds(start, group), :])):
                    target[at : at + group, :] = value

    def place(slot, value):
        merged[slot * chunk : (slot + 1) * chunk, :] = value

    for index in range(8):
        merged[index * chunk // 2 : (index + 1) * chunk // 2, :] = panels[index][...]
    each_far(step, steps, panels[8:], place)
    one, two = split2(merged[...])
    first, second = high[...], low[...]

    def tn(left, right):
        return lax.dot_general(left, right, (((0,), (0,)), ((), ())), preferred_element_type=F32)

    change = (tn(one, second) + tn(two, first)) + tn(one, first)
    out_own[...] = current_own[...] - change[:, :WIDE]
    out_other[...] = current_other[...] - change[:, WIDE:]


def per_device(vectors, panel_one, panel_two):
    rows, columns = vectors.shape
    group = panel_one.shape[1]
    half = rows // 2
    size = 2 * group * CHIPS * CORES
    quarter = half // 2
    chunk = 4 * group
    steps = half // TILE
    at = lax.axis_index("col")
    core, depth, plane = at % CORES, (at // CORES) % DEPTH, at // (CORES * DEPTH)

    def permute(value, move):
        pairs = []
        for source in range(CHIPS * CORES):
            k, z, x = source % CORES, (source // CORES) % DEPTH, source // (CORES * DEPTH)
            k, z, x = move(k, z, x)
            pairs.append((source, (x * DEPTH + z % DEPTH) * CORES + k))
        return lax.ppermute(value, "col", pairs)

    def core_swap(value):
        return permute(value, lambda k, z, x: (1 - k, z, x))

    def up(value):
        return permute(value, lambda k, z, x: (k, z + 1, x))

    def down(value):
        return permute(value, lambda k, z, x: (k, z - 1, x))

    def across(value):
        return permute(value, lambda k, z, x: (k, z, 1 - x))

    def half_of(which):
        picked = [lax.dynamic_slice_in_dim(v.T, which * half, half, 1) for v in (panel_one, panel_two)]
        return jnp.concatenate(picked, axis=0)

    a_own = half_of(core)
    b_own = core_swap(half_of(1 - core))
    own = jnp.concatenate([a_own, b_own], axis=0)
    a_away, a_below, a_above = across(a_own), up(a_own), down(a_own)
    b_own, other = lax.optimization_barrier((b_own, core_swap(vectors)))
    b_away, b_below, b_above = across(b_own), up(b_own), down(b_own)
    near = (a_own, b_own, a_below, b_below, a_above, b_above, a_away, b_away)

    def early_half(*values):
        return [v[:, :quarter] for v in values]

    def late_half(*values):
        return [v[:, quarter:] for v in values]

    to_up = jnp.concatenate(early_half(a_below, b_below, a_away, b_away), axis=0)
    to_down = jnp.concatenate(
        late_half(a_above, b_above) + early_half(a_away, b_away), axis=0
    )
    to_across = jnp.concatenate(late_half(a_below, b_below, a_above, b_above), axis=0)
    sent_up, sent_down, sent_across = up(to_up), down(to_down), across(to_across)

    chips = []
    for x_step, z_step in ((0, 0), (0, -1), (0, 1), (1, 0), (0, 2), (1, -1), (1, 1), (1, 2)):
        chips.append(jnp.bitwise_xor(plane, x_step) * DEPTH + (depth + z_step) % DEPTH)
    where = jnp.stack(chips + [core]).astype(jnp.int32)

    turn = steps // 2
    whole = [pl.BlockSpec((chunk // 2, TILE), lambda j, w: (0, j))] * 8

    def early(lines):
        return pl.BlockSpec((lines, TILE), lambda j, w: (0, jnp.minimum(j, turn - 1)))

    def late(lines):
        return pl.BlockSpec((lines, TILE), lambda j, w: (0, jnp.maximum(j - turn, 0)))

    both = pl.BlockSpec(
        (chunk, TILE), lambda j, w: (jnp.where(j < turn, 1, 0), jnp.where(j < turn, j, j - turn))
    )
    parts_far = [early(2 * chunk), both, late(2 * chunk), early(chunk), late(chunk)]
    own_spec = pl.BlockSpec((TILE, columns), lambda j, w: (w[CHIPS] * steps + j, 0))
    length = size + 5 * WIDE
    span = size // 2

    def gram(first, pieces, extra):
        if first:
            shapes = [jax.ShapeDtypeStruct((2, span + 3 * WIDE, WIDE), F32)]
        else:
            shapes = [jax.ShapeDtypeStruct((length, WIDE), F32)] * 2
        height = span if first else size
        units = 10 if first else 16
        return pl.pallas_call(
            functools.partial(gram_kernel, first=first),
            out_shape=shapes,
            grid_spec=pltpu.PrefetchScalarGridSpec(
                num_scalar_prefetch=1,
                grid=(steps,),
                in_specs=whole
                + ([] if first else parts_far)
                + [own_spec, own_spec]
                + [pl.BlockSpec(v.shape, lambda j, w: (0, 0, 0)) for v in extra],
                out_specs=[
                    pl.BlockSpec(v.shape, lambda j, w, n=len(v.shape): (0,) * n) for v in shapes
                ],
                scratch_shapes=[pltpu.VMEM((height, TILE), BF16)] * 2
                + [
                    pltpu.VMEM((height, span), F32),
                    pltpu.VMEM((span, span), F32),
                    pltpu.VMEM((span, 2 * WIDE), F32),
                ],
            ),
            compiler_params=pltpu.CompilerParams(
                dimension_semantics=("arbitrary",), vmem_limit_bytes=LIMIT
            ),
            cost_estimate=pl.CostEstimate(
                flops=2 * 3 * units * span * span * half,
                bytes_accessed=4 * half * (height + columns * 2),
                transcendentals=0,
            ),
            name="gram_near" if first else "gram_far",
        )(where, *pieces, vectors, other, *extra)

    (before,) = gram(True, near, ())
    before, sent_up, sent_down = lax.optimization_barrier((before, sent_up, sent_down))
    end_up = up(sent_up[chunk:])
    end_across = across(sent_down[:chunk])
    far = (sent_up, sent_down, sent_across, end_up, end_across)
    kept, sent = gram(False, near + far, (before,))
    mine = kept + core_swap(sent)
    members = lax.axis_size("row")
    parts = lax.all_to_all(mine.reshape(members, length // members, WIDE), "row", 0, 0)
    total = jnp.sum(parts, axis=0)
    spread = jnp.broadcast_to(total[None], (members,) + total.shape)
    mine = lax.all_to_all(spread, "row", 0, 0).reshape(length, WIDE)
    theirs = core_swap(mine)

    *held, vectors_held, other_held = [
        pltpu.with_memory_space_constraint(v, pltpu.HBM) for v in near + far + (vectors, other)
    ]
    result_own, result_other = pl.pallas_call(
        apply_kernel,
        out_shape=[jax.ShapeDtypeStruct((half, columns), F32)] * 2,
        grid_spec=pltpu.PrefetchScalarGridSpec(
            num_scalar_prefetch=1,
            grid=(steps,),
            in_specs=whole
            + parts_far
            + [own_spec, own_spec]
            + [pl.BlockSpec((length, WIDE), lambda j, w: (0, 0))] * 2,
            out_specs=[pl.BlockSpec((TILE, columns), lambda j, w: (j, 0))] * 2,
            scratch_shapes=[pltpu.VMEM((size, 2 * WIDE), F32)]
            + [pltpu.VMEM((size, 2 * WIDE), BF16)] * 2
            + [pltpu.VMEM((size, TILE), F32), pltpu.VMEM((2, length, WIDE), F32)]
            + [pltpu.VMEM((size, size), F32)] * 2
            + [pltpu.VMEM((size, 2 * WIDE), F32)],
        ),
        compiler_params=pltpu.CompilerParams(
            dimension_semantics=("arbitrary",), vmem_limit_bytes=LIMIT
        ),
        name="solve_apply",
    )(where, *held, vectors_held, other_held, mine, theirs)

    returned = core_swap(result_other)
    result = jnp.zeros((rows, columns), F32)
    result = lax.dynamic_update_slice_in_dim(result, result_own, core * half, 0)
    return lax.dynamic_update_slice_in_dim(result, returned, (1 - core) * half, 0)


def solution(mesh):
    specs = (P("row", "col"), P("row", "col"), P("row", "col"))
    return jax.shard_map(
        per_device, mesh=mesh, in_specs=specs, out_specs=P("row", "col"), check_vma=False
    )
```

```python
import functools

import jax
import jax.numpy as jnp
from jax import lax
from jax.experimental import pallas as pl
from jax.experimental.pallas import tpu as pltpu
from jax.sharding import PartitionSpec as P

F32 = jnp.float32
BF16 = jnp.bfloat16
HIGHEST = lax.Precision.HIGHEST
PLANES, DEPTH, CORES = 2, 4, 2
CHIPS = PLANES * DEPTH
WIDE = 128
TILE = 2048
LIMIT = 32 << 20
PIECES = ((0, 0), (0, 1), (1, 1), (0, 2), (0, 3)), ((1, 2), (1, 3), (2, 2), (2, 3), (3, 3))


def split2(value):
    high = value.astype(BF16)
    return high, (value - high.astype(F32)).astype(BF16)


def nn(left, right):
    return lax.dot_general(left, right, (((1,), (0,)), ((), ())), preferred_element_type=F32)


def nt(left, right):
    return lax.dot_general(left, right, (((1,), (1,)), ((), ())), preferred_element_type=F32)


def full(left, right):
    return lax.dot_general(
        left, right, (((1,), (0,)), ((), ())), precision=HIGHEST, preferred_element_type=F32
    )


def each_middle(early, refs, place):
    up_ref, down_ref, across_ref = refs
    chunk = down_ref.shape[0]

    @pl.when(early)
    def _():
        place(4, up_ref[:chunk])
        place(5, up_ref[chunk:])
        place(6, down_ref[...])

    @pl.when(jnp.logical_not(early))
    def _():
        place(4, down_ref[...])
        place(5, across_ref[:chunk])
        place(6, across_ref[chunk:])


def each_last(early, refs, place):
    @pl.when(early)
    def _():
        place(7, refs[0][...])

    @pl.when(jnp.logical_not(early))
    def _():
        place(7, refs[1][...])


def each_far(step, steps, refs, place):
    each_middle(step < steps // 2, refs[:3], place)
    each_last(step < steps // 2, refs[3:], place)


def placer(core, lines, high, low):
    def place_half(slot, swap, value):
        begin = pl.multiple_of(slot * 2 * lines + lines * (core ^ swap), lines)
        for target, part in zip((high, low), split2(value)):
            target[pl.ds(begin, lines), :] = part

    def place(slot, value):
        place_half(slot, 0, value[:lines])
        place_half(slot, 1, value[lines:])

    return place_half, place


def gram_kernel(where_ref, *refs, first):
    steps = pl.num_programs(0)
    step = pl.program_id(0)
    count = 8 if first else 11
    panels = refs[:count]
    own_ref, other_ref, out_ref, high, low, even, skew, proj = refs[count:]
    core = where_ref[CHIPS]
    half = even.shape[1]
    start_row = high.shape[0] - half
    place_half, place = placer(core, panels[0].shape[0], high, low)

    @pl.when(step == 0)
    def _():
        even[...] = jnp.zeros_like(even)
        skew[...] = jnp.zeros_like(skew)
        proj[...] = jnp.zeros_like(proj)
        if not first:
            empty = half // 4
            high[2 * half - empty :, :] = jnp.zeros((empty, high.shape[1]), BF16)
            low[2 * half - empty :, :] = jnp.zeros((empty, low.shape[1]), BF16)

    for index in range(8):
        place_half(index // 2, index % 2, panels[index][...])
    if not first:
        each_middle(step < steps // 2, panels[8:], place)

    one, two = high[start_row:, :], low[start_row:, :]
    skew[...] += nt(one, two)
    if first:
        even[...] += nt(one, one)
    else:
        even[half:, :] += nt(one, one)
        one_a, two_a = high[:half, :], low[:half, :]
        even[:half, :] += (nt(one_a, two) + nt(two_a, one)) + nt(one_a, one)
    x_one, x_two = split2(jnp.concatenate([own_ref[...], other_ref[...]], axis=1))
    proj[...] += (nn(one, x_two) + nn(two, x_one)) + nn(one, x_one)

    @pl.when(step == steps - 1)
    def _():
        out_ref[0:half, :] = proj[...]
        out_ref[half : 2 * half, :] = even[start_row:, :] + (skew[...] + skew[...].T)
        if not first:
            out_ref[2 * half :, :] = even[:half, :]


def last_kernel(where_ref, *refs):
    steps = pl.num_programs(0)
    step = pl.program_id(0)
    panels = refs[:13]
    own_ref, other_ref, near_ref, middle_ref, keep_ref, send_ref, high, low, gram, proj = refs[13:]
    core = where_ref[CHIPS]
    size = gram.shape[1]
    half = size // 2
    chunk = gram.shape[0]
    place_half, place = placer(core, panels[0].shape[0], high, low)
    for index in range(8):
        place_half(index // 2, index % 2, panels[index][...])
    each_far(step, steps, panels[8:], place)

    @pl.when(step == 0)
    def _():
        gram[...] = jnp.zeros_like(gram)
        proj[...] = jnp.zeros_like(proj)

    one, two = high[...], low[...]
    last, rest = one[size - chunk :], two[size - chunk :]
    pair = jnp.concatenate([last, rest], axis=0)
    partial = nt(pair, one)
    gram[...] += nt(last, two) + (partial[chunk:] + partial[:chunk])
    x_one, x_two = split2(jnp.concatenate([own_ref[...], other_ref[...]], axis=1))
    partial = nn(pair, x_one)
    proj[...] += nn(last, x_two) + (partial[chunk:] + partial[:chunk])

    @pl.when(step == steps - 1)
    def _():
        for target, lanes in ((keep_ref, slice(0, WIDE)), (send_ref, slice(WIDE, 2 * WIDE))):
            target[0:half, :] = near_ref[0:half, lanes]
            target[half : size - chunk, :] = middle_ref[0 : half - chunk, lanes]
            target[size - chunk : size, :] = proj[:, lanes]

        def spot(ref, base, i, j):
            return ref[base + i * WIDE : base + (i + 1) * WIDE, j * WIDE : (j + 1) * WIDE]

        def lower(j):
            return jnp.concatenate(
                [jnp.zeros((WIDE - chunk, WIDE), F32), gram[:, j * WIDE : (j + 1) * WIDE]], axis=0
            )

        lane = lax.broadcasted_iota(jnp.int32, (WIDE, WIDE), 1)

        def blocks(part, target):
            for at, (i, j) in enumerate(PIECES[part]):
                begin = size + at * WIDE
                if j < 2:
                    block = spot(near_ref, half, i, j)
                elif i < 2:
                    block = spot(middle_ref, 2 * half, i, j - 2)
                else:
                    block = spot(middle_ref, half, i - 2, j - 2)
                if j == 3:
                    added = lower(i)
                    if i == 3:
                        block = block + added
                        added = jnp.where(lane < WIDE - chunk, added, 0.0)
                    block = block + added.T
                target[begin : begin + WIDE, :] = block

        @pl.when(core == 0)
        def _():
            blocks(0, keep_ref)
            blocks(1, send_ref)

        @pl.when(core != 0)
        def _():
            blocks(1, keep_ref)
            blocks(0, send_ref)


def solve(where_ref, mine_ref, other_ref, solved_ref, both, rows_done, ordered, sides):
    core = where_ref[CHIPS]
    both[core] = mine_ref[...]
    both[1 - core] = other_ref[...]
    count = 4
    size = count * WIDE
    panel = size // 2
    base = 16

    def relative(i, j):
        for part in range(2):
            if (i, j) in PIECES[part]:
                start = size + PIECES[part].index((i, j)) * WIDE
                return both[part, start : start + WIDE, :]

    group = size // (2 * CORES * CHIPS)

    def target(index):
        slot, at_core, part = index // (2 * CORES), (index // 2) % CORES, index % 2
        start = part * panel + where_ref[slot] * CORES * group + at_core * group
        return pl.ds(pl.multiple_of(start, group), group)

    for i in range(count):
        strip = jnp.concatenate(
            [relative(i, j) if i <= j else relative(j, i).T for j in range(count)], axis=1
        )
        for k in range(WIDE // group):
            rows_done[target(i * (WIDE // group) + k), :] = strip[k * group : (k + 1) * group]
    for i in range(count):
        strip = jnp.concatenate(
            [
                rows_done[j * WIDE : (j + 1) * WIDE, i * WIDE : (i + 1) * WIDE].T
                for j in range(count)
            ],
            axis=1,
        )
        for k in range(WIDE // group):
            ordered[target(i * (WIDE // group) + k), :] = strip[k * group : (k + 1) * group]
    for index in range(size // group):
        at = slice(index * group, (index + 1) * group)
        sides[target(index), :] = jnp.concatenate([mine_ref[at, :], other_ref[at, :]], axis=1)

    def block(i, j):
        return ordered[i * WIDE : (i + 1) * WIDE, j * WIDE : (j + 1) * WIDE]

    row = lax.broadcasted_iota(jnp.int32, (WIDE, WIDE), 0)
    column = lax.broadcasted_iota(jnp.int32, (WIDE, WIDE), 1)
    same = (row // base) == (column // base)
    diagonals = []
    for i in range(count):
        value = block(i, i)
        diagonals.append(
            jnp.where(row < column, value, jnp.where(row == column, value * 0.5, 0.0))
        )
    lane = lax.broadcasted_iota(jnp.int32, (base, WIDE), 1) % base
    ones = jnp.where(same, 1.0, 0.0).astype(F32)
    spread = []
    for i in range(count):
        flipped = jnp.where(same, diagonals[i], 0.0).T
        folded = flipped[0:base]
        for k in range(1, WIDE // base):
            folded = folded + flipped[k * base : (k + 1) * base]
        stacked = jnp.concatenate([jnp.where(lane == k, folded, 0.0) for k in range(base)], axis=0)
        spread.append(full(stacked, ones))
    wide_lane = lax.broadcasted_iota(jnp.int32, (1, size), 1) % base
    wide_row = lax.broadcasted_iota(jnp.int32, (base, size), 0)
    solved = jnp.zeros((base, size), F32)
    for i in range(base - 1, -1, -1):
        factor = jnp.concatenate([s[i * base : (i + 1) * base] for s in spread], axis=1)
        total = jnp.sum(factor * solved, axis=0, keepdims=True)
        line = (jnp.where(wide_lane == i, 1.0, 0.0) - total) / factor[i : i + 1]
        solved = jnp.where(wide_row == i, line, solved)

    def three(left, right):
        return (nn(left[0], right[1]) + nn(left[1], right[0])) + nn(left[0], right[0])

    small = []
    for i in range(count):
        tiled = jnp.concatenate([solved[:, i * WIDE : (i + 1) * WIDE]] * (WIDE // base), axis=0)
        small.append(jnp.where(same, tiled, 0.0))
    width = base
    while width < WIDE:
        picked = ((row // width) % 2 == 0) & (column // width == row // width + 1)
        for i in range(count):
            inverse = split2(small[i])
            coupling = split2(jnp.where(picked, diagonals[i], 0.0))
            small[i] = small[i] - three(split2(three(inverse, coupling)), inverse)
        width *= 2
    inverses = []
    for half in range(2):
        left, right = small[2 * half], small[2 * half + 1]
        coupling = split2(block(2 * half, 2 * half + 1))
        corner = -three(split2(three(split2(left), coupling)), split2(right))
        top = jnp.concatenate([left, corner], axis=1)
        bottom = jnp.concatenate([jnp.zeros((WIDE, WIDE), F32), right], axis=1)
        inverses.append(split2(jnp.concatenate([top, bottom], axis=0)))
    corner = jnp.concatenate(
        [
            jnp.concatenate([block(0, 2), block(0, 3)], axis=1),
            jnp.concatenate([block(1, 2), block(1, 3)], axis=1),
        ],
        axis=0,
    )
    right_side = sides[...]
    second = three(inverses[1], split2(right_side[panel:]))
    first = three(
        inverses[0], split2(right_side[:panel] - three(split2(corner), split2(second)))
    )
    solved_ref[0:panel, :] = first
    solved_ref[panel:, :] = second


def apply_kernel(where_ref, *refs):
    step = pl.program_id(0)
    steps = pl.num_programs(0)
    panels = refs[:13]
    current_own, current_other, mine_ref, theirs_ref, out_own, out_other = refs[13:19]
    solved, high, low, merged, both, rows_done, ordered, sides = refs[19:]
    core = where_ref[CHIPS]
    panel = solved.shape[0] // 2
    chunk = 2 * panels[0].shape[0]
    group = chunk // 4

    @pl.when(step == 0)
    def _():
        solve(where_ref, mine_ref, theirs_ref, solved, both, rows_done, ordered, sides)
        for index in range(2 * CHIPS):
            chip = where_ref[index // 2]
            for part in range(2):
                start = pl.multiple_of(
                    part * panel + chip * 2 * group + group * (core ^ (index % 2)), group
                )
                at = (2 * index + part) * group
                for target, value in zip((high, low), split2(solved[pl.ds(start, group), :])):
                    target[at : at + group, :] = value

    def place(slot, value):
        merged[slot * chunk : (slot + 1) * chunk, :] = value

    for index in range(8):
        merged[index * chunk // 2 : (index + 1) * chunk // 2, :] = panels[index][...]
    each_far(step, steps, panels[8:], place)
    one, two = split2(merged[...])
    first, second = high[...], low[...]

    def tn(left, right):
        return lax.dot_general(left, right, (((0,), (0,)), ((), ())), preferred_element_type=F32)

    change = (tn(one, second) + tn(two, first)) + tn(one, first)
    out_own[...] = current_own[...] - change[:, :WIDE]
    out_other[...] = current_other[...] - change[:, WIDE:]


def per_device(vectors, panel_one, panel_two):
    rows, columns = vectors.shape
    group = panel_one.shape[1]
    half = rows // 2
    size = 2 * group * CHIPS * CORES
    quarter = half // 2
    chunk = 4 * group
    steps = half // TILE
    at = lax.axis_index("col")
    core, depth, plane = at % CORES, (at // CORES) % DEPTH, at // (CORES * DEPTH)

    def permute(value, move):
        pairs = []
        for source in range(CHIPS * CORES):
            k, z, x = source % CORES, (source // CORES) % DEPTH, source // (CORES * DEPTH)
            k, z, x = move(k, z, x)
            pairs.append((source, (x * DEPTH + z % DEPTH) * CORES + k))
        return lax.ppermute(value, "col", pairs)

    def core_swap(value):
        return permute(value, lambda k, z, x: (1 - k, z, x))

    def up(value):
        return permute(value, lambda k, z, x: (k, z + 1, x))

    def down(value):
        return permute(value, lambda k, z, x: (k, z - 1, x))

    def across(value):
        return permute(value, lambda k, z, x: (k, z, 1 - x))

    def half_of(which):
        picked = [lax.dynamic_slice_in_dim(v.T, which * half, half, 1) for v in (panel_one, panel_two)]
        return jnp.concatenate(picked, axis=0)

    a_own = half_of(core)
    b_own = core_swap(half_of(1 - core))
    own = jnp.concatenate([a_own, b_own], axis=0)
    a_away, a_below, a_above = across(a_own), up(a_own), down(a_own)
    b_own, other = lax.optimization_barrier((b_own, core_swap(vectors)))
    b_away, b_below, b_above = across(b_own), up(b_own), down(b_own)
    near = (a_own, b_own, a_below, b_below, a_above, b_above, a_away, b_away)

    def early_half(*values):
        return [v[:, :quarter] for v in values]

    def late_half(*values):
        return [v[:, quarter:] for v in values]

    to_up = jnp.concatenate(early_half(a_below, b_below, a_away, b_away), axis=0)
    to_down = jnp.concatenate(
        late_half(a_above, b_above) + early_half(a_away, b_away), axis=0
    )
    to_across = jnp.concatenate(late_half(a_below, b_below, a_above, b_above), axis=0)
    sent_up, sent_down, sent_across = up(to_up), down(to_down), across(to_across)

    chips = []
    for x_step, z_step in ((0, 0), (0, -1), (0, 1), (1, 0), (0, 2), (1, -1), (1, 1), (1, 2)):
        chips.append(jnp.bitwise_xor(plane, x_step) * DEPTH + (depth + z_step) % DEPTH)
    where = jnp.stack(chips + [core]).astype(jnp.int32)

    turn = steps // 2
    whole = [pl.BlockSpec((chunk // 2, TILE), lambda j, w: (0, j))] * 8

    def early(lines):
        return pl.BlockSpec((lines, TILE), lambda j, w: (0, jnp.minimum(j, turn - 1)))

    def late(lines):
        return pl.BlockSpec((lines, TILE), lambda j, w: (0, jnp.maximum(j - turn, 0)))

    both = pl.BlockSpec(
        (chunk, TILE), lambda j, w: (jnp.where(j < turn, 1, 0), jnp.where(j < turn, j, j - turn))
    )
    parts_far = [early(2 * chunk), both, late(2 * chunk), early(chunk), late(chunk)]
    own_spec = pl.BlockSpec((TILE, columns), lambda j, w: (w[CHIPS] * steps + j, 0))
    length = size + 5 * WIDE
    span = size // 2

    def products(kernel, pieces, specs, extra, shapes, scratch, units, name):
        return pl.pallas_call(
            kernel,
            out_shape=[jax.ShapeDtypeStruct(v, F32) for v in shapes],
            grid_spec=pltpu.PrefetchScalarGridSpec(
                num_scalar_prefetch=1,
                grid=(steps,),
                in_specs=specs
                + [own_spec, own_spec]
                + [pl.BlockSpec(v.shape, lambda j, w: (0, 0)) for v in extra],
                out_specs=[pl.BlockSpec(v, lambda j, w: (0, 0)) for v in shapes],
                scratch_shapes=scratch,
            ),
            compiler_params=pltpu.CompilerParams(
                dimension_semantics=("arbitrary",), vmem_limit_bytes=LIMIT
            ),
            cost_estimate=pl.CostEstimate(
                flops=2 * 3 * units * span * span * half,
                bytes_accessed=4 * half * (size + columns * 2),
                transcendentals=0,
            ),
            name=name,
        )(where, *pieces, vectors, other, *extra)

    def split_scratch(height):
        return [pltpu.VMEM((height, TILE), BF16)] * 2

    square = pltpu.VMEM((span, span), F32)
    (before,) = products(
        functools.partial(gram_kernel, first=True), near, whole, (),
        [(2 * span, span)], split_scratch(span) + [square] * 3, 10, "gram_near",
    )
    before, sent_up, sent_down = lax.optimization_barrier((before, sent_up, sent_down))
    end_up = up(sent_up[chunk:])
    end_across = across(sent_down[:chunk])
    middle = (sent_up, sent_down, sent_across)
    (between,) = products(
        functools.partial(gram_kernel, first=False), near + middle, whole + parts_far[:3], (),
        [(3 * span, span)],
        split_scratch(size) + [pltpu.VMEM((size, span), F32), square, square], 16, "gram_middle",
    )
    end_up, end_across, between = lax.optimization_barrier((end_up, end_across, between))
    far = middle + (end_up, end_across)
    kept, sent = products(
        last_kernel, near + far, whole + parts_far, (before, between),
        [(length, WIDE)] * 2,
        split_scratch(size) + [pltpu.VMEM((chunk, size), F32), pltpu.VMEM((chunk, span), F32)],
        8, "gram_last",
    )
    mine = kept + core_swap(sent)
    members = lax.axis_size("row")
    parts = lax.all_to_all(mine.reshape(members, length // members, WIDE), "row", 0, 0)
    total = jnp.sum(parts, axis=0)
    spread = jnp.broadcast_to(total[None], (members,) + total.shape)
    mine = lax.all_to_all(spread, "row", 0, 0).reshape(length, WIDE)
    theirs = core_swap(mine)

    *held, vectors_held, other_held = [
        pltpu.with_memory_space_constraint(v, pltpu.HBM) for v in near + far + (vectors, other)
    ]
    result_own, result_other = pl.pallas_call(
        apply_kernel,
        out_shape=[jax.ShapeDtypeStruct((half, columns), F32)] * 2,
        grid_spec=pltpu.PrefetchScalarGridSpec(
            num_scalar_prefetch=1,
            grid=(steps,),
            in_specs=whole
            + parts_far
            + [own_spec, own_spec]
            + [pl.BlockSpec((length, WIDE), lambda j, w: (0, 0))] * 2,
            out_specs=[pl.BlockSpec((TILE, columns), lambda j, w: (j, 0))] * 2,
            scratch_shapes=[pltpu.VMEM((size, 2 * WIDE), F32)]
            + [pltpu.VMEM((size, 2 * WIDE), BF16)] * 2
            + [pltpu.VMEM((size, TILE), F32), pltpu.VMEM((2, length, WIDE), F32)]
            + [pltpu.VMEM((size, size), F32)] * 2
            + [pltpu.VMEM((size, 2 * WIDE), F32)],
        ),
        compiler_params=pltpu.CompilerParams(
            dimension_semantics=("arbitrary",), vmem_limit_bytes=LIMIT
        ),
        name="solve_apply",
    )(where, *held, vectors_held, other_held, mine, theirs)

    returned = core_swap(result_other)
    result = jnp.zeros((rows, columns), F32)
    result = lax.dynamic_update_slice_in_dim(result, result_own, core * half, 0)
    return lax.dynamic_update_slice_in_dim(result, returned, (1 - core) * half, 0)


def solution(mesh):
    specs = (P("row", "col"), P("row", "col"), P("row", "col"))
    return jax.shard_map(
        per_device, mesh=mesh, in_specs=specs, out_specs=P("row", "col"), check_vma=False
    )
```

```python
import functools

import jax
import jax.numpy as jnp
from jax import lax
from jax.experimental import pallas as pl
from jax.experimental.pallas import tpu as pltpu
from jax.sharding import PartitionSpec as P

F32 = jnp.float32
BF16 = jnp.bfloat16
HIGHEST = lax.Precision.HIGHEST
PLANES, DEPTH, CORES = 2, 4, 2
CHIPS = PLANES * DEPTH
WIDE = 128
TILE = 2048
LIMIT = 32 << 20
PIECES = ((0, 0), (0, 1), (1, 1), (0, 2), (0, 3)), ((1, 2), (1, 3), (2, 2), (2, 3), (3, 3))


def split2(value):
    high = value.astype(BF16)
    return high, (value - high.astype(F32)).astype(BF16)


def nn(left, right):
    return lax.dot_general(left, right, (((1,), (0,)), ((), ())), preferred_element_type=F32)


def nt(left, right):
    return lax.dot_general(left, right, (((1,), (1,)), ((), ())), preferred_element_type=F32)


def full(left, right):
    return lax.dot_general(
        left, right, (((1,), (0,)), ((), ())), precision=HIGHEST, preferred_element_type=F32
    )


def each_middle(early, refs, place):
    up_ref, down_ref, across_ref = refs
    chunk = down_ref.shape[0]

    @pl.when(early)
    def _():
        place(4, up_ref[:chunk])
        place(5, up_ref[chunk:])
        place(6, down_ref[...])

    @pl.when(jnp.logical_not(early))
    def _():
        place(4, down_ref[...])
        place(5, across_ref[:chunk])
        place(6, across_ref[chunk:])


def each_last(early, refs, place):
    @pl.when(early)
    def _():
        place(7, refs[0][...])

    @pl.when(jnp.logical_not(early))
    def _():
        place(7, refs[1][...])


def each_far(step, steps, refs, place):
    each_middle(step < steps // 2, refs[:3], place)
    each_last(step < steps // 2, refs[3:], place)


def placer(core, lines, high, low):
    def place_half(slot, swap, value):
        begin = pl.multiple_of(slot * 2 * lines + lines * (core ^ swap), lines)
        for target, part in zip((high, low), split2(value)):
            target[pl.ds(begin, lines), :] = part

    def place(slot, value):
        place_half(slot, 0, value[:lines])
        place_half(slot, 1, value[lines:])

    return place_half, place


def gram_kernel(where_ref, *refs, first):
    steps = pl.num_programs(0)
    step = pl.program_id(0)
    count = 8 if first else 11
    panels = refs[:count]
    own_ref, other_ref, out_ref, high, low, even, skew, proj = refs[count:]
    core = where_ref[CHIPS]
    half = even.shape[1]
    start_row = high.shape[0] - half
    place_half, place = placer(core, panels[0].shape[0], high, low)

    @pl.when(step == 0)
    def _():
        even[...] = jnp.zeros_like(even)
        skew[...] = jnp.zeros_like(skew)
        proj[...] = jnp.zeros_like(proj)
        if not first:
            empty = half // 4
            high[2 * half - empty :, :] = jnp.zeros((empty, high.shape[1]), BF16)
            low[2 * half - empty :, :] = jnp.zeros((empty, low.shape[1]), BF16)

    for index in range(8):
        place_half(index // 2, index % 2, panels[index][...])
    if not first:
        each_middle(step < steps // 2, panels[8:], place)

    one, two = high[start_row:, :], low[start_row:, :]
    skew[...] += nt(one, two)
    if first:
        even[...] += nt(one, one)
    else:
        even[half:, :] += nt(one, one)
        one_a, two_a = high[:half, :], low[:half, :]
        even[:half, :] += (nt(one_a, two) + nt(two_a, one)) + nt(one_a, one)
    x_one, x_two = split2(jnp.concatenate([own_ref[...], other_ref[...]], axis=1))
    proj[...] += (nn(one, x_two) + nn(two, x_one)) + nn(one, x_one)

    @pl.when(step == steps - 1)
    def _():
        out_ref[0:half, :] = proj[...]
        out_ref[half : 2 * half, :] = even[start_row:, :] + (skew[...] + skew[...].T)
        if not first:
            out_ref[2 * half :, :] = even[:half, :]


def last_kernel(where_ref, *refs):
    steps = pl.num_programs(0)
    step = pl.program_id(0)
    panels = refs[:13]
    own_ref, other_ref, near_ref, middle_ref, keep_ref, send_ref, high, low, gram, proj = refs[13:]
    core = where_ref[CHIPS]
    size = gram.shape[1]
    half = size // 2
    chunk = gram.shape[0]
    place_half, place = placer(core, panels[0].shape[0], high, low)
    for index in range(8):
        place_half(index // 2, index % 2, panels[index][...])
    each_far(step, steps, panels[8:], place)

    @pl.when(step == 0)
    def _():
        gram[...] = jnp.zeros_like(gram)
        proj[...] = jnp.zeros_like(proj)

    one, two = high[...], low[...]
    last, rest = one[size - chunk :], two[size - chunk :]
    pair = jnp.concatenate([last, rest], axis=0)
    partial = nt(pair, one)
    gram[...] += nt(last, two) + (partial[chunk:] + partial[:chunk])
    x_one, x_two = split2(jnp.concatenate([own_ref[...], other_ref[...]], axis=1))
    partial = nn(pair, x_one)
    proj[...] += nn(last, x_two) + (partial[chunk:] + partial[:chunk])

    @pl.when(step == steps - 1)
    def _():
        for target, lanes in ((keep_ref, slice(0, WIDE)), (send_ref, slice(WIDE, 2 * WIDE))):
            target[0:half, :] = near_ref[0:half, lanes]
            target[half : size - chunk, :] = middle_ref[0 : half - chunk, lanes]
            target[size - chunk : size, :] = proj[:, lanes]

        def spot(ref, base, i, j):
            return ref[base + i * WIDE : base + (i + 1) * WIDE, j * WIDE : (j + 1) * WIDE]

        def lower(j):
            return jnp.concatenate(
                [jnp.zeros((WIDE - chunk, WIDE), F32), gram[:, j * WIDE : (j + 1) * WIDE]], axis=0
            )

        lane = lax.broadcasted_iota(jnp.int32, (WIDE, WIDE), 1)

        def blocks(part, target):
            for at, (i, j) in enumerate(PIECES[part]):
                begin = size + at * WIDE
                if j < 2:
                    block = spot(near_ref, half, i, j)
                elif i < 2:
                    block = spot(middle_ref, 2 * half, i, j - 2)
                else:
                    block = spot(middle_ref, half, i - 2, j - 2)
                if j == 3:
                    added = lower(i)
                    if i == 3:
                        block = block + added
                        added = jnp.where(lane < WIDE - chunk, added, 0.0)
                    block = block + added.T
                target[begin : begin + WIDE, :] = block

        @pl.when(core == 0)
        def _():
            blocks(0, keep_ref)
            blocks(1, send_ref)

        @pl.when(core != 0)
        def _():
            blocks(1, keep_ref)
            blocks(0, send_ref)


def solve(where_ref, mine_ref, other_ref, solved_ref, both, rows_done, ordered, sides):
    core = where_ref[CHIPS]
    both[core] = mine_ref[...]
    both[1 - core] = other_ref[...]
    count = 4
    size = count * WIDE
    panel = size // 2
    base = 16

    def relative(i, j):
        for part in range(2):
            if (i, j) in PIECES[part]:
                start = size + PIECES[part].index((i, j)) * WIDE
                return both[part, start : start + WIDE, :]

    group = size // (2 * CORES * CHIPS)

    def target(index):
        slot, at_core, part = index // (2 * CORES), (index // 2) % CORES, index % 2
        start = part * panel + where_ref[slot] * CORES * group + at_core * group
        return pl.ds(pl.multiple_of(start, group), group)

    for i in range(count):
        strip = jnp.concatenate(
            [relative(i, j) if i <= j else relative(j, i).T for j in range(count)], axis=1
        )
        for k in range(WIDE // group):
            rows_done[target(i * (WIDE // group) + k), :] = strip[k * group : (k + 1) * group]
    for i in range(count):
        strip = jnp.concatenate(
            [
                rows_done[j * WIDE : (j + 1) * WIDE, i * WIDE : (i + 1) * WIDE].T
                for j in range(count)
            ],
            axis=1,
        )
        for k in range(WIDE // group):
            ordered[target(i * (WIDE // group) + k), :] = strip[k * group : (k + 1) * group]
    for index in range(size // group):
        at = slice(index * group, (index + 1) * group)
        sides[target(index), :] = jnp.concatenate([mine_ref[at, :], other_ref[at, :]], axis=1)

    def block(i, j):
        return ordered[i * WIDE : (i + 1) * WIDE, j * WIDE : (j + 1) * WIDE]

    row = lax.broadcasted_iota(jnp.int32, (WIDE, WIDE), 0)
    column = lax.broadcasted_iota(jnp.int32, (WIDE, WIDE), 1)
    same = (row // base) == (column // base)
    diagonals = []
    for i in range(count):
        value = block(i, i)
        diagonals.append(
            jnp.where(row < column, value, jnp.where(row == column, value * 0.5, 0.0))
        )
    lane = lax.broadcasted_iota(jnp.int32, (base, WIDE), 1) % base
    ones = jnp.where(same, 1.0, 0.0).astype(F32)
    spread = []
    for i in range(count):
        flipped = jnp.where(same, diagonals[i], 0.0).T
        folded = flipped[0:base]
        for k in range(1, WIDE // base):
            folded = folded + flipped[k * base : (k + 1) * base]
        stacked = jnp.concatenate([jnp.where(lane == k, folded, 0.0) for k in range(base)], axis=0)
        spread.append(full(stacked, ones))
    wide_lane = lax.broadcasted_iota(jnp.int32, (1, size), 1) % base
    wide_row = lax.broadcasted_iota(jnp.int32, (base, size), 0)
    solved = jnp.zeros((base, size), F32)
    for i in range(base - 1, -1, -1):
        factor = jnp.concatenate([s[i * base : (i + 1) * base] for s in spread], axis=1)
        total = jnp.sum(factor * solved, axis=0, keepdims=True)
        line = (jnp.where(wide_lane == i, 1.0, 0.0) - total) / factor[i : i + 1]
        solved = jnp.where(wide_row == i, line, solved)

    def three(left, right):
        return (nn(left[0], right[1]) + nn(left[1], right[0])) + nn(left[0], right[0])

    small = []
    for i in range(count):
        tiled = jnp.concatenate([solved[:, i * WIDE : (i + 1) * WIDE]] * (WIDE // base), axis=0)
        small.append(jnp.where(same, tiled, 0.0))
    width = base
    while width < WIDE:
        picked = ((row // width) % 2 == 0) & (column // width == row // width + 1)
        for i in range(count):
            inverse = split2(small[i])
            coupling = split2(jnp.where(picked, diagonals[i], 0.0))
            small[i] = small[i] - three(split2(three(inverse, coupling)), inverse)
        width *= 2
    inverses = []
    for half in range(2):
        left, right = small[2 * half], small[2 * half + 1]
        coupling = split2(block(2 * half, 2 * half + 1))
        corner = -three(split2(three(split2(left), coupling)), split2(right))
        top = jnp.concatenate([left, corner], axis=1)
        bottom = jnp.concatenate([jnp.zeros((WIDE, WIDE), F32), right], axis=1)
        inverses.append(split2(jnp.concatenate([top, bottom], axis=0)))
    corner = jnp.concatenate(
        [
            jnp.concatenate([block(0, 2), block(0, 3)], axis=1),
            jnp.concatenate([block(1, 2), block(1, 3)], axis=1),
        ],
        axis=0,
    )
    right_side = sides[...]
    second = three(inverses[1], split2(right_side[panel:]))
    first = three(
        inverses[0], split2(right_side[:panel] - three(split2(corner), split2(second)))
    )
    solved_ref[0:panel, :] = first
    solved_ref[panel:, :] = second


def apply_kernel(where_ref, *refs):
    step = pl.program_id(0)
    steps = pl.num_programs(0)
    panels = refs[:13]
    current_own, current_other, mine_ref, theirs_ref, out_own, out_other = refs[13:19]
    solved, high, low, merged, both, rows_done, ordered, sides = refs[19:]
    core = where_ref[CHIPS]
    panel = solved.shape[0] // 2
    chunk = 2 * panels[0].shape[0]
    group = chunk // 4

    @pl.when(step == 0)
    def _():
        solve(where_ref, mine_ref, theirs_ref, solved, both, rows_done, ordered, sides)
        for index in range(2 * CHIPS):
            chip = where_ref[index // 2]
            for part in range(2):
                start = pl.multiple_of(
                    part * panel + chip * 2 * group + group * (core ^ (index % 2)), group
                )
                at = (2 * index + part) * group
                for target, value in zip((high, low), split2(solved[pl.ds(start, group), :])):
                    target[at : at + group, :] = value

    def place(slot, value):
        merged[slot * chunk : (slot + 1) * chunk, :] = value

    for index in range(8):
        merged[index * chunk // 2 : (index + 1) * chunk // 2, :] = panels[index][...]
    each_far(step, steps, panels[8:], place)
    one, two = split2(merged[...])
    first, second = high[...], low[...]

    def tn(left, right):
        return lax.dot_general(left, right, (((0,), (0,)), ((), ())), preferred_element_type=F32)

    change = (tn(one, second) + tn(two, first)) + tn(one, first)
    out_own[...] = current_own[...] - change[:, :WIDE]
    out_other[...] = current_other[...] - change[:, WIDE:]


def per_device(vectors, panel_one, panel_two):
    rows, columns = vectors.shape
    group = panel_one.shape[1]
    half = rows // 2
    size = 2 * group * CHIPS * CORES
    quarter = half // 2
    chunk = 4 * group
    steps = half // TILE
    at = lax.axis_index("col")
    core, depth, plane = at % CORES, (at // CORES) % DEPTH, at // (CORES * DEPTH)

    def permute(value, move):
        pairs = []
        for source in range(CHIPS * CORES):
            k, z, x = source % CORES, (source // CORES) % DEPTH, source // (CORES * DEPTH)
            k, z, x = move(k, z, x)
            pairs.append((source, (x * DEPTH + z % DEPTH) * CORES + k))
        return lax.ppermute(value, "col", pairs)

    def core_swap(value):
        return permute(value, lambda k, z, x: (1 - k, z, x))

    def up(value):
        return permute(value, lambda k, z, x: (k, z + 1, x))

    def down(value):
        return permute(value, lambda k, z, x: (k, z - 1, x))

    def across(value):
        return permute(value, lambda k, z, x: (k, z, 1 - x))

    def half_of(which):
        picked = [lax.dynamic_slice_in_dim(v.T, which * half, half, 1) for v in (panel_one, panel_two)]
        return jnp.concatenate(picked, axis=0)

    a_own = half_of(core)
    b_own = core_swap(half_of(1 - core))
    own = jnp.concatenate([a_own, b_own], axis=0)
    a_away, a_below, a_above = across(a_own), up(a_own), down(a_own)
    b_own, other = lax.optimization_barrier((b_own, core_swap(vectors)))
    b_away, b_below, b_above = across(b_own), up(b_own), down(b_own)
    near = (a_own, b_own, a_below, b_below, a_above, b_above, a_away, b_away)

    def early_half(*values):
        return [v[:, :quarter] for v in values]

    def late_half(*values):
        return [v[:, quarter:] for v in values]

    to_up = jnp.concatenate(early_half(a_below, b_below, a_away, b_away), axis=0)
    to_down = jnp.concatenate(
        late_half(a_above, b_above) + early_half(a_away, b_away), axis=0
    )
    to_across = jnp.concatenate(late_half(a_below, b_below, a_above, b_above), axis=0)
    sent_up, sent_down, sent_across = up(to_up), down(to_down), across(to_across)

    chips = []
    for x_step, z_step in ((0, 0), (0, -1), (0, 1), (1, 0), (0, 2), (1, -1), (1, 1), (1, 2)):
        chips.append(jnp.bitwise_xor(plane, x_step) * DEPTH + (depth + z_step) % DEPTH)
    where = jnp.stack(chips + [core]).astype(jnp.int32)

    turn = steps // 2
    whole = [pl.BlockSpec((chunk // 2, TILE), lambda j, w: (0, j))] * 8

    def early(lines):
        return pl.BlockSpec((lines, TILE), lambda j, w: (0, jnp.minimum(j, turn - 1)))

    def late(lines):
        return pl.BlockSpec((lines, TILE), lambda j, w: (0, jnp.maximum(j - turn, 0)))

    both = pl.BlockSpec(
        (chunk, TILE), lambda j, w: (jnp.where(j < turn, 1, 0), jnp.where(j < turn, j, j - turn))
    )
    parts_far = [early(2 * chunk), both, late(2 * chunk), early(chunk), late(chunk)]
    own_spec = pl.BlockSpec((TILE, columns), lambda j, w: (w[CHIPS] * steps + j, 0))
    length = size + 5 * WIDE
    span = size // 2

    def products(kernel, pieces, specs, extra, shapes, scratch, units, name):
        return pl.pallas_call(
            kernel,
            out_shape=[jax.ShapeDtypeStruct(v, F32) for v in shapes],
            grid_spec=pltpu.PrefetchScalarGridSpec(
                num_scalar_prefetch=1,
                grid=(steps,),
                in_specs=specs
                + [own_spec, own_spec]
                + [pl.BlockSpec(v.shape, lambda j, w: (0, 0)) for v in extra],
                out_specs=[pl.BlockSpec(v, lambda j, w: (0, 0)) for v in shapes],
                scratch_shapes=scratch,
            ),
            compiler_params=pltpu.CompilerParams(
                dimension_semantics=("arbitrary",), vmem_limit_bytes=LIMIT
            ),
            cost_estimate=pl.CostEstimate(
                flops=2 * 3 * units * span * span * half,
                bytes_accessed=4 * half * (size + columns * 2),
                transcendentals=0,
            ),
            name=name,
        )(where, *pieces, vectors, other, *extra)

    def split_scratch(height):
        return [pltpu.VMEM((height, TILE), BF16)] * 2

    square = pltpu.VMEM((span, span), F32)
    (before,) = products(
        functools.partial(gram_kernel, first=True), near, whole, (),
        [(2 * span, span)], split_scratch(span) + [square] * 3, 10, "gram_near",
    )
    before, sent_up, sent_down = lax.optimization_barrier((before, sent_up, sent_down))
    end_up = up(sent_up[chunk:])
    end_across = across(sent_down[:chunk])
    middle = (sent_up, sent_down, sent_across)
    (between,) = products(
        functools.partial(gram_kernel, first=False), near + middle, whole + parts_far[:3], (),
        [(3 * span, span)],
        split_scratch(size) + [pltpu.VMEM((size, span), F32), square, square], 16, "gram_middle",
    )
    end_up, end_across, between = lax.optimization_barrier((end_up, end_across, between))
    far = middle + (end_up, end_across)
    kept, sent = products(
        last_kernel, near + far, whole + parts_far, (before, between),
        [(length, WIDE)] * 2,
        split_scratch(size) + [pltpu.VMEM((chunk, size), F32), pltpu.VMEM((chunk, span), F32)],
        8, "gram_last",
    )
    mine = kept + core_swap(sent)
    members = lax.axis_size("row")
    parts = lax.all_to_all(mine.reshape(members, length // members, WIDE), "row", 0, 0)
    total = jnp.sum(parts, axis=0)
    spread = jnp.broadcast_to(total[None], (members,) + total.shape)
    mine = lax.all_to_all(spread, "row", 0, 0).reshape(length, WIDE)
    theirs = core_swap(mine)

    *held, vectors_held, other_held = [
        pltpu.with_memory_space_constraint(v, pltpu.HBM) for v in near[2:4] + far + (vectors, other)
    ]
    result_own, result_other = pl.pallas_call(
        apply_kernel,
        out_shape=[jax.ShapeDtypeStruct((half, columns), F32)] * 2,
        grid_spec=pltpu.PrefetchScalarGridSpec(
            num_scalar_prefetch=1,
            grid=(steps,),
            in_specs=whole
            + parts_far
            + [own_spec, own_spec]
            + [pl.BlockSpec((length, WIDE), lambda j, w: (0, 0))] * 2,
            out_specs=[pl.BlockSpec((TILE, columns), lambda j, w: (j, 0))] * 2,
            scratch_shapes=[pltpu.VMEM((size, 2 * WIDE), F32)]
            + [pltpu.VMEM((size, 2 * WIDE), BF16)] * 2
            + [pltpu.VMEM((size, TILE), F32), pltpu.VMEM((2, length, WIDE), F32)]
            + [pltpu.VMEM((size, size), F32)] * 2
            + [pltpu.VMEM((size, 2 * WIDE), F32)],
        ),
        compiler_params=pltpu.CompilerParams(
            dimension_semantics=("arbitrary",), vmem_limit_bytes=LIMIT
        ),
        name="solve_apply",
    )(where, *near[:2], *held[:2], *near[4:], *held[2:], vectors_held, other_held, mine, theirs)

    returned = core_swap(result_other)
    result = jnp.zeros((rows, columns), F32)
    result = lax.dynamic_update_slice_in_dim(result, result_own, core * half, 0)
    return lax.dynamic_update_slice_in_dim(result, returned, (1 - core) * half, 0)


def solution(mesh):
    specs = (P("row", "col"), P("row", "col"), P("row", "col"))
    return jax.shard_map(
        per_device, mesh=mesh, in_specs=specs, out_specs=P("row", "col"), check_vma=False
    )
```

```python
import functools

import jax
import jax.numpy as jnp
from jax import lax
from jax.experimental import pallas as pl
from jax.experimental.pallas import tpu as pltpu
from jax.sharding import PartitionSpec as P

F32 = jnp.float32
BF16 = jnp.bfloat16
HIGHEST = lax.Precision.HIGHEST
PLANES, DEPTH, CORES = 2, 4, 2
CHIPS = PLANES * DEPTH
WIDE = 128
TILE = 2048
LIMIT = 32 << 20
PIECES = ((0, 0), (0, 1), (1, 1), (0, 2), (0, 3)), ((1, 2), (1, 3), (2, 2), (2, 3), (3, 3))


def split2(value):
    high = value.astype(BF16)
    return high, (value - high.astype(F32)).astype(BF16)


def nn(left, right):
    return lax.dot_general(left, right, (((1,), (0,)), ((), ())), preferred_element_type=F32)


def nt(left, right):
    return lax.dot_general(left, right, (((1,), (1,)), ((), ())), preferred_element_type=F32)


def full(left, right):
    return lax.dot_general(
        left, right, (((1,), (0,)), ((), ())), precision=HIGHEST, preferred_element_type=F32
    )


def each_middle(early, refs, place):
    up_ref, down_ref, across_ref = refs
    chunk = down_ref.shape[0]

    @pl.when(early)
    def _():
        place(4, up_ref[:chunk])
        place(5, up_ref[chunk:])
        place(6, down_ref[...])

    @pl.when(jnp.logical_not(early))
    def _():
        place(4, down_ref[...])
        place(5, across_ref[:chunk])
        place(6, across_ref[chunk:])


def each_last(early, refs, place):
    @pl.when(early)
    def _():
        place(7, refs[0][...])

    @pl.when(jnp.logical_not(early))
    def _():
        place(7, refs[1][...])


def each_far(step, steps, refs, place):
    each_middle(step < steps // 2, refs[:3], place)
    each_last(step < steps // 2, refs[3:], place)


def placer(core, lines, high, low):
    def place_half(slot, swap, value):
        begin = pl.multiple_of(slot * 2 * lines + lines * (core ^ swap), lines)
        for target, part in zip((high, low), split2(value)):
            target[pl.ds(begin, lines), :] = part

    def place(slot, value):
        place_half(slot, 0, value[:lines])
        place_half(slot, 1, value[lines:])

    return place_half, place


def gram_kernel(where_ref, *refs, first):
    steps = pl.num_programs(0)
    step = pl.program_id(0)
    count = 8 if first else 11
    panels = refs[:count]
    own_ref, other_ref, out_ref, high, low, even, skew, proj = refs[count:]
    core = where_ref[CHIPS]
    half = even.shape[1]
    start_row = high.shape[0] - half
    place_half, place = placer(core, panels[0].shape[0], high, low)

    @pl.when(step == 0)
    def _():
        even[...] = jnp.zeros_like(even)
        skew[...] = jnp.zeros_like(skew)
        proj[...] = jnp.zeros_like(proj)
        if not first:
            empty = half // 4
            high[2 * half - empty :, :] = jnp.zeros((empty, high.shape[1]), BF16)
            low[2 * half - empty :, :] = jnp.zeros((empty, low.shape[1]), BF16)

    for index in range(8):
        place_half(index // 2, index % 2, panels[index][...])
    if not first:
        each_middle(step < steps // 2, panels[8:], place)

    one, two = high[start_row:, :], low[start_row:, :]
    skew[...] += nt(one, two)
    if first:
        even[...] += nt(one, one)
    else:
        even[half:, :] += nt(one, one)
        one_a, two_a = high[:half, :], low[:half, :]
        even[:half, :] += (nt(one_a, two) + nt(two_a, one)) + nt(one_a, one)
    x_one, x_two = split2(jnp.concatenate([own_ref[...], other_ref[...]], axis=1))
    proj[...] += (nn(one, x_two) + nn(two, x_one)) + nn(one, x_one)

    @pl.when(step == steps - 1)
    def _():
        out_ref[0:half, :] = proj[...]
        out_ref[half : 2 * half, :] = even[start_row:, :] + (skew[...] + skew[...].T)
        if not first:
            out_ref[2 * half :, :] = even[:half, :]


def last_kernel(where_ref, *refs):
    steps = pl.num_programs(0)
    step = pl.program_id(0)
    panels = refs[:13]
    own_ref, other_ref, near_ref, middle_ref, keep_ref, send_ref, high, low, gram, proj = refs[13:]
    core = where_ref[CHIPS]
    size = gram.shape[1]
    half = size // 2
    chunk = gram.shape[0]
    place_half, place = placer(core, panels[0].shape[0], high, low)
    for index in range(8):
        place_half(index // 2, index % 2, panels[index][...])
    each_far(step, steps, panels[8:], place)

    @pl.when(step == 0)
    def _():
        gram[...] = jnp.zeros_like(gram)
        proj[...] = jnp.zeros_like(proj)

    one, two = high[...], low[...]
    last, rest = one[size - chunk :], two[size - chunk :]
    pair = jnp.concatenate([last, rest], axis=0)
    partial = nt(pair, one)
    gram[...] += nt(last, two) + (partial[chunk:] + partial[:chunk])
    x_one, x_two = split2(jnp.concatenate([own_ref[...], other_ref[...]], axis=1))
    partial = nn(pair, x_one)
    proj[...] += nn(last, x_two) + (partial[chunk:] + partial[:chunk])

    @pl.when(step == steps - 1)
    def _():
        for target, lanes in ((keep_ref, slice(0, WIDE)), (send_ref, slice(WIDE, 2 * WIDE))):
            target[0:half, :] = near_ref[0:half, lanes]
            target[half : size - chunk, :] = middle_ref[0 : half - chunk, lanes]
            target[size - chunk : size, :] = proj[:, lanes]

        def spot(ref, base, i, j):
            return ref[base + i * WIDE : base + (i + 1) * WIDE, j * WIDE : (j + 1) * WIDE]

        def lower(j):
            return jnp.concatenate(
                [jnp.zeros((WIDE - chunk, WIDE), F32), gram[:, j * WIDE : (j + 1) * WIDE]], axis=0
            )

        lane = lax.broadcasted_iota(jnp.int32, (WIDE, WIDE), 1)

        def blocks(part, target):
            for at, (i, j) in enumerate(PIECES[part]):
                begin = size + at * WIDE
                if j < 2:
                    block = spot(near_ref, half, i, j)
                elif i < 2:
                    block = spot(middle_ref, 2 * half, i, j - 2)
                else:
                    block = spot(middle_ref, half, i - 2, j - 2)
                if j == 3:
                    added = lower(i)
                    if i == 3:
                        block = block + added
                        added = jnp.where(lane < WIDE - chunk, added, 0.0)
                    block = block + added.T
                target[begin : begin + WIDE, :] = block

        @pl.when(core == 0)
        def _():
            blocks(0, keep_ref)
            blocks(1, send_ref)

        @pl.when(core != 0)
        def _():
            blocks(1, keep_ref)
            blocks(0, send_ref)


def solve(where_ref, mine_ref, other_ref, solved_ref, both, rows_done, ordered, sides):
    core = where_ref[CHIPS]
    both[core] = mine_ref[...]
    both[1 - core] = other_ref[...]
    count = 4
    size = count * WIDE
    panel = size // 2
    base = 16

    def relative(i, j):
        for part in range(2):
            if (i, j) in PIECES[part]:
                start = size + PIECES[part].index((i, j)) * WIDE
                return both[part, start : start + WIDE, :]

    group = size // (2 * CORES * CHIPS)

    def target(index):
        slot, at_core, part = index // (2 * CORES), (index // 2) % CORES, index % 2
        start = part * panel + where_ref[slot] * CORES * group + at_core * group
        return pl.ds(pl.multiple_of(start, group), group)

    for i in range(count):
        strip = jnp.concatenate(
            [relative(i, j) if i <= j else relative(j, i).T for j in range(count)], axis=1
        )
        for k in range(WIDE // group):
            rows_done[target(i * (WIDE // group) + k), :] = strip[k * group : (k + 1) * group]
    for i in range(count):
        strip = jnp.concatenate(
            [
                rows_done[j * WIDE : (j + 1) * WIDE, i * WIDE : (i + 1) * WIDE].T
                for j in range(count)
            ],
            axis=1,
        )
        for k in range(WIDE // group):
            ordered[target(i * (WIDE // group) + k), :] = strip[k * group : (k + 1) * group]
    for index in range(size // group):
        at = slice(index * group, (index + 1) * group)
        sides[target(index), :] = jnp.concatenate([mine_ref[at, :], other_ref[at, :]], axis=1)

    def block(i, j):
        return ordered[i * WIDE : (i + 1) * WIDE, j * WIDE : (j + 1) * WIDE]

    row = lax.broadcasted_iota(jnp.int32, (WIDE, WIDE), 0)
    column = lax.broadcasted_iota(jnp.int32, (WIDE, WIDE), 1)
    same = (row // base) == (column // base)
    diagonals = []
    for i in range(count):
        value = block(i, i)
        diagonals.append(
            jnp.where(row < column, value, jnp.where(row == column, value * 0.5, 0.0))
        )
    lane = lax.broadcasted_iota(jnp.int32, (base, WIDE), 1) % base
    ones = jnp.where(same, 1.0, 0.0).astype(BF16)
    spread = []
    for i in range(count):
        flipped = jnp.where(same, diagonals[i], 0.0).T
        folded = flipped[0:base]
        for k in range(1, WIDE // base):
            folded = folded + flipped[k * base : (k + 1) * base]
        stacked = jnp.concatenate([jnp.where(lane == k, folded, 0.0) for k in range(base)], axis=0)
        high = stacked.astype(BF16)
        rest = stacked - high.astype(F32)
        middle = rest.astype(BF16)
        low = (rest - middle.astype(F32)).astype(BF16)
        spread.append((nn(low, ones) + nn(middle, ones)) + nn(high, ones))
    wide_lane = lax.broadcasted_iota(jnp.int32, (1, size), 1) % base
    wide_row = lax.broadcasted_iota(jnp.int32, (base, size), 0)
    solved = jnp.zeros((base, size), F32)
    for i in range(base - 1, -1, -1):
        factor = jnp.concatenate([s[i * base : (i + 1) * base] for s in spread], axis=1)
        total = jnp.sum(factor * solved, axis=0, keepdims=True)
        line = (jnp.where(wide_lane == i, 1.0, 0.0) - total) / factor[i : i + 1]
        solved = jnp.where(wide_row == i, line, solved)

    def three(left, right):
        return (nn(left[0], right[1]) + nn(left[1], right[0])) + nn(left[0], right[0])

    small = []
    for i in range(count):
        tiled = jnp.concatenate([solved[:, i * WIDE : (i + 1) * WIDE]] * (WIDE // base), axis=0)
        small.append(jnp.where(same, tiled, 0.0))
    width = base
    while width < WIDE:
        picked = ((row // width) % 2 == 0) & (column // width == row // width + 1)
        for i in range(count):
            inverse = split2(small[i])
            coupling = split2(jnp.where(picked, diagonals[i], 0.0))
            small[i] = small[i] - three(split2(three(inverse, coupling)), inverse)
        width *= 2
    inverses = []
    for half in range(2):
        left, right = small[2 * half], small[2 * half + 1]
        coupling = split2(block(2 * half, 2 * half + 1))
        corner = -three(split2(three(split2(left), coupling)), split2(right))
        top = jnp.concatenate([left, corner], axis=1)
        bottom = jnp.concatenate([jnp.zeros((WIDE, WIDE), F32), right], axis=1)
        inverses.append(split2(jnp.concatenate([top, bottom], axis=0)))
    corner = jnp.concatenate(
        [
            jnp.concatenate([block(0, 2), block(0, 3)], axis=1),
            jnp.concatenate([block(1, 2), block(1, 3)], axis=1),
        ],
        axis=0,
    )
    right_side = sides[...]
    second = three(inverses[1], split2(right_side[panel:]))
    first = three(
        inverses[0], split2(right_side[:panel] - three(split2(corner), split2(second)))
    )
    solved_ref[0:panel, :] = first
    solved_ref[panel:, :] = second


def apply_kernel(where_ref, *refs):
    step = pl.program_id(0)
    steps = pl.num_programs(0)
    panels = refs[:13]
    current_own, current_other, mine_ref, theirs_ref, out_own, out_other = refs[13:19]
    solved, high, low, merged, both, rows_done, ordered, sides = refs[19:]
    core = where_ref[CHIPS]
    panel = solved.shape[0] // 2
    chunk = 2 * panels[0].shape[0]
    group = chunk // 4

    @pl.when(step == 0)
    def _():
        solve(where_ref, mine_ref, theirs_ref, solved, both, rows_done, ordered, sides)
        for index in range(2 * CHIPS):
            chip = where_ref[index // 2]
            for part in range(2):
                start = pl.multiple_of(
                    part * panel + chip * 2 * group + group * (core ^ (index % 2)), group
                )
                at = (2 * index + part) * group
                for target, value in zip((high, low), split2(solved[pl.ds(start, group), :])):
                    target[at : at + group, :] = value

    def place(slot, value):
        merged[slot * chunk : (slot + 1) * chunk, :] = value

    for index in range(8):
        merged[index * chunk // 2 : (index + 1) * chunk // 2, :] = panels[index][...]
    each_far(step, steps, panels[8:], place)
    one, two = split2(merged[...])
    first, second = high[...], low[...]

    def tn(left, right):
        return lax.dot_general(left, right, (((0,), (0,)), ((), ())), preferred_element_type=F32)

    change = (tn(one, second) + tn(two, first)) + tn(one, first)
    out_own[...] = current_own[...] - change[:, :WIDE]
    out_other[...] = current_other[...] - change[:, WIDE:]


def per_device(vectors, panel_one, panel_two):
    rows, columns = vectors.shape
    group = panel_one.shape[1]
    half = rows // 2
    size = 2 * group * CHIPS * CORES
    quarter = half // 2
    chunk = 4 * group
    steps = half // TILE
    at = lax.axis_index("col")
    core, depth, plane = at % CORES, (at // CORES) % DEPTH, at // (CORES * DEPTH)

    def permute(value, move):
        pairs = []
        for source in range(CHIPS * CORES):
            k, z, x = source % CORES, (source // CORES) % DEPTH, source // (CORES * DEPTH)
            k, z, x = move(k, z, x)
            pairs.append((source, (x * DEPTH + z % DEPTH) * CORES + k))
        return lax.ppermute(value, "col", pairs)

    def core_swap(value):
        return permute(value, lambda k, z, x: (1 - k, z, x))

    def up(value):
        return permute(value, lambda k, z, x: (k, z + 1, x))

    def down(value):
        return permute(value, lambda k, z, x: (k, z - 1, x))

    def across(value):
        return permute(value, lambda k, z, x: (k, z, 1 - x))

    def half_of(which):
        picked = [lax.dynamic_slice_in_dim(v.T, which * half, half, 1) for v in (panel_one, panel_two)]
        return jnp.concatenate(picked, axis=0)

    a_own = half_of(core)
    b_own = core_swap(half_of(1 - core))
    own = jnp.concatenate([a_own, b_own], axis=0)
    a_away, a_below, a_above = across(a_own), up(a_own), down(a_own)
    b_own, other = lax.optimization_barrier((b_own, core_swap(vectors)))
    b_away, b_below, b_above = across(b_own), up(b_own), down(b_own)
    near = (a_own, b_own, a_below, b_below, a_above, b_above, a_away, b_away)

    def early_half(*values):
        return [v[:, :quarter] for v in values]

    def late_half(*values):
        return [v[:, quarter:] for v in values]

    to_up = jnp.concatenate(early_half(a_below, b_below, a_away, b_away), axis=0)
    to_down = jnp.concatenate(
        late_half(a_above, b_above) + early_half(a_away, b_away), axis=0
    )
    to_across = jnp.concatenate(late_half(a_below, b_below, a_above, b_above), axis=0)
    sent_up, sent_down, sent_across = up(to_up), down(to_down), across(to_across)

    chips = []
    for x_step, z_step in ((0, 0), (0, -1), (0, 1), (1, 0), (0, 2), (1, -1), (1, 1), (1, 2)):
        chips.append(jnp.bitwise_xor(plane, x_step) * DEPTH + (depth + z_step) % DEPTH)
    where = jnp.stack(chips + [core]).astype(jnp.int32)

    turn = steps // 2
    whole = [pl.BlockSpec((chunk // 2, TILE), lambda j, w: (0, j))] * 8

    def early(lines):
        return pl.BlockSpec((lines, TILE), lambda j, w: (0, jnp.minimum(j, turn - 1)))

    def late(lines):
        return pl.BlockSpec((lines, TILE), lambda j, w: (0, jnp.maximum(j - turn, 0)))

    both = pl.BlockSpec(
        (chunk, TILE), lambda j, w: (jnp.where(j < turn, 1, 0), jnp.where(j < turn, j, j - turn))
    )
    parts_far = [early(2 * chunk), both, late(2 * chunk), early(chunk), late(chunk)]
    own_spec = pl.BlockSpec((TILE, columns), lambda j, w: (w[CHIPS] * steps + j, 0))
    length = size + 5 * WIDE
    span = size // 2

    def products(kernel, pieces, specs, extra, shapes, scratch, units, name):
        return pl.pallas_call(
            kernel,
            out_shape=[jax.ShapeDtypeStruct(v, F32) for v in shapes],
            grid_spec=pltpu.PrefetchScalarGridSpec(
                num_scalar_prefetch=1,
                grid=(steps,),
                in_specs=specs
                + [own_spec, own_spec]
                + [pl.BlockSpec(v.shape, lambda j, w: (0, 0)) for v in extra],
                out_specs=[pl.BlockSpec(v, lambda j, w: (0, 0)) for v in shapes],
                scratch_shapes=scratch,
            ),
            compiler_params=pltpu.CompilerParams(
                dimension_semantics=("arbitrary",), vmem_limit_bytes=LIMIT
            ),
            cost_estimate=pl.CostEstimate(
                flops=2 * 3 * units * span * span * half,
                bytes_accessed=4 * half * (size + columns * 2),
                transcendentals=0,
            ),
            name=name,
        )(where, *pieces, vectors, other, *extra)

    def split_scratch(height):
        return [pltpu.VMEM((height, TILE), BF16)] * 2

    square = pltpu.VMEM((span, span), F32)
    (before,) = products(
        functools.partial(gram_kernel, first=True), near, whole, (),
        [(2 * span, span)], split_scratch(span) + [square] * 3, 10, "gram_near",
    )
    before, sent_up, sent_down = lax.optimization_barrier((before, sent_up, sent_down))
    end_up = up(sent_up[chunk:])
    end_across = across(sent_down[:chunk])
    middle = (sent_up, sent_down, sent_across)
    (between,) = products(
        functools.partial(gram_kernel, first=False), near + middle, whole + parts_far[:3], (),
        [(3 * span, span)],
        split_scratch(size) + [pltpu.VMEM((size, span), F32), square, square], 16, "gram_middle",
    )
    end_up, end_across, between = lax.optimization_barrier((end_up, end_across, between))
    far = middle + (end_up, end_across)
    kept, sent = products(
        last_kernel, near + far, whole + parts_far, (before, between),
        [(length, WIDE)] * 2,
        split_scratch(size) + [pltpu.VMEM((chunk, size), F32), pltpu.VMEM((chunk, span), F32)],
        8, "gram_last",
    )
    mine = kept + core_swap(sent)
    members = lax.axis_size("row")
    parts = lax.all_to_all(mine.reshape(members, length // members, WIDE), "row", 0, 0)
    total = jnp.sum(parts, axis=0)
    spread = jnp.broadcast_to(total[None], (members,) + total.shape)
    mine = lax.all_to_all(spread, "row", 0, 0).reshape(length, WIDE)
    theirs = core_swap(mine)

    *held, vectors_held, other_held = [
        pltpu.with_memory_space_constraint(v, pltpu.HBM) for v in near + far + (vectors, other)
    ]
    result_own, result_other = pl.pallas_call(
        apply_kernel,
        out_shape=[jax.ShapeDtypeStruct((half, columns), F32)] * 2,
        grid_spec=pltpu.PrefetchScalarGridSpec(
            num_scalar_prefetch=1,
            grid=(steps,),
            in_specs=whole
            + parts_far
            + [own_spec, own_spec]
            + [pl.BlockSpec((length, WIDE), lambda j, w: (0, 0))] * 2,
            out_specs=[pl.BlockSpec((TILE, columns), lambda j, w: (j, 0))] * 2,
            scratch_shapes=[pltpu.VMEM((size, 2 * WIDE), F32)]
            + [pltpu.VMEM((size, 2 * WIDE), BF16)] * 2
            + [pltpu.VMEM((size, TILE), F32), pltpu.VMEM((2, length, WIDE), F32)]
            + [pltpu.VMEM((size, size), F32)] * 2
            + [pltpu.VMEM((size, 2 * WIDE), F32)],
        ),
        compiler_params=pltpu.CompilerParams(
            dimension_semantics=("arbitrary",), vmem_limit_bytes=LIMIT
        ),
        name="solve_apply",
    )(where, *held, vectors_held, other_held, mine, theirs)

    returned = core_swap(result_other)
    result = jnp.zeros((rows, columns), F32)
    result = lax.dynamic_update_slice_in_dim(result, result_own, core * half, 0)
    return lax.dynamic_update_slice_in_dim(result, returned, (1 - core) * half, 0)


def solution(mesh):
    specs = (P("row", "col"), P("row", "col"), P("row", "col"))
    return jax.shard_map(
        per_device, mesh=mesh, in_specs=specs, out_specs=P("row", "col"), check_vma=False
    )
```
